512 devices in a mesh: gx: 32 (over z, core), gy: 16 (over x, y).
Axes of the slice: x: 4, y: 4, z: 16, core: 2. Of those that a mesh axis runs over, the one named last changes fastest.
Arguments:
- right_side: float32 [512, 512, 128], P('gx', 'gy'), may hold values from -1 to 2
- screening: float32 [512, 512, 128], P('gx', 'gy'), may hold values from 0.5 to 5
- active_blocks: int32 [32, 16, 12], P('gx', 'gy'), may hold values from -1 to 15, as said below
- visible_bricks: int32 [32, 16, 8], P('gx', 'gy'), may hold values from -1 to 15, as said below
Outputs:
- indicator: float32 [512, 512, 128], P('gx', 'gy')
- crossing: float32 [256, 16, 3, 4096], P('gx', 'gy')
The draws below stay inside these ranges and needn't reach their ends.
Inputs may be any that keep to these rules, and one draw needn't show every extreme that they name: `active_blocks`: each device's row lists distinct block numbers of that device's 16 blocks first, then -1 in the unused slots; at least one entry is a block number; some device fills all 12 slots and some leaves slots unused. `visible_bricks`: each device's row lists distinct block numbers of that device's 16 blocks first, then -1 in the unused slots; at least one entry is a block number; some device fills all 8 slots.
All inputs are finite; a program needn't handle non-finite values.
Results may differ from the reference program's by a relative error of at most 0.0003.
Values sent between devices are 32-bit elements; how exact they have to be, the bound alone decides.
A program may use at most 64 MiB of HBM per device.

```python
import math
import jax
import jax.numpy as jnp
from jax import lax

BLK = 16
CX = 16
CY = 32
CZ = 128
ITERS = 3
ACT = 12
VIS = 8
NX = 512
NY = 512
N_GX = 32
N_GY = 16


def slot_lists(key, slots, salt):
    blocks = CX // BLK * (CY // BLK) * (CZ // BLK)
    devices = N_GX * N_GY

    def one_row(row_key, forced, sparse):
        perm_key, count_key = jax.random.split(row_key)
        order = jax.random.permutation(perm_key, blocks).astype(jnp.int32)
        place = jnp.argmax(order == blocks - 1)
        order = order.at[place].set(order[0]).at[0].set(blocks - 1)
        count = jax.random.randint(count_key, (), 1, slots + 1)
        count = jnp.where(sparse, max(1, slots // 4), count)
        count = jnp.where(forced, slots, count)
        taken = order[:slots]
        return jnp.where(jnp.arange(slots) < count, taken, -1).astype(jnp.int32)
    keys = jax.random.split(jax.random.fold_in(key, salt), devices)
    chosen = jax.random.randint(jax.random.fold_in(key, salt + 1), (), 0, devices)
    forced = jnp.arange(devices) == chosen
    sparse = jnp.arange(devices) == (chosen + 1) % devices
    return jax.vmap(one_row)(keys, forced, sparse).reshape(N_GX, N_GY, slots)


def draw_active_blocks(key, part):
    return slot_lists(key, ACT, 11)


def draw_visible_bricks(key, part):
    return slot_lists(key, VIS, 23)


def block_scale(stream_key, dims, shards, smallest, high):
    def one(dim, shards_of):
        heights = jax.random.uniform(jax.random.fold_in(jax.random.fold_in(stream_key, 6), dim), (shards_of,), jnp.float32, smallest / len(shards), high / len(shards))
        return jnp.repeat(jnp.exp(heights), dims[dim] // shards_of).reshape((-1,) + (1,) * (len(dims) - dim - 1))

    factor_of = one(*shards[0])
    for cut in shards[1:]:
        factor_of = factor_of * one(*cut)
    return factor_of


def setup_inputs(seed: int = 0) -> dict:
    arg_keys = jax.random.split(jax.random.key(seed), 5)
    right_side = jnp.clip(-1.0 + 3.0 * jax.random.uniform(arg_keys[0], (NX, NY, CZ), jnp.float32) ** block_scale(arg_keys[0], (NX, NY, CZ), ((0, 32), (1, 16)), -0.2, 0.2), -1.0, 2.0)
    screening = jnp.clip(jnp.exp(math.log(5.0) - 2.3025851 * jax.random.uniform(arg_keys[1], (NX, NY, CZ), jnp.float32) ** block_scale(arg_keys[1], (NX, NY, CZ), ((0, 32), (1, 16)), -0.2, 0.2)), 0.5, 5.0)
    active_blocks = draw_active_blocks(jax.random.fold_in(arg_keys[4], 71), 0)
    visible_bricks = draw_visible_bricks(jax.random.fold_in(arg_keys[4], 71), 0)
    return {"right_side": right_side, "screening": screening, "active_blocks": active_blocks, "visible_bricks": visible_bricks}


MASS = (11.0 / 20.0, 13.0 / 60.0, 1.0 / 120.0)
STIFF = (1.0, -1.0 / 3.0, -1.0 / 6.0)
SHARP = 4.0


def apply_axis(padded, axis, coef):
    count = padded.shape[axis] - 4

    def part(start):
        return lax.slice_in_dim(padded, start, start + count, axis=axis)

    return coef[0] * part(2) + coef[1] * (part(1) + part(3)) + coef[2] * (part(0) + part(4))


def pad_axis(field, axis):
    widths = [(0, 0)] * field.ndim
    widths[axis] = (2, 2)
    return jnp.pad(field, widths)


def operate(field, screening, mask):
    zpadded = pad_axis(field, 2)
    mass_z = pad_axis(apply_axis(zpadded, 2, MASS), 1)
    stiff_z = pad_axis(apply_axis(zpadded, 2, STIFF), 1)
    inner = pad_axis(apply_axis(stiff_z, 1, MASS) + apply_axis(mass_z, 1, STIFF), 0)
    outer = pad_axis(apply_axis(mass_z, 1, MASS), 0)
    return mask * (apply_axis(inner, 0, MASS) + apply_axis(outer, 0, STIFF) + screening * field)


def crossing_weight(low, high):
    lower = jax.nn.sigmoid(SHARP * low)
    upper = jax.nn.sigmoid(SHARP * high)
    return lower * (1.0 - upper) + (1.0 - lower) * upper


def reference(right_side, screening, active_blocks, visible_bricks):
    n_gx, n_gy = active_blocks.shape[0], active_blocks.shape[1]
    bx_dev, by_dev, bz_dev = CX // BLK, CY // BLK, CZ // BLK
    numbers = jnp.arange(bx_dev * by_dev * bz_dev, dtype=jnp.int32)
    block_mask = jnp.any(numbers[None, None, :, None] == active_blocks[:, :, None, :], axis=-1).astype(jnp.float32)
    block_mask = block_mask.reshape(n_gx, n_gy, bx_dev, by_dev, bz_dev).transpose(0, 2, 1, 3, 4)
    block_mask = block_mask.reshape(n_gx, bx_dev, 1, n_gy, by_dev, 1, bz_dev, 1)
    mask = jnp.broadcast_to(block_mask, (n_gx, bx_dev, BLK, n_gy, by_dev, BLK, bz_dev, BLK)).reshape(right_side.shape)
    indicator = jnp.zeros_like(right_side)
    residual = mask * right_side
    direction = residual
    norm_now = jnp.sum(residual * residual)
    for step in range(ITERS):
        image = operate(direction, screening, mask)
        alpha = norm_now / jnp.sum(direction * image)
        indicator = indicator + alpha * direction
        residual = residual - alpha * image
        if step + 1 < ITERS:
            norm_next = jnp.sum(residual * residual)
            direction = residual + (norm_next / norm_now) * direction
            norm_now = norm_next
    total = jnp.sum(indicator)
    count = jnp.sum((active_blocks >= 0).astype(jnp.float32)) * float(BLK ** 3)
    iso = total / count
    extended = jnp.pad(indicator, ((0, 1), (0, 1), (0, 1)))
    flat = visible_bricks.reshape(-1)
    slots = visible_bricks.shape[2]
    owner_x = jnp.arange(flat.shape[0], dtype=jnp.int32) // (n_gy * slots)
    owner_y = (jnp.arange(flat.shape[0], dtype=jnp.int32) // slots) % n_gy

    def brick_weights(entry):
        number, dev_x, dev_y = entry
        safe = jnp.maximum(number, 0)
        block_x = safe // (by_dev * bz_dev)
        block_y = (safe // bz_dev) % by_dev
        block_z = safe % bz_dev
        start = (dev_x * CX + block_x * BLK, dev_y * CY + block_y * BLK, block_z * BLK)
        region = lax.dynamic_slice(extended, [s.astype(jnp.int32) for s in start], (BLK + 1, BLK + 1, BLK + 1)) - iso
        base = region[:-1, :-1, :-1]
        result = jnp.stack([crossing_weight(base, region[1:, :-1, :-1]),
                            crossing_weight(base, region[:-1, 1:, :-1]),
                            crossing_weight(base, region[:-1, :-1, 1:])]).reshape(3, BLK * BLK * BLK)
        return jnp.where(number >= 0, result, jnp.zeros_like(result))

    weights = lax.map(brick_weights, (flat, owner_x, owner_y))
    weights = weights.reshape(n_gx, n_gy, slots, 3, BLK * BLK * BLK).transpose(0, 2, 1, 3, 4)
    crossing = weights.reshape(n_gx * slots, n_gy, 3, BLK * BLK * BLK)
    return indicator, crossing
```

```python
import jax
import jax.numpy as jnp
from jax import lax
from jax.experimental import pallas as pl
from jax.experimental.pallas import tpu as pltpu
from jax.sharding import PartitionSpec as P

MESH = pl.DeviceIdType.MESH
BLK = 16
ACT = 12
VIS = 8
NGX = 32
NGY = 16
NZ = 16
SIGMA = 2.5
HR = 6
HS = 4
SCALE = 1.0 / 86400.0
NEIGHBOURS = [(1, 1), (1, -1), (-1, 1), (-1, -1), (0, 1), (0, -1), (1, 0), (-1, 0)]


def two_sum(a, b):
    s = a + b
    t = s - a
    return s, (a - (s - t)) + (b - t)


def quick_two_sum(a, b):
    s = a + b
    return s, b - (s - a)


def split(a):
    c = 4097.0 * a
    hi = c - (c - a)
    return hi, a - hi


def two_prod(a, b):
    p = a * b
    ah, al = split(a)
    bh, bl = split(b)
    return p, ((ah * bh - p) + ah * bl + al * bh) + al * bl


def dd_add(x, y):
    s, e = two_sum(x[0], y[0])
    return quick_two_sum(s, e + (x[1] + y[1]))


def dd_neg(x):
    return -x[0], -x[1]


def dd_sub(x, y):
    return dd_add(x, dd_neg(y))


def dd_mul(x, y):
    p, e = two_prod(x[0], y[0])
    return quick_two_sum(p, e + (x[0] * y[1] + x[1] * y[0]))


def dd_div(x, y):
    q = x[0] / y[0]
    r = dd_sub(x, dd_mul(y, (q, jnp.zeros_like(q))))
    return quick_two_sum(q, r[0] / y[0])


def cg_weights(mu):
    one = (jnp.ones_like(mu[0][0]), jnp.zeros_like(mu[0][0]))
    inv = dd_div(one, mu[0])
    row = [dd_mul(m, inv) for m in mu[1:]]
    a = row[0]
    level = [dd_sub(row[k + 1], dd_mul(a, row[k])) for k in range(4)]
    first = [(jnp.zeros_like(a[0]), jnp.zeros_like(a[0]))] + level
    central = []
    for _ in range(4):
        first = [dd_sub(first[k + 1], dd_mul(a, first[k])) for k in range(len(first) - 1)]
        central.append(first[0])
    m2, m3, m4, m5 = central
    tiny = 1e-30
    m2s = (jnp.maximum(m2[0], tiny), jnp.where(m2[0] > tiny, m2[1], 0.0))
    b1 = dd_div(m3, m2s)
    m22 = dd_mul(m2, m2)
    h2 = dd_sub(dd_sub(m4, dd_mul(b1, m3)), m22)
    h2s = jnp.maximum(h2[0], tiny)
    inner = dd_sub(dd_mul(b1, m3), dd_add(m4, m4))
    inner = dd_add(inner, dd_add(m22, m22))
    top = dd_add(m5, dd_mul(b1, inner))
    m23 = dd_mul(m2, m3)
    top = dd_sub(top, dd_add(m23, m23))
    d0 = a[0] + SIGMA
    d1 = jnp.clip(d0 + b1[0], 0.25, 9.0)
    d2 = jnp.clip(d0 + top[0] / h2s, 0.25, 9.0)
    beta1 = jnp.maximum(m2[0], 0.0)
    beta2 = jnp.clip(h2[0] / m2s[0], 0.0, 25.0)
    bb1 = d1 - d0
    minor = d1 * d2 - beta2
    y2 = 1.0 / (d0 * minor - beta1 * d2)
    y1 = -d2 * y2
    y0 = minor * y2
    c2 = y2
    c1 = y1 - y2 * (2.0 * a[0] + bb1)
    c0 = y0 - a[0] * y1 + y2 * (a[0] * a[0] + a[0] * bb1 - m2[0])
    return c0, c1, c2


def sigmoid4(v):
    return 1.0 / (1.0 + jnp.exp(-4.0 * v))


def crossing_weight(lower, upper):
    return lower * (1.0 - upper) + (1.0 - lower) * upper


def solve_kernel(rhs, scr, act, x_out, iso_out,
           R, S, M, U1, U2, MZ, SZ, IN, OUT, act_s, ar1, ar2, ar3, stage,
           lsem, ssem, rsem, asem, arsem):
    gx = lax.axis_index("gx")
    gy = lax.axis_index("gy")
    z = gx // 2
    core = lax.rem(gx, 2)

    def at_z(off, c):
        return lax.rem(z + off + NZ, NZ) * 2 + c

    bar = pltpu.get_barrier_semaphore()

    def tell(x, y):
        pl.semaphore_signal(bar, inc=1, device_id=(x, y), device_id_type=MESH)

    tell(at_z(-4, core), gy)
    for off in (4, -3, 3, -2, 2, -1, 1):
        for c in (0, 1):
            tell(at_z(off, c), gy)
    tell(at_z(0, 1 - core), gy)
    for j in range(1, NGY):
        tell(gx, lax.rem(gy + j, NGY))
    has = []
    for dx, dy in NEIGHBOURS:
        ok = None
        for cond in ([gx < NGX - 1] if dx == 1 else []) + ([gx > 0] if dx == -1 else []) + (
            [gy < NGY - 1] if dy == 1 else []) + ([gy > 0] if dy == -1 else []):
            ok = cond if ok is None else jnp.logical_and(ok, cond)
        has.append(ok)
    for dx, dy in NEIGHBOURS:
        if dx and dy:
            tell(lax.rem(gx + dx + NGX, NGX), lax.rem(gy + dy + NGY, NGY))

    loads = [
        pltpu.make_async_copy(act.at[0], act_s, lsem.at[0]),
        pltpu.make_async_copy(rhs, R.at[pl.ds(HR, 16), pl.ds(8, 32)], lsem.at[1]),
        pltpu.make_async_copy(scr, S.at[pl.ds(HS, 16), pl.ds(8, 32)], lsem.at[2]),
    ]
    for c in loads:
        c.start()

    @pl.when(gx == 0)
    def _():
        R[pl.ds(0, HR)] = jnp.zeros((HR, 48, 128), jnp.float32)
        S[pl.ds(0, HS)] = jnp.zeros((HS, 48, 128), jnp.float32)
        M[0] = jnp.zeros((48, 128), jnp.float32)

    @pl.when(gx == NGX - 1)
    def _():
        R[pl.ds(HR + 16, HR)] = jnp.zeros((HR, 48, 128), jnp.float32)
        S[pl.ds(HS + 16, HS)] = jnp.zeros((HS, 48, 128), jnp.float32)
        M[2] = jnp.zeros((48, 128), jnp.float32)

    def clear_rows(row):
        R[:, pl.ds(row, 8)] = jnp.zeros((28, 8, 128), jnp.float32)
        S[:, pl.ds(row, 8)] = jnp.zeros((24, 8, 128), jnp.float32)
        M[:, pl.ds(row, 8)] = jnp.zeros((3, 8, 128), jnp.float32)

    @pl.when(gy == 0)
    def _():
        clear_rows(0)

    @pl.when(gy == NGY - 1)
    def _():
        clear_rows(40)

    lane = lax.broadcasted_iota(jnp.int32, (8, 128), 1)
    loads[0].wait()
    entries = [act_s[0, q] for q in range(ACT)]
    count = jnp.int32(0)
    for e in entries:
        count = count + jnp.where(e >= 0, 1, 0)
    for w in range(2):
        number = lane // BLK + 8 * w
        own = jnp.zeros((8, 128), jnp.float32)
        for e in entries:
            own = jnp.where(number == e, 1.0, own)
        M[1, pl.ds(8 + 16 * w, 8)] = own
        M[1, pl.ds(16 + 16 * w, 8)] = own
    loads[1].wait()
    loads[2].wait()

    def prepare(p, carry):
        R[HR + p, pl.ds(8, 32)] = R[HR + p, pl.ds(8, 32)] * M[1, pl.ds(8, 32)]
        S[HS + p, pl.ds(8, 32)] = S[HS + p, pl.ds(8, 32)] - SIGMA
        return carry

    lax.fori_loop(0, 16, prepare, 0)

    pl.semaphore_wait(bar, 35)

    def pieces(i):
        dx, dy = NEIGHBOURS[i]
        rows = {0: (8, 8, 32), 1: (32, 0, 8), -1: (8, 40, 8)}[dy]
        out = []
        for n, (ref, h) in enumerate(((R, HR), (S, HS))):
            planes = {0: (h, h, 16), 1: (16, 0, h), -1: (h, h + 16, h)}[dx]
            out.append((ref.at[pl.ds(planes[0], planes[2]), pl.ds(rows[0], rows[2])],
                        ref.at[pl.ds(planes[1], planes[2]), pl.ds(rows[1], rows[2])], n))
        out.append((M.at[1, pl.ds(rows[0], rows[2])], M.at[1 - dx, pl.ds(rows[1], rows[2])], 2))
        return [pltpu.make_async_remote_copy(s, d, ssem.at[i, n], rsem.at[i, n],
                                             device_id=(gx + dx, gy + dy), device_id_type=MESH)
                for s, d, n in out]

    opposite = [NEIGHBOURS.index((-dx, -dy)) for dx, dy in NEIGHBOURS]
    for i, ok in enumerate(has):
        @pl.when(ok)
        def _():
            for c in pieces(i):
                c.start()
    for i in range(8):
        @pl.when(has[opposite[i]])
        def _():
            for c in pieces(i):
                c.wait_recv()

    lane48 = lax.broadcasted_iota(jnp.int32, (48, 128), 1)
    low1, low2 = lane48 < 1, lane48 < 2
    high1, high2 = lane48 > 126, lane48 > 125

    def zy_pass(src, count, tiles):
        first, rows = tiles

        def step(p, carry):
            v = src[p]
            p1 = jnp.where(low1, 0.0, pltpu.roll(v, 1, 1)) + jnp.where(high1, 0.0, pltpu.roll(v, 127, 1))
            p2 = jnp.where(low2, 0.0, pltpu.roll(v, 2, 1)) + jnp.where(high2, 0.0, pltpu.roll(v, 126, 1))
            MZ[p, pl.ds(8, 48)] = 66.0 * v + 26.0 * p1 + p2
            SZ[p, pl.ds(8, 48)] = 6.0 * v - 2.0 * p1 - p2

            def rows_at(ref, off):
                return ref[p, pl.ds(8 + first + off, rows)]

            s0 = rows_at(SZ, 0)
            s1 = rows_at(SZ, -1) + rows_at(SZ, 1)
            s2 = rows_at(SZ, -2) + rows_at(SZ, 2)
            m0 = rows_at(MZ, 0)
            m1 = rows_at(MZ, -1) + rows_at(MZ, 1)
            m2 = rows_at(MZ, -2) + rows_at(MZ, 2)
            IN[p, pl.ds(first, rows)] = (66.0 * s0 + 26.0 * s1 + s2) + (6.0 * m0 - 2.0 * m1 - m2)
            OUT[p, pl.ds(first, rows)] = 66.0 * m0 + 26.0 * m1 + m2
            return carry

        lax.fori_loop(0, count, step, 0)

    def x_value(p, src, smap, m, first, rows):
        def pick(ref, off):
            return ref[p + off, pl.ds(first, rows)]

        i1 = pick(IN, 1) + pick(IN, 3)
        i2 = pick(IN, 0) + pick(IN, 4)
        o1 = pick(OUT, 1) + pick(OUT, 3)
        o2 = pick(OUT, 0) + pick(OUT, 4)
        k = (66.0 * pick(IN, 2) + 26.0 * i1 + i2) + (6.0 * pick(OUT, 2) - 2.0 * o1 - o2)
        centre = src[p + 2, pl.ds(first, rows)]
        return m * (k * SCALE + S[p + smap, pl.ds(first, rows)] * centre), centre

    def fold(v):
        return (v[0:8] + v[8:16]) + (v[16:24] + v[24:32])

    def apply(src, dst, planes, halo, smap):
        zero = jnp.zeros((8, 128), jnp.float32)
        for lo, hi, dx in ((0, halo, 0), (halo, halo + 16, 1), (halo + 16, planes, 2)):
            def step(p, acc):
                value, centre = x_value(p, src, smap, M[dx], 0, 48)
                dst[p] = value
                if dx != 1:
                    return acc
                u, v = value[8:40], centre[8:40]
                return acc[0] + fold(v * u), acc[1] + fold(u * u), acc[2] + fold(u)

            out = lax.fori_loop(lo, hi, step, (zero, zero, zero))
            if dx == 1:
                sums = out
        return sums

    zero = jnp.zeros((8, 128), jnp.float32)

    def first_sums(p, acc):
        v = R[HR + p, pl.ds(8, 32)]
        return acc[0] + fold(v * v), acc[1] + fold(v)

    mu0, sum0 = lax.fori_loop(0, 16, first_sums, (zero, zero))
    zy_pass(R, 28, (0, 48))
    mu1, mu2, sum1 = apply(R, U1, 24, 4, 0)
    zy_pass(U1, 24, (0, 48))
    mu3, mu4, sum2 = apply(U1, U2, 20, 2, 2)
    zy_pass(U2, 20, (8, 32))

    def last(p, acc):
        value, centre = x_value(p, U2, 4, M[1, pl.ds(8, 32)], 8, 32)
        return acc + fold(value * centre)

    mu5 = lax.fori_loop(0, 16, last, zero)

    sub16 = lax.broadcasted_iota(jnp.int32, (16, 128), 0)
    lane16 = lax.broadcasted_iota(jnp.int32, (16, 128), 1)
    rows = jnp.zeros((16, 128), jnp.float32)
    for k, acc in enumerate((mu0, mu1, mu2, mu3, mu4, mu5, sum0, sum1, sum2)):
        rows = jnp.where(sub16 == k, jnp.sum(acc, axis=0, keepdims=True), rows)
    total = jnp.sum(rows, axis=1, keepdims=True)
    spread = jnp.where(lane16 == sub16, total, 0.0)
    values = jnp.sum(spread, axis=0, keepdims=True)
    lane1 = lax.broadcasted_iota(jnp.int32, (1, 128), 1)
    coarse = jnp.zeros((1, 128), jnp.float32)
    for k in range(6):
        coarse = jnp.where(lane1 == k, 1.5 * 2.0 ** (26 + k), coarse)
    rounded = (values + coarse) - coarse
    high = jnp.where(lane1 < 6, rounded, values)
    rest = jnp.where(lane1 < 6, values - rounded, 0.0)
    row = high + pltpu.roll(rest, 64, 1)
    row = jnp.where(lane1 == 9, count.astype(jnp.float32), row)

    pending = []

    ar1[gy] = row
    for j in (8, 7, 9, 6, 10, 5, 11, 4, 12, 3, 13, 2, 14, 1, 15):
        pltpu.make_async_remote_copy(
            ar1.at[gy], ar1.at[gy], asem.at[0], arsem.at[0],
            device_id=(gx, lax.rem(gy + j, NGY)), device_id_type=MESH).start()
    wait = pltpu.make_async_remote_copy(
        ar1.at[pl.ds(0, 15)], ar1.at[pl.ds(0, 15)], asem.at[0], arsem.at[0],
        device_id=(gx, lax.rem(gy + 1, NGY)), device_id_type=MESH)
    wait.wait_recv()
    pending.append(wait)
    row = jnp.sum(ar1[...], axis=0)

    ar2[6 + core] = row
    targets = [(off, c) for off in (-4, 3, -3, 2, -2, 1, -1) for c in (0, 1)]
    for off, c in targets:
        pltpu.make_async_remote_copy(
            ar2.at[6 + core], ar2.at[(3 - off) * 2 + core], asem.at[1], arsem.at[1],
            device_id=(at_z(off, c), gy), device_id_type=MESH).start()
    pltpu.make_async_remote_copy(
        ar2.at[6 + core], ar2.at[6 + core], asem.at[1], arsem.at[1],
        device_id=(at_z(0, 1 - core), gy), device_id_type=MESH).start()
    wait = pltpu.make_async_remote_copy(
        ar2.at[pl.ds(0, 15)], ar2.at[pl.ds(0, 15)], asem.at[1], arsem.at[1],
        device_id=(at_z(1, core), gy), device_id_type=MESH)
    wait.wait_recv()
    pending.append(wait)
    stage[...] = jnp.sum(ar2[...], axis=0)
    for slot, off in ((0, -4), (1, 4)):
        pltpu.make_async_remote_copy(
            stage, ar3.at[slot], asem.at[2], arsem.at[2],
            device_id=(at_z(off, core), gy), device_id_type=MESH).start()
    wait = pltpu.make_async_remote_copy(
        ar3, ar3, asem.at[2], arsem.at[2], device_id=(at_z(4, core), gy), device_id_type=MESH)
    wait.wait_recv()
    pending.append(wait)
    row = ar3[0] + ar3[1]

    goal = jnp.where(sub16 < 10, sub16, sub16 + 54)
    picked = jnp.sum(jnp.where(lane16 == goal, row, 0.0), axis=1, keepdims=True)
    value = [jnp.broadcast_to(picked[k:k + 1], (8, 128)) for k in range(16)]
    mu = [two_sum(value[k], value[10 + k]) for k in range(6)]
    c0, c1, c2 = cg_weights(mu)
    iso = (c0 * value[6] + c1 * value[7] + c2 * value[8]) / (value[9] * float(BLK ** 3))

    def tile5(v):
        return jnp.concatenate([v] * 5, axis=0)

    iso_out[...] = iso
    c0, c1, c2 = tile5(c0), tile5(c1), tile5(c2)

    def solve(p, carry):
        x_out[p] = c0 * R[HR + p, pl.ds(8, 40)] + c1 * U1[4 + p, pl.ds(8, 40)] + c2 * U2[2 + p, pl.ds(8, 40)]
        return carry

    lax.fori_loop(0, 17, solve, 0)

    for i, ok in enumerate(has):
        @pl.when(ok)
        def _():
            for c in pieces(i):
                c.wait_send()
    for c in pending:
        c.wait_send()


def crossing_kernel(x_ref, iso_ref, vis, ind_out, cross_out, G, W, BR, vis_s, sem):
    load = pltpu.make_async_copy(vis.at[0], vis_s, sem.at[0])
    load.start()
    store = pltpu.make_async_copy(x_ref.at[pl.ds(0, 16), pl.ds(0, 32)], ind_out, sem.at[1])
    store.start()
    lane = lax.broadcasted_iota(jnp.int32, (8, 128), 1)
    iso = jnp.concatenate([iso_ref[...]] * 5, axis=0)

    def squash(p, carry):
        G[p] = sigmoid4(x_ref[p] - iso)
        return carry

    lax.fori_loop(0, 17, squash, 0)
    BR[pl.ds(16 * 96, 96)] = jnp.zeros((96, 128), jnp.float32)

    lane32 = lax.broadcasted_iota(jnp.int32, (32, 128), 1)
    edge = lane32 == 127
    empty = sigmoid4(0.0 - iso[0:32])

    def weigh(p, carry):
        g = G[p, pl.ds(0, 32)]
        gx1 = G[p + 1, pl.ds(0, 32)]
        gy1 = G[p, pl.ds(1, 32)]
        gz1 = jnp.where(edge, empty, pltpu.roll(g, 127, 1))
        for e, other in enumerate((gx1, gy1, gz1)):
            h = crossing_weight(g, other)
            for w in range(2):
                base = (p // 4) * 128 + w * 64 + lax.rem(p, 4) * 16
                W[e, pl.ds(pl.multiple_of(base, 16), 16)] = h[16 * w:16 * w + 16]
        return carry

    lax.fori_loop(0, 16, weigh, 0)

    group = lane // BLK

    def regroup(b, carry):
        e = b // 8
        part = lax.rem(b, 8)
        w = lax.rem(b, 2)
        ib = part // 2
        vs = [W[e, pl.ds(part * 64 + j, 8, stride=8)] for j in range(8)]
        for bit in range(3):
            d = 1 << bit
            odd = (group // d) % 2 == 1
            new = list(vs)
            for j in range(8):
                if not j & d:
                    lo, hi = vs[j], vs[j + d]
                    new[j] = jnp.where(odd, pltpu.roll(hi, 16 * d, 1), lo)
                    new[j + d] = jnp.where(odd, hi, pltpu.roll(lo, 128 - 16 * d, 1))
            vs = new
        for t in range(8):
            base = (w * 8 + t) * 96 + e * 32 + ib * 8
            BR[pl.ds(pl.multiple_of(base, 8), 8)] = vs[t]
        return carry

    lax.fori_loop(0, 24, regroup, 0)

    load.wait()
    stores = []
    for q in range(VIS):
        n = vis_s[0, q]
        start = pl.multiple_of(jnp.where(n >= 0, n, 16) * 96, 8)
        stores.append(pltpu.make_async_copy(
            BR.at[pl.ds(start, 96)], cross_out.at[pl.ds(q * 96, 96)], sem.at[2 + q]))
        stores[-1].start()
    store.wait()
    for c in stores:
        c.wait()


def body(right_side, screening, active_blocks, visible_bricks):
    f32 = jnp.float32
    right_side, screening, active_blocks, visible_bricks = (
        pltpu.with_memory_space_constraint(v, pltpu.HBM)
        for v in (right_side, screening, active_blocks, visible_bricks))
    hbm = pl.BlockSpec(memory_space=pltpu.HBM)
    vmem = pl.BlockSpec(memory_space=pltpu.VMEM)
    x, iso = pl.pallas_call(
        solve_kernel,
        out_shape=(jax.ShapeDtypeStruct((17, 40, 128), f32), jax.ShapeDtypeStruct((8, 128), f32)),
        in_specs=[hbm] * 3,
        out_specs=(vmem, vmem),
        scratch_shapes=[
            pltpu.VMEM((28, 48, 128), f32),
            pltpu.VMEM((24, 48, 128), f32),
            pltpu.VMEM((3, 48, 128), f32),
            pltpu.VMEM((24, 48, 128), f32),
            pltpu.VMEM((20, 48, 128), f32),
            pltpu.VMEM((28, 64, 128), f32),
            pltpu.VMEM((28, 64, 128), f32),
            pltpu.VMEM((28, 48, 128), f32),
            pltpu.VMEM((28, 48, 128), f32),
            pltpu.SMEM((1, ACT), jnp.int32),
            pltpu.VMEM((16, 1, 128), f32),
            pltpu.VMEM((16, 1, 128), f32),
            pltpu.VMEM((2, 1, 128), f32),
            pltpu.VMEM((1, 128), f32),
            pltpu.SemaphoreType.DMA((3,)),
            pltpu.SemaphoreType.DMA((8, 3)),
            pltpu.SemaphoreType.DMA((8, 3)),
            pltpu.SemaphoreType.DMA((3,)),
            pltpu.SemaphoreType.DMA((3,)),
        ],
        compiler_params=pltpu.CompilerParams(
            collective_id=0, has_side_effects=True, vmem_limit_bytes=32 << 20),
    )(right_side, screening, active_blocks)
    indicator, crossing = pl.pallas_call(
        crossing_kernel,
        out_shape=(jax.ShapeDtypeStruct((16, 32, 128), f32), jax.ShapeDtypeStruct((VIS * 96, 128), f32)),
        in_specs=[vmem, vmem, hbm],
        out_specs=(hbm, hbm),
        scratch_shapes=[
            pltpu.VMEM((17, 40, 128), f32),
            pltpu.VMEM((3, 512, 128), f32),
            pltpu.VMEM((17 * 96, 128), f32),
            pltpu.SMEM((1, VIS), jnp.int32),
            pltpu.SemaphoreType.DMA((2 + VIS,)),
        ],
        compiler_params=pltpu.CompilerParams(vmem_limit_bytes=24 << 20),
    )(x, iso, visible_bricks)
    return indicator, crossing.reshape(VIS, 1, 3, BLK ** 3)


def solution(mesh):
    spec = P("gx", "gy", None)
    return jax.shard_map(
        body,
        mesh=mesh,
        in_specs=(spec, spec, spec, spec),
        out_specs=(spec, P("gx", "gy", None, None)),
        check_vma=False,
    )
```

```python
import jax
import jax.numpy as jnp
from jax import lax
from jax.experimental import pallas as pl
from jax.experimental.pallas import tpu as pltpu
from jax.sharding import PartitionSpec as P

MESH = pl.DeviceIdType.MESH
BLK = 16
ACT = 12
VIS = 8
NGX = 32
NGY = 16
NZ = 16
SIGMA = 2.5
HR = 6
HS = 4
SCALE = 1.0 / 86400.0
NEIGHBOURS = [(1, 1), (1, -1), (-1, 1), (-1, -1), (0, 1), (0, -1), (1, 0), (-1, 0)]


def two_sum(a, b):
    s = a + b
    t = s - a
    return s, (a - (s - t)) + (b - t)


def quick_two_sum(a, b):
    s = a + b
    return s, b - (s - a)


def split(a):
    c = 4097.0 * a
    hi = c - (c - a)
    return hi, a - hi


def two_prod(a, b):
    p = a * b
    ah, al = split(a)
    bh, bl = split(b)
    return p, ((ah * bh - p) + ah * bl + al * bh) + al * bl


def dd_add(x, y):
    s, e = two_sum(x[0], y[0])
    return quick_two_sum(s, e + (x[1] + y[1]))


def dd_neg(x):
    return -x[0], -x[1]


def dd_sub(x, y):
    return dd_add(x, dd_neg(y))


def dd_mul(x, y):
    p, e = two_prod(x[0], y[0])
    return quick_two_sum(p, e + (x[0] * y[1] + x[1] * y[0]))


def dd_div(x, y):
    q = x[0] / y[0]
    r = dd_sub(x, dd_mul(y, (q, jnp.zeros_like(q))))
    return quick_two_sum(q, r[0] / y[0])


def cg_weights(mu):
    one = (jnp.ones_like(mu[0][0]), jnp.zeros_like(mu[0][0]))
    inv = dd_div(one, mu[0])
    row = [dd_mul(m, inv) for m in mu[1:]]
    a = row[0]
    level = [dd_sub(row[k + 1], dd_mul(a, row[k])) for k in range(4)]
    first = [(jnp.zeros_like(a[0]), jnp.zeros_like(a[0]))] + level
    central = []
    for _ in range(4):
        first = [dd_sub(first[k + 1], dd_mul(a, first[k])) for k in range(len(first) - 1)]
        central.append(first[0])
    m2, m3, m4, m5 = central
    tiny = 1e-30
    m2s = (jnp.maximum(m2[0], tiny), jnp.where(m2[0] > tiny, m2[1], 0.0))
    b1 = dd_div(m3, m2s)
    m22 = dd_mul(m2, m2)
    h2 = dd_sub(dd_sub(m4, dd_mul(b1, m3)), m22)
    h2s = jnp.maximum(h2[0], tiny)
    inner = dd_sub(dd_mul(b1, m3), dd_add(m4, m4))
    inner = dd_add(inner, dd_add(m22, m22))
    top = dd_add(m5, dd_mul(b1, inner))
    m23 = dd_mul(m2, m3)
    top = dd_sub(top, dd_add(m23, m23))
    d0 = a[0] + SIGMA
    d1 = jnp.clip(d0 + b1[0], 0.25, 9.0)
    d2 = jnp.clip(d0 + top[0] / h2s, 0.25, 9.0)
    beta1 = jnp.maximum(m2[0], 0.0)
    beta2 = jnp.clip(h2[0] / m2s[0], 0.0, 25.0)
    bb1 = d1 - d0
    minor = d1 * d2 - beta2
    y2 = 1.0 / (d0 * minor - beta1 * d2)
    y1 = -d2 * y2
    y0 = minor * y2
    c2 = y2
    c1 = y1 - y2 * (2.0 * a[0] + bb1)
    c0 = y0 - a[0] * y1 + y2 * (a[0] * a[0] + a[0] * bb1 - m2[0])
    return c0, c1, c2


def sigmoid4(v):
    return 1.0 / (1.0 + jnp.exp(-4.0 * v))


def crossing_weight(lower, upper):
    return lower * (1.0 - upper) + (1.0 - lower) * upper


def solve_kernel(rhs, scr, act, x_out, iso_out,
           R, S, M, U1, U2, MZ, SZ, IN, OUT, act_s, ar1, ar2, ar3, stage,
           lsem, ssem, rsem, asem, arsem):
    gx = lax.axis_index("gx")
    gy = lax.axis_index("gy")
    z = gx // 2
    core = lax.rem(gx, 2)

    def at_z(off, c):
        return lax.rem(z + off + NZ, NZ) * 2 + c

    bar = pltpu.get_barrier_semaphore()

    def tell(x, y):
        pl.semaphore_signal(bar, inc=1, device_id=(x, y), device_id_type=MESH)

    tell(at_z(-4, core), gy)
    for off in (4, -3, 3, -2, 2, -1, 1):
        for c in (0, 1):
            tell(at_z(off, c), gy)
    tell(at_z(0, 1 - core), gy)
    for j in range(1, NGY):
        tell(gx, lax.rem(gy + j, NGY))
    has = []
    for dx, dy in NEIGHBOURS:
        ok = None
        for cond in ([gx < NGX - 1] if dx == 1 else []) + ([gx > 0] if dx == -1 else []) + (
            [gy < NGY - 1] if dy == 1 else []) + ([gy > 0] if dy == -1 else []):
            ok = cond if ok is None else jnp.logical_and(ok, cond)
        has.append(ok)
    for dx, dy in NEIGHBOURS:
        if dx and dy:
            tell(lax.rem(gx + dx + NGX, NGX), lax.rem(gy + dy + NGY, NGY))

    loads = [
        pltpu.make_async_copy(act.at[0], act_s, lsem.at[0]),
        pltpu.make_async_copy(rhs, R.at[pl.ds(HR, 16), pl.ds(8, 32)], lsem.at[1]),
        pltpu.make_async_copy(scr, S.at[pl.ds(HS, 16), pl.ds(8, 32)], lsem.at[2]),
    ]
    for c in loads:
        c.start()

    @pl.when(gx == 0)
    def _():
        R[pl.ds(0, HR)] = jnp.zeros((HR, 48, 128), jnp.float32)
        S[pl.ds(0, HS)] = jnp.zeros((HS, 48, 128), jnp.float32)
        M[0] = jnp.zeros((48, 128), jnp.float32)

    @pl.when(gx == NGX - 1)
    def _():
        R[pl.ds(HR + 16, HR)] = jnp.zeros((HR, 48, 128), jnp.float32)
        S[pl.ds(HS + 16, HS)] = jnp.zeros((HS, 48, 128), jnp.float32)
        M[2] = jnp.zeros((48, 128), jnp.float32)

    def clear_rows(row):
        R[:, pl.ds(row, 8)] = jnp.zeros((28, 8, 128), jnp.float32)
        S[:, pl.ds(row, 8)] = jnp.zeros((24, 8, 128), jnp.float32)
        M[:, pl.ds(row, 8)] = jnp.zeros((3, 8, 128), jnp.float32)

    @pl.when(gy == 0)
    def _():
        clear_rows(0)

    @pl.when(gy == NGY - 1)
    def _():
        clear_rows(40)

    lane = lax.broadcasted_iota(jnp.int32, (8, 128), 1)
    loads[0].wait()
    entries = [act_s[0, q] for q in range(ACT)]
    count = jnp.int32(0)
    for e in entries:
        count = count + jnp.where(e >= 0, 1, 0)
    for w in range(2):
        number = lane // BLK + 8 * w
        own = jnp.zeros((8, 128), jnp.float32)
        for e in entries:
            own = jnp.where(number == e, 1.0, own)
        M[1, pl.ds(8 + 16 * w, 8)] = own
        M[1, pl.ds(16 + 16 * w, 8)] = own
    loads[1].wait()
    loads[2].wait()

    def prepare(p, carry):
        R[HR + p, pl.ds(8, 32)] = R[HR + p, pl.ds(8, 32)] * M[1, pl.ds(8, 32)]
        S[HS + p, pl.ds(8, 32)] = S[HS + p, pl.ds(8, 32)] - SIGMA
        return carry

    lax.fori_loop(0, 16, prepare, 0, unroll=4)

    pl.semaphore_wait(bar, 35)

    def pieces(i):
        dx, dy = NEIGHBOURS[i]
        rows = {0: (8, 8, 32), 1: (32, 0, 8), -1: (8, 40, 8)}[dy]
        out = []
        for n, (ref, h) in enumerate(((R, HR), (S, HS))):
            planes = {0: (h, h, 16), 1: (16, 0, h), -1: (h, h + 16, h)}[dx]
            out.append((ref.at[pl.ds(planes[0], planes[2]), pl.ds(rows[0], rows[2])],
                        ref.at[pl.ds(planes[1], planes[2]), pl.ds(rows[1], rows[2])], n))
        out.append((M.at[1, pl.ds(rows[0], rows[2])], M.at[1 - dx, pl.ds(rows[1], rows[2])], 2))
        return [pltpu.make_async_remote_copy(s, d, ssem.at[i, n], rsem.at[i, n],
                                             device_id=(gx + dx, gy + dy), device_id_type=MESH)
                for s, d, n in out]

    opposite = [NEIGHBOURS.index((-dx, -dy)) for dx, dy in NEIGHBOURS]
    for i, ok in enumerate(has):
        @pl.when(ok)
        def _():
            for c in pieces(i):
                c.start()
    for i in range(8):
        @pl.when(has[opposite[i]])
        def _():
            for c in pieces(i):
                c.wait_recv()

    lane48 = lax.broadcasted_iota(jnp.int32, (48, 128), 1)
    low1, low2 = lane48 < 1, lane48 < 2
    high1, high2 = lane48 > 126, lane48 > 125

    def zy_pass(src, count, tiles):
        first, rows = tiles

        def step(p, carry):
            v = src[p]
            p1 = jnp.where(low1, 0.0, pltpu.roll(v, 1, 1)) + jnp.where(high1, 0.0, pltpu.roll(v, 127, 1))
            p2 = jnp.where(low2, 0.0, pltpu.roll(v, 2, 1)) + jnp.where(high2, 0.0, pltpu.roll(v, 126, 1))
            MZ[p, pl.ds(8, 48)] = 66.0 * v + 26.0 * p1 + p2
            SZ[p, pl.ds(8, 48)] = 6.0 * v - 2.0 * p1 - p2

            def rows_at(ref, off):
                return ref[p, pl.ds(8 + first + off, rows)]

            s0 = rows_at(SZ, 0)
            s1 = rows_at(SZ, -1) + rows_at(SZ, 1)
            s2 = rows_at(SZ, -2) + rows_at(SZ, 2)
            m0 = rows_at(MZ, 0)
            m1 = rows_at(MZ, -1) + rows_at(MZ, 1)
            m2 = rows_at(MZ, -2) + rows_at(MZ, 2)
            IN[p, pl.ds(first, rows)] = (66.0 * s0 + 26.0 * s1 + s2) + (6.0 * m0 - 2.0 * m1 - m2)
            OUT[p, pl.ds(first, rows)] = 66.0 * m0 + 26.0 * m1 + m2
            return carry

        lax.fori_loop(0, count, step, 0, unroll=4)

    def x_value(p, src, smap, m, first, rows):
        def pick(ref, off):
            return ref[p + off, pl.ds(first, rows)]

        i1 = pick(IN, 1) + pick(IN, 3)
        i2 = pick(IN, 0) + pick(IN, 4)
        o1 = pick(OUT, 1) + pick(OUT, 3)
        o2 = pick(OUT, 0) + pick(OUT, 4)
        k = (66.0 * pick(IN, 2) + 26.0 * i1 + i2) + (6.0 * pick(OUT, 2) - 2.0 * o1 - o2)
        centre = src[p + 2, pl.ds(first, rows)]
        return m * (k * SCALE + S[p + smap, pl.ds(first, rows)] * centre), centre

    def fold(v):
        return (v[0:8] + v[8:16]) + (v[16:24] + v[24:32])

    def apply(src, dst, planes, halo, smap):
        zero = jnp.zeros((8, 128), jnp.float32)
        for lo, hi, dx in ((0, halo, 0), (halo, halo + 16, 1), (halo + 16, planes, 2)):
            def step(p, acc):
                value, centre = x_value(p, src, smap, M[dx], 0, 48)
                dst[p] = value
                if dx != 1:
                    return acc
                u, v = value[8:40], centre[8:40]
                return acc[0] + fold(v * u), acc[1] + fold(u * u), acc[2] + fold(u)

            out = lax.fori_loop(lo, hi, step, (zero, zero, zero), unroll=min(4, hi - lo))
            if dx == 1:
                sums = out
        return sums

    zero = jnp.zeros((8, 128), jnp.float32)

    def first_sums(p, acc):
        v = R[HR + p, pl.ds(8, 32)]
        return acc[0] + fold(v * v), acc[1] + fold(v)

    mu0, sum0 = lax.fori_loop(0, 16, first_sums, (zero, zero), unroll=4)
    zy_pass(R, 28, (0, 48))
    mu1, mu2, sum1 = apply(R, U1, 24, 4, 0)
    zy_pass(U1, 24, (0, 48))
    mu3, mu4, sum2 = apply(U1, U2, 20, 2, 2)
    zy_pass(U2, 20, (8, 32))

    def last(p, acc):
        value, centre = x_value(p, U2, 4, M[1, pl.ds(8, 32)], 8, 32)
        return acc + fold(value * centre)

    mu5 = lax.fori_loop(0, 16, last, zero, unroll=4)

    sub16 = lax.broadcasted_iota(jnp.int32, (16, 128), 0)
    lane16 = lax.broadcasted_iota(jnp.int32, (16, 128), 1)
    rows = jnp.zeros((16, 128), jnp.float32)
    for k, acc in enumerate((mu0, mu1, mu2, mu3, mu4, mu5, sum0, sum1, sum2)):
        rows = jnp.where(sub16 == k, jnp.sum(acc, axis=0, keepdims=True), rows)
    total = jnp.sum(rows, axis=1, keepdims=True)
    spread = jnp.where(lane16 == sub16, total, 0.0)
    values = jnp.sum(spread, axis=0, keepdims=True)
    lane1 = lax.broadcasted_iota(jnp.int32, (1, 128), 1)
    coarse = jnp.zeros((1, 128), jnp.float32)
    for k in range(6):
        coarse = jnp.where(lane1 == k, 1.5 * 2.0 ** (26 + k), coarse)
    rounded = (values + coarse) - coarse
    high = jnp.where(lane1 < 6, rounded, values)
    rest = jnp.where(lane1 < 6, values - rounded, 0.0)
    row = high + pltpu.roll(rest, 64, 1)
    row = jnp.where(lane1 == 9, count.astype(jnp.float32), row)

    pending = []

    ar1[gy] = row
    for j in (8, 7, 9, 6, 10, 5, 11, 4, 12, 3, 13, 2, 14, 1, 15):
        pltpu.make_async_remote_copy(
            ar1.at[gy], ar1.at[gy], asem.at[0], arsem.at[0],
            device_id=(gx, lax.rem(gy + j, NGY)), device_id_type=MESH).start()
    wait = pltpu.make_async_remote_copy(
        ar1.at[pl.ds(0, 15)], ar1.at[pl.ds(0, 15)], asem.at[0], arsem.at[0],
        device_id=(gx, lax.rem(gy + 1, NGY)), device_id_type=MESH)
    wait.wait_recv()
    pending.append(wait)
    row = jnp.sum(ar1[...], axis=0)

    ar2[6 + core] = row
    targets = [(off, c) for off in (-4, 3, -3, 2, -2, 1, -1) for c in (0, 1)]
    for off, c in targets:
        pltpu.make_async_remote_copy(
            ar2.at[6 + core], ar2.at[(3 - off) * 2 + core], asem.at[1], arsem.at[1],
            device_id=(at_z(off, c), gy), device_id_type=MESH).start()
    pltpu.make_async_remote_copy(
        ar2.at[6 + core], ar2.at[6 + core], asem.at[1], arsem.at[1],
        device_id=(at_z(0, 1 - core), gy), device_id_type=MESH).start()
    wait = pltpu.make_async_remote_copy(
        ar2.at[pl.ds(0, 15)], ar2.at[pl.ds(0, 15)], asem.at[1], arsem.at[1],
        device_id=(at_z(1, core), gy), device_id_type=MESH)
    wait.wait_recv()
    pending.append(wait)
    stage[...] = jnp.sum(ar2[...], axis=0)
    for slot, off in ((0, -4), (1, 4)):
        pltpu.make_async_remote_copy(
            stage, ar3.at[slot], asem.at[2], arsem.at[2],
            device_id=(at_z(off, core), gy), device_id_type=MESH).start()
    wait = pltpu.make_async_remote_copy(
        ar3, ar3, asem.at[2], arsem.at[2], device_id=(at_z(4, core), gy), device_id_type=MESH)
    wait.wait_recv()
    pending.append(wait)
    row = ar3[0] + ar3[1]

    goal = jnp.where(sub16 < 10, sub16, sub16 + 54)
    picked = jnp.sum(jnp.where(lane16 == goal, row, 0.0), axis=1, keepdims=True)
    value = [jnp.broadcast_to(picked[k:k + 1], (8, 128)) for k in range(16)]
    mu = [two_sum(value[k], value[10 + k]) for k in range(6)]
    c0, c1, c2 = cg_weights(mu)
    iso = (c0 * value[6] + c1 * value[7] + c2 * value[8]) / (value[9] * float(BLK ** 3))

    def tile5(v):
        return jnp.concatenate([v] * 5, axis=0)

    iso_out[...] = iso
    c0, c1, c2 = tile5(c0), tile5(c1), tile5(c2)

    def solve(p, carry):
        x_out[p] = c0 * R[HR + p, pl.ds(8, 40)] + c1 * U1[4 + p, pl.ds(8, 40)] + c2 * U2[2 + p, pl.ds(8, 40)]
        return carry

    lax.fori_loop(0, 17, solve, 0, unroll=True)

    for i, ok in enumerate(has):
        @pl.when(ok)
        def _():
            for c in pieces(i):
                c.wait_send()
    for c in pending:
        c.wait_send()


def crossing_kernel(x_ref, iso_ref, vis, ind_out, cross_out, G, W, BR, vis_s, sem):
    load = pltpu.make_async_copy(vis.at[0], vis_s, sem.at[0])
    load.start()
    store = pltpu.make_async_copy(x_ref.at[pl.ds(0, 16), pl.ds(0, 32)], ind_out, sem.at[1])
    store.start()
    lane = lax.broadcasted_iota(jnp.int32, (8, 128), 1)
    iso = jnp.concatenate([iso_ref[...]] * 5, axis=0)

    for p in range(17):
        G[p] = sigmoid4(x_ref[p] - iso)
    BR[pl.ds(16 * 96, 96)] = jnp.zeros((96, 128), jnp.float32)

    lane32 = lax.broadcasted_iota(jnp.int32, (32, 128), 1)
    edge = lane32 == 127
    empty = sigmoid4(0.0 - iso[0:32])
    group = lane // BLK
    odd = [(group // (1 << bit)) % 2 == 1 for bit in range(3)]
    load.wait()
    slots = []
    for q in range(VIS):
        n = vis_s[0, q]
        slots.append(jnp.where(n >= 0, n, 16) * 96)
    stores = [store]
    for e in range(3):
        for p in range(16):
            g = G[p, pl.ds(0, 32)]
            if e == 0:
                other = G[p + 1, pl.ds(0, 32)]
            elif e == 1:
                other = G[p, pl.ds(1, 32)]
            else:
                other = jnp.where(edge, empty, pltpu.roll(g, 127, 1))
            h = crossing_weight(g, other)
            for w in range(2):
                W[e, pl.ds((p // 4) * 128 + w * 64 + p % 4 * 16, 16)] = h[16 * w:16 * w + 16]
        for part in range(8):
            w, ib = part % 2, part // 2
            vs = [W[e, pl.ds(part * 64 + j, 8, stride=8)] for j in range(8)]
            for bit in range(3):
                d = 1 << bit
                new = list(vs)
                for j in range(8):
                    if not j & d:
                        lo, hi = vs[j], vs[j + d]
                        new[j] = jnp.where(odd[bit], pltpu.roll(hi, 16 * d, 1), lo)
                        new[j + d] = jnp.where(odd[bit], hi, pltpu.roll(lo, 128 - 16 * d, 1))
                vs = new
            for t in range(8):
                BR[pl.ds((w * 8 + t) * 96 + e * 32 + ib * 8, 8)] = vs[t]
        for q in range(VIS):
            start = pl.multiple_of(slots[q] + e * 32, 8)
            stores.append(pltpu.make_async_copy(
                BR.at[pl.ds(start, 32)], cross_out.at[pl.ds(q * 96 + e * 32, 32)], sem.at[2 + q * 3 + e]))
            stores[-1].start()
    for c in stores:
        c.wait()


def body(right_side, screening, active_blocks, visible_bricks):
    f32 = jnp.float32
    right_side, screening, active_blocks, visible_bricks = (
        pltpu.with_memory_space_constraint(v, pltpu.HBM)
        for v in (right_side, screening, active_blocks, visible_bricks))
    hbm = pl.BlockSpec(memory_space=pltpu.HBM)
    vmem = pl.BlockSpec(memory_space=pltpu.VMEM)
    x, iso = pl.pallas_call(
        solve_kernel,
        out_shape=(jax.ShapeDtypeStruct((17, 40, 128), f32), jax.ShapeDtypeStruct((8, 128), f32)),
        in_specs=[hbm] * 3,
        out_specs=(vmem, vmem),
        scratch_shapes=[
            pltpu.VMEM((28, 48, 128), f32),
            pltpu.VMEM((24, 48, 128), f32),
            pltpu.VMEM((3, 48, 128), f32),
            pltpu.VMEM((24, 48, 128), f32),
            pltpu.VMEM((20, 48, 128), f32),
            pltpu.VMEM((28, 64, 128), f32),
            pltpu.VMEM((28, 64, 128), f32),
            pltpu.VMEM((28, 48, 128), f32),
            pltpu.VMEM((28, 48, 128), f32),
            pltpu.SMEM((1, ACT), jnp.int32),
            pltpu.VMEM((16, 1, 128), f32),
            pltpu.VMEM((16, 1, 128), f32),
            pltpu.VMEM((2, 1, 128), f32),
            pltpu.VMEM((1, 128), f32),
            pltpu.SemaphoreType.DMA((3,)),
            pltpu.SemaphoreType.DMA((8, 3)),
            pltpu.SemaphoreType.DMA((8, 3)),
            pltpu.SemaphoreType.DMA((3,)),
            pltpu.SemaphoreType.DMA((3,)),
        ],
        compiler_params=pltpu.CompilerParams(
            collective_id=0, has_side_effects=True, vmem_limit_bytes=32 << 20),
    )(right_side, screening, active_blocks)
    indicator, crossing = pl.pallas_call(
        crossing_kernel,
        out_shape=(jax.ShapeDtypeStruct((16, 32, 128), f32), jax.ShapeDtypeStruct((VIS * 96, 128), f32)),
        in_specs=[vmem, vmem, hbm],
        out_specs=(hbm, hbm),
        scratch_shapes=[
            pltpu.VMEM((17, 40, 128), f32),
            pltpu.VMEM((3, 512, 128), f32),
            pltpu.VMEM((17 * 96, 128), f32),
            pltpu.SMEM((1, VIS), jnp.int32),
            pltpu.SemaphoreType.DMA((2 + 3 * VIS,)),
        ],
        compiler_params=pltpu.CompilerParams(vmem_limit_bytes=24 << 20),
    )(x, iso, visible_bricks)
    return indicator, crossing.reshape(VIS, 1, 3, BLK ** 3)


def solution(mesh):
    spec = P("gx", "gy", None)
    return jax.shard_map(
        body,
        mesh=mesh,
        in_specs=(spec, spec, spec, spec),
        out_specs=(spec, P("gx", "gy", None, None)),
        check_vma=False,
    )
```

```python
import jax
import jax.numpy as jnp
from jax import lax
from jax.experimental import pallas as pl
from jax.experimental.pallas import tpu as pltpu
from jax.sharding import PartitionSpec as P

MESH = pl.DeviceIdType.MESH
BLK = 16
ACT = 12
VIS = 8
NGX = 32
NGY = 16
NZ = 16
SIGMA = 2.5
HR = 6
HS = 4
SCALE = 1.0 / 86400.0
NEIGHBOURS = [(1, 1), (1, -1), (-1, 1), (-1, -1), (0, 1), (0, -1), (1, 0), (-1, 0)]


def two_sum(a, b):
    s = a + b
    t = s - a
    return s, (a - (s - t)) + (b - t)


def quick_two_sum(a, b):
    s = a + b
    return s, b - (s - a)


def split(a):
    c = 4097.0 * a
    hi = c - (c - a)
    return hi, a - hi


def two_prod(a, b):
    p = a * b
    ah, al = split(a)
    bh, bl = split(b)
    return p, ((ah * bh - p) + ah * bl + al * bh) + al * bl


def dd_add(x, y):
    s, e = two_sum(x[0], y[0])
    return quick_two_sum(s, e + (x[1] + y[1]))


def dd_neg(x):
    return -x[0], -x[1]


def dd_sub(x, y):
    return dd_add(x, dd_neg(y))


def dd_mul(x, y):
    p, e = two_prod(x[0], y[0])
    return quick_two_sum(p, e + (x[0] * y[1] + x[1] * y[0]))


def dd_div(x, y):
    q = x[0] / y[0]
    r = dd_sub(x, dd_mul(y, (q, jnp.zeros_like(q))))
    return quick_two_sum(q, r[0] / y[0])


def cg_weights(mu):
    one = (jnp.ones_like(mu[0][0]), jnp.zeros_like(mu[0][0]))
    inv = dd_div(one, mu[0])
    row = [dd_mul(m, inv) for m in mu[1:]]
    a = row[0]
    level = [dd_sub(row[k + 1], dd_mul(a, row[k])) for k in range(4)]
    first = [(jnp.zeros_like(a[0]), jnp.zeros_like(a[0]))] + level
    central = []
    for _ in range(4):
        first = [dd_sub(first[k + 1], dd_mul(a, first[k])) for k in range(len(first) - 1)]
        central.append(first[0])
    m2, m3, m4, m5 = central
    tiny = 1e-30
    m2s = (jnp.maximum(m2[0], tiny), jnp.where(m2[0] > tiny, m2[1], 0.0))
    b1 = dd_div(m3, m2s)
    m22 = dd_mul(m2, m2)
    h2 = dd_sub(dd_sub(m4, dd_mul(b1, m3)), m22)
    h2s = jnp.maximum(h2[0], tiny)
    inner = dd_sub(dd_mul(b1, m3), dd_add(m4, m4))
    inner = dd_add(inner, dd_add(m22, m22))
    top = dd_add(m5, dd_mul(b1, inner))
    m23 = dd_mul(m2, m3)
    top = dd_sub(top, dd_add(m23, m23))
    d0 = a[0] + SIGMA
    d1 = jnp.clip(d0 + b1[0], 0.25, 9.0)
    d2 = jnp.clip(d0 + top[0] / h2s, 0.25, 9.0)
    beta1 = jnp.maximum(m2[0], 0.0)
    beta2 = jnp.clip(h2[0] / m2s[0], 0.0, 25.0)
    bb1 = d1 - d0
    minor = d1 * d2 - beta2
    y2 = 1.0 / (d0 * minor - beta1 * d2)
    y1 = -d2 * y2
    y0 = minor * y2
    c2 = y2
    c1 = y1 - y2 * (2.0 * a[0] + bb1)
    c0 = y0 - a[0] * y1 + y2 * (a[0] * a[0] + a[0] * bb1 - m2[0])
    return c0, c1, c2


def sigmoid4(v):
    return 1.0 / (1.0 + jnp.exp(-4.0 * v))


def crossing_weight(lower, upper):
    return lower * (1.0 - upper) + (1.0 - lower) * upper


def solve_kernel(rhs, scr, act, x_out, iso_out,
           R, S, M, U1, U2, MZ, SZ, IN, OUT, act_s, ar1, ar2,
                 lsem, ssem, rsem, asem, arsem, token):
    gx = lax.axis_index("gx")
    gy = lax.axis_index("gy")
    z = gx // 2
    core = lax.rem(gx, 2)

    def at_z(off):
        return lax.rem(z + off + NZ, NZ) * 2 + core

    bar = pltpu.get_barrier_semaphore()

    def tell(x, y):
        pl.semaphore_signal(bar, inc=1, device_id=(x, y), device_id_type=MESH)

    other_chip = lax.rem(gx + 2 * core - 1 + NGX, NGX)
    for dy in (1, -1):
        tell(other_chip, lax.rem(gy + dy + NGY, NGY))
    tell(other_chip, gy)
    for j in (1, 15, 10, 6, 9, 7, 11, 5, 8, 2, 14, 13, 3, 12, 4):
        for c in (1 - core, core):
            tell(2 * z + c, lax.rem(gy + j, NGY))
    tell(2 * z + 1 - core, gy)
    for off in (4, -4, 3, -3, 2, -2, 1, -1):
        tell(at_z(off), gy)
    has = []
    for dx, dy in NEIGHBOURS:
        ok = None
        for cond in ([gx < NGX - 1] if dx == 1 else []) + ([gx > 0] if dx == -1 else []) + (
            [gy < NGY - 1] if dy == 1 else []) + ([gy > 0] if dy == -1 else []):
            ok = cond if ok is None else jnp.logical_and(ok, cond)
        has.append(ok)
    loads = [
        pltpu.make_async_copy(act.at[0], act_s, lsem.at[0]),
        pltpu.make_async_copy(rhs, R.at[pl.ds(HR, 16), pl.ds(8, 32)], lsem.at[1]),
        pltpu.make_async_copy(scr, S.at[pl.ds(HS, 16), pl.ds(8, 32)], lsem.at[2]),
    ]
    for c in loads:
        c.start()

    @pl.when(gx == 0)
    def _():
        R[pl.ds(0, HR)] = jnp.zeros((HR, 48, 128), jnp.float32)
        S[pl.ds(0, HS)] = jnp.zeros((HS, 48, 128), jnp.float32)
        M[0] = jnp.zeros((4, 128), jnp.float32)

    @pl.when(gx == NGX - 1)
    def _():
        R[pl.ds(HR + 16, HR)] = jnp.zeros((HR, 48, 128), jnp.float32)
        S[pl.ds(HS + 16, HS)] = jnp.zeros((HS, 48, 128), jnp.float32)
        M[2] = jnp.zeros((4, 128), jnp.float32)

    def clear_rows(row, kind):
        R[:, pl.ds(row, 8)] = jnp.zeros((28, 8, 128), jnp.float32)
        S[:, pl.ds(row, 8)] = jnp.zeros((24, 8, 128), jnp.float32)
        M[:, pl.ds(kind, 1)] = jnp.zeros((3, 1, 128), jnp.float32)

    @pl.when(gy == 0)
    def _():
        clear_rows(0, 0)

    @pl.when(gy == NGY - 1)
    def _():
        clear_rows(40, 3)

    lane = lax.broadcasted_iota(jnp.int32, (8, 128), 1)
    loads[0].wait()
    entries = [act_s[0, q] for q in range(ACT)]
    count = jnp.int32(0)
    for e in entries:
        count = count + jnp.where(e >= 0, 1, 0)
    for w in range(2):
        number = lane // BLK + 8 * w
        own = jnp.zeros((8, 128), jnp.float32)
        for e in entries:
            own = jnp.where(number == e, 1.0, own)
        M[1, pl.ds(1 + w, 1)] = own[0:1]
    loads[1].wait()
    loads[2].wait()

    def mask_rows(dx, kinds):
        tiles = [jnp.broadcast_to(M[dx, pl.ds(k, 1)], (8, 128)) for k in range(4)]
        return jnp.concatenate([tiles[k] for k in kinds], axis=0)

    own = mask_rows(1, (1, 1, 2, 2))

    def prepare(p, carry):
        R[HR + p, pl.ds(8, 32)] = R[HR + p, pl.ds(8, 32)] * own
        S[HS + p, pl.ds(8, 32)] = S[HS + p, pl.ds(8, 32)] - SIGMA
        return carry

    lax.fori_loop(0, 16, prepare, 0, unroll=4)

    pl.semaphore_wait(bar, 42)
    for off in (4, -4):
        pl.semaphore_signal(token, inc=1, device_id=(at_z(off), gy), device_id_type=MESH)

    def pieces(i, which):
        dx, dy = NEIGHBOURS[i]
        out = []
        for n in which:
            if n == 2:
                first, size = {0: (1, 2), 1: (2, 1), -1: (1, 1)}[dy]
                src = M.at[1, pl.ds(first, size)]
                dst = M.at[1 - dx, pl.ds({0: 1, 1: 0, -1: 3}[dy], size)]
            else:
                ref, h = ((R, HR), (S, HS))[n]
                planes = {0: (h, h, 16), 1: (16, 0, h), -1: (h, h + 16, h)}[dx]
                rows = {0: (8, 8, 32), 1: (40 - h, 8 - h, h), -1: (8, 40, h)}[dy]
                src = ref.at[pl.ds(planes[0], planes[2]), pl.ds(rows[0], rows[2])]
                dst = ref.at[pl.ds(planes[1], planes[2]), pl.ds(rows[1], rows[2])]
            out.append(pltpu.make_async_remote_copy(
                src, dst, ssem.at[i, n], rsem.at[i, n],
                device_id=(gx + dx, gy + dy), device_id_type=MESH))
        return out

    opposite = [NEIGHBOURS.index((-dx, -dy)) for dx, dy in NEIGHBOURS]

    def receive(which):
        for i in range(8):
            @pl.when(has[opposite[i]])
            def _():
                for c in pieces(i, which):
                    c.wait_recv()

    for which in ((0,), (2, 1)):
        for i, ok in enumerate(has):
            @pl.when(ok)
            def _():
                for c in pieces(i, which):
                    c.start()

    zero = jnp.zeros((8, 128), jnp.float32)

    def fold(v):
        return (v[0:8] + v[8:16]) + (v[16:24] + v[24:32])

    def first_sums(p, acc):
        v = R[HR + p, pl.ds(8, 32)]
        return acc[0] + fold(v * v), acc[1] + fold(v)

    mu0, sum0 = lax.fori_loop(0, 16, first_sums, (zero, zero), unroll=4)
    receive((0,))

    lane48 = lax.broadcasted_iota(jnp.int32, (48, 128), 1)
    low1, low2 = lane48 < 1, lane48 < 2
    high1, high2 = lane48 > 126, lane48 > 125

    def zy_pass(src, count, tiles):
        first, rows = tiles

        def step(p, carry):
            v = src[p]
            p1 = jnp.where(low1, 0.0, pltpu.roll(v, 1, 1)) + jnp.where(high1, 0.0, pltpu.roll(v, 127, 1))
            p2 = jnp.where(low2, 0.0, pltpu.roll(v, 2, 1)) + jnp.where(high2, 0.0, pltpu.roll(v, 126, 1))
            MZ[p, pl.ds(8, 48)] = 66.0 * v + 26.0 * p1 + p2
            SZ[p, pl.ds(8, 48)] = 6.0 * v - 2.0 * p1 - p2

            def rows_at(ref, off):
                return ref[p, pl.ds(8 + first + off, rows)]

            s0 = rows_at(SZ, 0)
            s1 = rows_at(SZ, -1) + rows_at(SZ, 1)
            s2 = rows_at(SZ, -2) + rows_at(SZ, 2)
            m0 = rows_at(MZ, 0)
            m1 = rows_at(MZ, -1) + rows_at(MZ, 1)
            m2 = rows_at(MZ, -2) + rows_at(MZ, 2)
            IN[p, pl.ds(first, rows)] = (66.0 * s0 + 26.0 * s1 + s2) + (6.0 * m0 - 2.0 * m1 - m2)
            OUT[p, pl.ds(first, rows)] = 66.0 * m0 + 26.0 * m1 + m2
            return carry

        lax.fori_loop(0, count, step, 0, unroll=4)

    def x_value(p, src, smap, m, first, rows):
        def pick(ref, off):
            return ref[p + off, pl.ds(first, rows)]

        i1 = pick(IN, 1) + pick(IN, 3)
        i2 = pick(IN, 0) + pick(IN, 4)
        o1 = pick(OUT, 1) + pick(OUT, 3)
        o2 = pick(OUT, 0) + pick(OUT, 4)
        k = (66.0 * pick(IN, 2) + 26.0 * i1 + i2) + (6.0 * pick(OUT, 2) - 2.0 * o1 - o2)
        centre = src[p + 2, pl.ds(first, rows)]
        return m * (k * SCALE + S[p + smap, pl.ds(first, rows)] * centre), centre

    def apply(src, dst, planes, halo, smap):
        for lo, hi, dx in ((0, halo, 0), (halo, halo + 16, 1), (halo + 16, planes, 2)):
            m = mask_rows(dx, (0, 1, 1, 2, 2, 3))

            def step(p, acc):
                value, centre = x_value(p, src, smap, m, 0, 48)
                dst[p] = value
                if dx != 1:
                    return acc
                u, v = value[8:40], centre[8:40]
                return acc[0] + fold(v * u), acc[1] + fold(u * u), acc[2] + fold(u)

            out = lax.fori_loop(lo, hi, step, (zero, zero, zero), unroll=min(4, hi - lo))
            if dx == 1:
                sums = out
        return sums

    zy_pass(R, 28, (0, 48))
    receive((2, 1))
    mu1, mu2, sum1 = apply(R, U1, 24, 4, 0)
    zy_pass(U1, 24, (0, 48))
    mu3, mu4, sum2 = apply(U1, U2, 20, 2, 2)
    zy_pass(U2, 20, (8, 32))

    def last(p, acc):
        value, centre = x_value(p, U2, 4, own, 8, 32)
        return acc + fold(value * centre)

    mu5 = lax.fori_loop(0, 16, last, zero, unroll=4)

    sub16 = lax.broadcasted_iota(jnp.int32, (16, 128), 0)
    lane16 = lax.broadcasted_iota(jnp.int32, (16, 128), 1)
    rows = jnp.zeros((16, 128), jnp.float32)
    for k, acc in enumerate((mu0, mu1, mu2, mu3, mu4, mu5, sum0, sum1, sum2)):
        rows = jnp.where(sub16 == k, jnp.sum(acc, axis=0, keepdims=True), rows)
    total = jnp.sum(rows, axis=1, keepdims=True)
    spread = jnp.where(lane16 == sub16, total, 0.0)
    values = jnp.sum(spread, axis=0, keepdims=True)
    lane1 = lax.broadcasted_iota(jnp.int32, (1, 128), 1)
    coarse = jnp.zeros((1, 128), jnp.float32)
    for k in range(6):
        coarse = jnp.where(lane1 == k, 1.5 * 2.0 ** (26 + k), coarse)
    rounded = (values + coarse) - coarse
    high = jnp.where(lane1 < 6, rounded, values)
    rest = jnp.where(lane1 < 6, values - rounded, 0.0)
    row = high + pltpu.roll(rest, 64, 1)
    row = jnp.where(lane1 == 9, count.astype(jnp.float32), row)

    pending = []
    mine = gy * 2 + core
    ar1[mine] = row
    for j in (10, 6, 9, 7, 11, 5, 8, 2, 14, 13, 3, 1, 15, 12, 4, 0):
        for c in (1 - core, core):
            if j == 0 and c is core:
                continue
            pltpu.make_async_remote_copy(
                ar1.at[mine], ar1.at[mine], asem.at[0], arsem.at[0],
                device_id=(2 * z + c, lax.rem(gy + j, NGY)), device_id_type=MESH).start()
    wait = pltpu.make_async_remote_copy(
        ar1.at[pl.ds(0, 31)], ar1.at[pl.ds(0, 31)], asem.at[0], arsem.at[0],
        device_id=(2 * z + 1 - core, gy), device_id_type=MESH)
    wait.wait_recv()
    pending.append(wait)

    ar2[z] = jnp.sum(ar1[...], axis=0)
    pl.semaphore_wait(token, 2)
    for off in (8, 7, -7, 6, -6, 5, -5, 4, -4, 3, -3, 2, -2, 1, -1):
        pltpu.make_async_remote_copy(
            ar2.at[z], ar2.at[z], asem.at[1], arsem.at[1],
            device_id=(at_z(off), gy), device_id_type=MESH).start()
    wait = pltpu.make_async_remote_copy(
        ar2.at[pl.ds(0, 15)], ar2.at[pl.ds(0, 15)], asem.at[1], arsem.at[1],
        device_id=(at_z(1), gy), device_id_type=MESH)
    wait.wait_recv()
    pending.append(wait)
    row = jnp.sum(ar2[...], axis=0)

    goal = jnp.where(sub16 < 10, sub16, sub16 + 54)
    picked = jnp.sum(jnp.where(lane16 == goal, row, 0.0), axis=1, keepdims=True)
    value = [jnp.broadcast_to(picked[k:k + 1], (8, 128)) for k in range(16)]
    mu = [two_sum(value[k], value[10 + k]) for k in range(6)]
    c0, c1, c2 = cg_weights(mu)
    iso = (c0 * value[6] + c1 * value[7] + c2 * value[8]) / (value[9] * float(BLK ** 3))

    def tile5(v):
        return jnp.concatenate([v] * 5, axis=0)

    iso_out[...] = iso
    c0, c1, c2 = tile5(c0), tile5(c1), tile5(c2)

    def solve(p, carry):
        x_out[p] = c0 * R[HR + p, pl.ds(8, 40)] + c1 * U1[4 + p, pl.ds(8, 40)] + c2 * U2[2 + p, pl.ds(8, 40)]
        return carry

    lax.fori_loop(0, 17, solve, 0, unroll=True)

    for i, ok in enumerate(has):
        @pl.when(ok)
        def _():
            for c in pieces(i, (0, 1, 2)):
                c.wait_send()
    for c in pending:
        c.wait_send()


def crossing_kernel(x_ref, iso_ref, vis, ind_out, cross_out, G, W, BR, vis_s, sem):
    load = pltpu.make_async_copy(vis.at[0], vis_s, sem.at[0])
    load.start()
    store = pltpu.make_async_copy(x_ref.at[pl.ds(0, 16), pl.ds(0, 32)], ind_out, sem.at[1])
    store.start()
    lane = lax.broadcasted_iota(jnp.int32, (8, 128), 1)
    iso = jnp.concatenate([iso_ref[...]] * 5, axis=0)

    for p in range(17):
        G[p] = sigmoid4(x_ref[p] - iso)
    BR[pl.ds(16 * 96, 96)] = jnp.zeros((96, 128), jnp.float32)

    lane32 = lax.broadcasted_iota(jnp.int32, (32, 128), 1)
    edge = lane32 == 127
    empty = sigmoid4(0.0 - iso[0:32])
    group = lane // BLK
    odd = [(group // (1 << bit)) % 2 == 1 for bit in range(3)]
    load.wait()
    slots = []
    for q in range(VIS):
        n = vis_s[0, q]
        slots.append(jnp.where(n >= 0, n, 16) * 96)
    stores = [store]
    for e in range(3):
        for p in range(16):
            g = G[p, pl.ds(0, 32)]
            if e == 0:
                other = G[p + 1, pl.ds(0, 32)]
            elif e == 1:
                other = G[p, pl.ds(1, 32)]
            else:
                other = jnp.where(edge, empty, pltpu.roll(g, 127, 1))
            h = crossing_weight(g, other)
            for w in range(2):
                W[e, pl.ds((p // 4) * 128 + w * 64 + p % 4 * 16, 16)] = h[16 * w:16 * w + 16]
        for part in range(8):
            w, ib = part % 2, part // 2
            vs = [W[e, pl.ds(part * 64 + j, 8, stride=8)] for j in range(8)]
            for bit in range(3):
                d = 1 << bit
                new = list(vs)
                for j in range(8):
                    if not j & d:
                        lo, hi = vs[j], vs[j + d]
                        new[j] = jnp.where(odd[bit], pltpu.roll(hi, 16 * d, 1), lo)
                        new[j + d] = jnp.where(odd[bit], hi, pltpu.roll(lo, 128 - 16 * d, 1))
                vs = new
            for t in range(8):
                BR[pl.ds((w * 8 + t) * 96 + e * 32 + ib * 8, 8)] = vs[t]
        for q in range(VIS):
            start = pl.multiple_of(slots[q] + e * 32, 8)
            stores.append(pltpu.make_async_copy(
                BR.at[pl.ds(start, 32)], cross_out.at[pl.ds(q * 96 + e * 32, 32)], sem.at[2 + q * 3 + e]))
            stores[-1].start()
    for c in stores:
        c.wait()


def body(right_side, screening, active_blocks, visible_bricks):
    f32 = jnp.float32
    right_side, screening, active_blocks, visible_bricks = (
        pltpu.with_memory_space_constraint(v, pltpu.HBM)
        for v in (right_side, screening, active_blocks, visible_bricks))
    hbm = pl.BlockSpec(memory_space=pltpu.HBM)
    vmem = pl.BlockSpec(memory_space=pltpu.VMEM)
    x, iso = pl.pallas_call(
        solve_kernel,
        out_shape=(jax.ShapeDtypeStruct((17, 40, 128), f32), jax.ShapeDtypeStruct((8, 128), f32)),
        in_specs=[hbm] * 3,
        out_specs=(vmem, vmem),
        scratch_shapes=[
            pltpu.VMEM((28, 48, 128), f32),
            pltpu.VMEM((24, 48, 128), f32),
            pltpu.VMEM((3, 4, 128), f32),
            pltpu.VMEM((24, 48, 128), f32),
            pltpu.VMEM((20, 48, 128), f32),
            pltpu.VMEM((28, 64, 128), f32),
            pltpu.VMEM((28, 64, 128), f32),
            pltpu.VMEM((28, 48, 128), f32),
            pltpu.VMEM((28, 48, 128), f32),
            pltpu.SMEM((1, ACT), jnp.int32),
            pltpu.VMEM((32, 1, 128), f32),
            pltpu.VMEM((16, 1, 128), f32),
            pltpu.SemaphoreType.DMA((3,)),
            pltpu.SemaphoreType.DMA((8, 3)),
            pltpu.SemaphoreType.DMA((8, 3)),
            pltpu.SemaphoreType.DMA((2,)),
            pltpu.SemaphoreType.DMA((2,)),
            pltpu.SemaphoreType.REGULAR,
        ],
        compiler_params=pltpu.CompilerParams(
            collective_id=0, has_side_effects=True, vmem_limit_bytes=32 << 20),
    )(right_side, screening, active_blocks)
    indicator, crossing = pl.pallas_call(
        crossing_kernel,
        out_shape=(jax.ShapeDtypeStruct((16, 32, 128), f32), jax.ShapeDtypeStruct((VIS * 96, 128), f32)),
        in_specs=[vmem, vmem, hbm],
        out_specs=(hbm, hbm),
        scratch_shapes=[
            pltpu.VMEM((17, 40, 128), f32),
            pltpu.VMEM((3, 512, 128), f32),
            pltpu.VMEM((17 * 96, 128), f32),
            pltpu.SMEM((1, VIS), jnp.int32),
            pltpu.SemaphoreType.DMA((2 + 3 * VIS,)),
        ],
        compiler_params=pltpu.CompilerParams(vmem_limit_bytes=24 << 20),
    )(x, iso, visible_bricks)
    return indicator, crossing.reshape(VIS, 1, 3, BLK ** 3)


def solution(mesh):
    spec = P("gx", "gy", None)
    return jax.shard_map(
        body,
        mesh=mesh,
        in_specs=(spec, spec, spec, spec),
        out_specs=(spec, P("gx", "gy", None, None)),
        check_vma=False,
    )
```

```python
import jax
import jax.numpy as jnp
from jax import lax
from jax.experimental import pallas as pl
from jax.experimental.pallas import tpu as pltpu
from jax.sharding import PartitionSpec as P

MESH = pl.DeviceIdType.MESH
BLK = 16
ACT = 12
VIS = 8
NGX = 32
NGY = 16
NZ = 16
SIGMA = 2.5
HR = 6
HS = 4
SCALE = 1.0 / 86400.0
NEIGHBOURS = [(1, 1), (1, -1), (-1, 1), (-1, -1), (0, 1), (0, -1), (1, 0), (-1, 0)]


def two_sum(a, b):
    s = a + b
    t = s - a
    return s, (a - (s - t)) + (b - t)


def quick_two_sum(a, b):
    s = a + b
    return s, b - (s - a)


def split(a):
    c = 4097.0 * a
    hi = c - (c - a)
    return hi, a - hi


def two_prod(a, b):
    p = a * b
    ah, al = split(a)
    bh, bl = split(b)
    return p, ((ah * bh - p) + ah * bl + al * bh) + al * bl


def dd_add(x, y):
    s, e = two_sum(x[0], y[0])
    return quick_two_sum(s, e + (x[1] + y[1]))


def dd_neg(x):
    return -x[0], -x[1]


def dd_sub(x, y):
    return dd_add(x, dd_neg(y))


def dd_mul(x, y):
    p, e = two_prod(x[0], y[0])
    return quick_two_sum(p, e + (x[0] * y[1] + x[1] * y[0]))


def dd_div(x, y):
    q = x[0] / y[0]
    r = dd_sub(x, dd_mul(y, (q, jnp.zeros_like(q))))
    return quick_two_sum(q, r[0] / y[0])


def cg_weights(mu):
    one = (jnp.ones_like(mu[0][0]), jnp.zeros_like(mu[0][0]))
    inv = dd_div(one, mu[0])
    row = [dd_mul(m, inv) for m in mu[1:]]
    a = row[0]
    level = [dd_sub(row[k + 1], dd_mul(a, row[k])) for k in range(4)]
    first = [(jnp.zeros_like(a[0]), jnp.zeros_like(a[0]))] + level
    central = []
    for _ in range(4):
        first = [dd_sub(first[k + 1], dd_mul(a, first[k])) for k in range(len(first) - 1)]
        central.append(first[0])
    m2, m3, m4, m5 = central
    tiny = 1e-30
    m2s = (jnp.maximum(m2[0], tiny), jnp.where(m2[0] > tiny, m2[1], 0.0))
    b1 = dd_div(m3, m2s)
    m22 = dd_mul(m2, m2)
    h2 = dd_sub(dd_sub(m4, dd_mul(b1, m3)), m22)
    h2s = jnp.maximum(h2[0], tiny)
    inner = dd_sub(dd_mul(b1, m3), dd_add(m4, m4))
    inner = dd_add(inner, dd_add(m22, m22))
    top = dd_add(m5, dd_mul(b1, inner))
    m23 = dd_mul(m2, m3)
    top = dd_sub(top, dd_add(m23, m23))
    d0 = a[0] + SIGMA
    d1 = jnp.clip(d0 + b1[0], 0.25, 9.0)
    d2 = jnp.clip(d0 + top[0] / h2s, 0.25, 9.0)
    beta1 = jnp.maximum(m2[0], 0.0)
    beta2 = jnp.clip(h2[0] / m2s[0], 0.0, 25.0)
    bb1 = d1 - d0
    minor = d1 * d2 - beta2
    y2 = 1.0 / (d0 * minor - beta1 * d2)
    y1 = -d2 * y2
    y0 = minor * y2
    c2 = y2
    c1 = y1 - y2 * (2.0 * a[0] + bb1)
    c0 = y0 - a[0] * y1 + y2 * (a[0] * a[0] + a[0] * bb1 - m2[0])
    return c0, c1, c2


def sigmoid4(v):
    return 1.0 / (1.0 + jnp.exp(-4.0 * v))


def crossing_weight(lower, upper):
    return lower * (1.0 - upper) + (1.0 - lower) * upper


def solve_kernel(rhs, scr, act, x_out, iso_out,
           R, S, M, U1, U2, MZ, SZ, IN, OUT, act_s, ar1, ar2,
                 lsem, ssem, rsem, asem, arsem, token):
    gx = lax.axis_index("gx")
    gy = lax.axis_index("gy")
    z = gx // 2
    core = lax.rem(gx, 2)

    def at_z(off):
        return lax.rem(z + off + NZ, NZ) * 2 + core

    bar = pltpu.get_barrier_semaphore()

    def tell(x, y):
        pl.semaphore_signal(bar, inc=1, device_id=(x, y), device_id_type=MESH)

    other_chip = lax.rem(gx + 2 * core - 1 + NGX, NGX)
    for dy in (1, -1):
        tell(other_chip, lax.rem(gy + dy + NGY, NGY))
    tell(other_chip, gy)
    for j in (1, 15, 10, 6, 9, 7, 11, 5, 8, 2, 14, 13, 3, 12, 4):
        for c in (1 - core, core):
            tell(2 * z + c, lax.rem(gy + j, NGY))
    tell(2 * z + 1 - core, gy)
    for off in (4, -4, 3, -3, 2, -2, 1, -1):
        tell(at_z(off), gy)
    has = []
    for dx, dy in NEIGHBOURS:
        ok = None
        for cond in ([gx < NGX - 1] if dx == 1 else []) + ([gx > 0] if dx == -1 else []) + (
            [gy < NGY - 1] if dy == 1 else []) + ([gy > 0] if dy == -1 else []):
            ok = cond if ok is None else jnp.logical_and(ok, cond)
        has.append(ok)
    loads = [
        pltpu.make_async_copy(act.at[0], act_s, lsem.at[0]),
        pltpu.make_async_copy(rhs, R.at[pl.ds(HR, 16), pl.ds(8, 32)], lsem.at[1]),
        pltpu.make_async_copy(scr, S.at[pl.ds(HS, 16), pl.ds(8, 32)], lsem.at[2]),
    ]
    for c in loads:
        c.start()

    @pl.when(gx == 0)
    def _():
        R[pl.ds(0, HR)] = jnp.zeros((HR, 48, 128), jnp.float32)
        S[pl.ds(0, HS)] = jnp.zeros((HS, 48, 128), jnp.float32)
        M[0] = jnp.zeros((4, 128), jnp.float32)

    @pl.when(gx == NGX - 1)
    def _():
        R[pl.ds(HR + 16, HR)] = jnp.zeros((HR, 48, 128), jnp.float32)
        S[pl.ds(HS + 16, HS)] = jnp.zeros((HS, 48, 128), jnp.float32)
        M[2] = jnp.zeros((4, 128), jnp.float32)

    def clear_rows(row, kind):
        R[:, pl.ds(row, 8)] = jnp.zeros((28, 8, 128), jnp.float32)
        S[:, pl.ds(row, 8)] = jnp.zeros((24, 8, 128), jnp.float32)
        M[:, pl.ds(kind, 1)] = jnp.zeros((3, 1, 128), jnp.float32)

    @pl.when(gy == 0)
    def _():
        clear_rows(0, 0)

    @pl.when(gy == NGY - 1)
    def _():
        clear_rows(40, 3)

    lane = lax.broadcasted_iota(jnp.int32, (8, 128), 1)
    loads[0].wait()
    entries = [act_s[0, q] for q in range(ACT)]
    count = jnp.int32(0)
    for e in entries:
        count = count + jnp.where(e >= 0, 1, 0)
    for w in range(2):
        number = lane // BLK + 8 * w
        own = jnp.zeros((8, 128), jnp.float32)
        for e in entries:
            own = jnp.where(number == e, 1.0, own)
        M[1, pl.ds(1 + w, 1)] = own[0:1]
    loads[1].wait()
    loads[2].wait()

    def mask_rows(dx, kinds):
        tiles = [jnp.broadcast_to(M[dx, pl.ds(k, 1)], (8, 128)) for k in range(4)]
        return jnp.concatenate([tiles[k] for k in kinds], axis=0)

    own = mask_rows(1, (1, 1, 2, 2))

    def prepare(p, carry):
        R[HR + p, pl.ds(8, 32)] = R[HR + p, pl.ds(8, 32)] * own
        S[HS + p, pl.ds(8, 32)] = S[HS + p, pl.ds(8, 32)] - SIGMA
        return carry

    lax.fori_loop(0, 16, prepare, 0, unroll=4)

    pl.semaphore_wait(bar, 42)
    for off in (4, -4):
        pl.semaphore_signal(token, inc=1, device_id=(at_z(off), gy), device_id_type=MESH)

    def pieces(i, which):
        dx, dy = NEIGHBOURS[i]
        out = []
        for n in which:
            if n == 2:
                first, size = {0: (1, 2), 1: (2, 1), -1: (1, 1)}[dy]
                src = M.at[1, pl.ds(first, size)]
                dst = M.at[1 - dx, pl.ds({0: 1, 1: 0, -1: 3}[dy], size)]
            else:
                ref, h = ((R, HR), (S, HS))[n]
                planes = {0: (h, h, 16), 1: (16, 0, h), -1: (h, h + 16, h)}[dx]
                rows = {0: (8, 8, 32), 1: (40 - h, 8 - h, h), -1: (8, 40, h)}[dy]
                src = ref.at[pl.ds(planes[0], planes[2]), pl.ds(rows[0], rows[2])]
                dst = ref.at[pl.ds(planes[1], planes[2]), pl.ds(rows[1], rows[2])]
            out.append(pltpu.make_async_remote_copy(
                src, dst, ssem.at[i, n], rsem.at[i, n],
                device_id=(gx + dx, gy + dy), device_id_type=MESH))
        return out

    opposite = [NEIGHBOURS.index((-dx, -dy)) for dx, dy in NEIGHBOURS]

    def receive(which):
        for i in range(8):
            @pl.when(has[opposite[i]])
            def _():
                for c in pieces(i, which):
                    c.wait_recv()

    for which in ((0,), (2, 1)):
        for i, ok in enumerate(has):
            @pl.when(ok)
            def _():
                for c in pieces(i, which):
                    c.start()

    zero = jnp.zeros((8, 128), jnp.float32)

    def fold(v):
        return (v[0:8] + v[8:16]) + (v[16:24] + v[24:32])

    def first_sums(p, acc):
        v = R[HR + p, pl.ds(8, 32)]
        return acc[0] + fold(v * v), acc[1] + fold(v)

    mu0, sum0 = lax.fori_loop(0, 16, first_sums, (zero, zero), unroll=4)
    receive((0,))

    lane48 = lax.broadcasted_iota(jnp.int32, (48, 128), 1)
    low1, low2 = lane48 < 1, lane48 < 2
    high1, high2 = lane48 > 126, lane48 > 125

    def zy_pass(src, count, tiles):
        first, rows = tiles

        def step(p, carry):
            v = src[p]
            p1 = jnp.where(low1, 0.0, pltpu.roll(v, 1, 1)) + jnp.where(high1, 0.0, pltpu.roll(v, 127, 1))
            p2 = jnp.where(low2, 0.0, pltpu.roll(v, 2, 1)) + jnp.where(high2, 0.0, pltpu.roll(v, 126, 1))
            MZ[p, pl.ds(8, 48)] = 66.0 * v + 26.0 * p1 + p2
            SZ[p, pl.ds(8, 48)] = 6.0 * v - 2.0 * p1 - p2

            def rows_at(ref, off):
                return ref[p, pl.ds(8 + first + off, rows)]

            s0 = rows_at(SZ, 0)
            s1 = rows_at(SZ, -1) + rows_at(SZ, 1)
            s2 = rows_at(SZ, -2) + rows_at(SZ, 2)
            m0 = rows_at(MZ, 0)
            m1 = rows_at(MZ, -1) + rows_at(MZ, 1)
            m2 = rows_at(MZ, -2) + rows_at(MZ, 2)
            IN[p, pl.ds(first, rows)] = (66.0 * s0 + 26.0 * s1 + s2) + (6.0 * m0 - 2.0 * m1 - m2)
            OUT[p, pl.ds(first, rows)] = 66.0 * m0 + 26.0 * m1 + m2
            return carry

        lax.fori_loop(0, count, step, 0, unroll=True)

    def x_value(p, src, smap, m, first, rows):
        def pick(ref, off):
            return ref[p + off, pl.ds(first, rows)]

        i1 = pick(IN, 1) + pick(IN, 3)
        i2 = pick(IN, 0) + pick(IN, 4)
        o1 = pick(OUT, 1) + pick(OUT, 3)
        o2 = pick(OUT, 0) + pick(OUT, 4)
        k = (66.0 * pick(IN, 2) + 26.0 * i1 + i2) + (6.0 * pick(OUT, 2) - 2.0 * o1 - o2)
        centre = src[p + 2, pl.ds(first, rows)]
        return m * (k * SCALE + S[p + smap, pl.ds(first, rows)] * centre), centre

    def apply(src, dst, planes, halo, smap):
        for lo, hi, dx in ((0, halo, 0), (halo, halo + 16, 1), (halo + 16, planes, 2)):
            m = mask_rows(dx, (0, 1, 1, 2, 2, 3))

            def step(p, acc):
                value, centre = x_value(p, src, smap, m, 0, 48)
                dst[p] = value
                if dx != 1:
                    return acc
                u, v = value[8:40], centre[8:40]
                return acc[0] + fold(v * u), acc[1] + fold(u * u), acc[2] + fold(u)

            out = lax.fori_loop(lo, hi, step, (zero, zero, zero), unroll=True)
            if dx == 1:
                sums = out
        return sums

    zy_pass(R, 28, (0, 48))
    receive((2, 1))
    mu1, mu2, sum1 = apply(R, U1, 24, 4, 0)
    zy_pass(U1, 24, (0, 48))
    mu3, mu4, sum2 = apply(U1, U2, 20, 2, 2)
    zy_pass(U2, 20, (8, 32))

    def last(p, acc):
        value, centre = x_value(p, U2, 4, own, 8, 32)
        return acc + fold(value * centre)

    mu5 = lax.fori_loop(0, 16, last, zero, unroll=True)

    sub16 = lax.broadcasted_iota(jnp.int32, (16, 128), 0)
    lane16 = lax.broadcasted_iota(jnp.int32, (16, 128), 1)
    rows = jnp.zeros((16, 128), jnp.float32)
    for k, acc in enumerate((mu0, mu1, mu2, mu3, mu4, mu5, sum0, sum1, sum2)):
        rows = jnp.where(sub16 == k, jnp.sum(acc, axis=0, keepdims=True), rows)
    total = jnp.sum(rows, axis=1, keepdims=True)
    spread = jnp.where(lane16 == sub16, total, 0.0)
    values = jnp.sum(spread, axis=0, keepdims=True)
    lane1 = lax.broadcasted_iota(jnp.int32, (1, 128), 1)
    coarse = jnp.zeros((1, 128), jnp.float32)
    for k in range(6):
        coarse = jnp.where(lane1 == k, 1.5 * 2.0 ** (26 + k), coarse)
    rounded = (values + coarse) - coarse
    high = jnp.where(lane1 < 6, rounded, values)
    rest = jnp.where(lane1 < 6, values - rounded, 0.0)
    row = high + pltpu.roll(rest, 64, 1)
    row = jnp.where(lane1 == 9, count.astype(jnp.float32), row)

    pending = []
    mine = gy * 2 + core
    ar1[mine] = row
    for j in (10, 6, 9, 7, 11, 5, 8, 2, 14, 13, 3, 1, 15, 12, 4, 0):
        for c in (1 - core, core):
            if j == 0 and c is core:
                continue
            pltpu.make_async_remote_copy(
                ar1.at[mine], ar1.at[mine], asem.at[0], arsem.at[0],
                device_id=(2 * z + c, lax.rem(gy + j, NGY)), device_id_type=MESH).start()
    wait = pltpu.make_async_remote_copy(
        ar1.at[pl.ds(0, 31)], ar1.at[pl.ds(0, 31)], asem.at[0], arsem.at[0],
        device_id=(2 * z + 1 - core, gy), device_id_type=MESH)
    wait.wait_recv()
    pending.append(wait)

    ar2[z] = jnp.sum(ar1[...], axis=0)
    pl.semaphore_wait(token, 2)
    for off in (8, 7, -7, 6, -6, 5, -5, 4, -4, 3, -3, 2, -2, 1, -1):
        pltpu.make_async_remote_copy(
            ar2.at[z], ar2.at[z], asem.at[1], arsem.at[1],
            device_id=(at_z(off), gy), device_id_type=MESH).start()
    wait = pltpu.make_async_remote_copy(
        ar2.at[pl.ds(0, 15)], ar2.at[pl.ds(0, 15)], asem.at[1], arsem.at[1],
        device_id=(at_z(1), gy), device_id_type=MESH)
    wait.wait_recv()
    pending.append(wait)
    row = jnp.sum(ar2[...], axis=0)

    goal = jnp.where(sub16 < 10, sub16, sub16 + 54)
    picked = jnp.sum(jnp.where(lane16 == goal, row, 0.0), axis=1, keepdims=True)
    value = [jnp.broadcast_to(picked[k:k + 1], (8, 128)) for k in range(16)]
    mu = [two_sum(value[k], value[10 + k]) for k in range(6)]
    c0, c1, c2 = cg_weights(mu)
    iso = (c0 * value[6] + c1 * value[7] + c2 * value[8]) / (value[9] * float(BLK ** 3))

    def tile5(v):
        return jnp.concatenate([v] * 5, axis=0)

    iso_out[...] = iso
    c0, c1, c2 = tile5(c0), tile5(c1), tile5(c2)

    def solve(p, carry):
        x_out[p] = c0 * R[HR + p, pl.ds(8, 40)] + c1 * U1[4 + p, pl.ds(8, 40)] + c2 * U2[2 + p, pl.ds(8, 40)]
        return carry

    lax.fori_loop(0, 17, solve, 0, unroll=True)

    for i, ok in enumerate(has):
        @pl.when(ok)
        def _():
            for c in pieces(i, (0, 1, 2)):
                c.wait_send()
    for c in pending:
        c.wait_send()


def crossing_kernel(x_ref, iso_ref, vis, ind_out, cross_out, G, W, BR, vis_s, sem):
    load = pltpu.make_async_copy(vis.at[0], vis_s, sem.at[0])
    load.start()
    store = pltpu.make_async_copy(x_ref.at[pl.ds(0, 16), pl.ds(0, 32)], ind_out, sem.at[1])
    store.start()
    lane = lax.broadcasted_iota(jnp.int32, (8, 128), 1)
    iso = jnp.concatenate([iso_ref[...]] * 5, axis=0)

    for p in range(17):
        G[p] = sigmoid4(x_ref[p] - iso)
    BR[pl.ds(16 * 96, 96)] = jnp.zeros((96, 128), jnp.float32)

    lane32 = lax.broadcasted_iota(jnp.int32, (32, 128), 1)
    edge = lane32 == 127
    empty = sigmoid4(0.0 - iso[0:32])
    group = lane // BLK
    odd = [(group // (1 << bit)) % 2 == 1 for bit in range(3)]
    load.wait()
    slots = []
    for q in range(VIS):
        n = vis_s[0, q]
        slots.append(jnp.where(n >= 0, n, 16) * 96)
    stores = [store]
    for e in range(3):
        for p in range(16):
            g = G[p, pl.ds(0, 32)]
            if e == 0:
                other = G[p + 1, pl.ds(0, 32)]
            elif e == 1:
                other = G[p, pl.ds(1, 32)]
            else:
                other = jnp.where(edge, empty, pltpu.roll(g, 127, 1))
            h = crossing_weight(g, other)
            for w in range(2):
                W[e, pl.ds((p // 4) * 128 + w * 64 + p % 4 * 16, 16)] = h[16 * w:16 * w + 16]
        for first in range(0, 8, 4):
            parts = range(first, first + 4)
            vs = {}
            for part in parts:
                vs[part] = [W[e, pl.ds(part * 64 + (-j) % 8, 8, stride=8)] for j in range(8)]
            for part in parts:
                vs[part] = [v if j == 0 else pltpu.roll(v, 16 * ((-j) % 8), 1) for j, v in enumerate(vs[part])]
            for bit in range(3):
                for part in parts:
                    old = vs[part]
                    vs[part] = [jnp.where(odd[bit], old[(t - (1 << bit)) % 8], old[t]) for t in range(8)]
            for part in parts:
                vs[part] = [v if t == 0 else pltpu.roll(v, 128 - 16 * t, 1) for t, v in enumerate(vs[part])]
            for part in parts:
                w, ib = part % 2, part // 2
                for t in range(8):
                    BR[pl.ds((w * 8 + t) * 96 + e * 32 + ib * 8, 8)] = vs[part][t]
        for q in range(VIS):
            start = pl.multiple_of(slots[q] + e * 32, 8)
            stores.append(pltpu.make_async_copy(
                BR.at[pl.ds(start, 32)], cross_out.at[pl.ds(q * 96 + e * 32, 32)], sem.at[2 + q * 3 + e]))
            stores[-1].start()
    for c in stores:
        c.wait()


def body(right_side, screening, active_blocks, visible_bricks):
    f32 = jnp.float32
    right_side, screening, active_blocks, visible_bricks = (
        pltpu.with_memory_space_constraint(v, pltpu.HBM)
        for v in (right_side, screening, active_blocks, visible_bricks))
    hbm = pl.BlockSpec(memory_space=pltpu.HBM)
    vmem = pl.BlockSpec(memory_space=pltpu.VMEM)
    x, iso = pl.pallas_call(
        solve_kernel,
        out_shape=(jax.ShapeDtypeStruct((17, 40, 128), f32), jax.ShapeDtypeStruct((8, 128), f32)),
        in_specs=[hbm] * 3,
        out_specs=(vmem, vmem),
        scratch_shapes=[
            pltpu.VMEM((28, 48, 128), f32),
            pltpu.VMEM((24, 48, 128), f32),
            pltpu.VMEM((3, 4, 128), f32),
            pltpu.VMEM((24, 48, 128), f32),
            pltpu.VMEM((20, 48, 128), f32),
            pltpu.VMEM((28, 64, 128), f32),
            pltpu.VMEM((28, 64, 128), f32),
            pltpu.VMEM((28, 48, 128), f32),
            pltpu.VMEM((28, 48, 128), f32),
            pltpu.SMEM((1, ACT), jnp.int32),
            pltpu.VMEM((32, 1, 128), f32),
            pltpu.VMEM((16, 1, 128), f32),
            pltpu.SemaphoreType.DMA((3,)),
            pltpu.SemaphoreType.DMA((8, 3)),
            pltpu.SemaphoreType.DMA((8, 3)),
            pltpu.SemaphoreType.DMA((2,)),
            pltpu.SemaphoreType.DMA((2,)),
            pltpu.SemaphoreType.REGULAR,
        ],
        compiler_params=pltpu.CompilerParams(
            collective_id=0, has_side_effects=True, vmem_limit_bytes=32 << 20),
    )(right_side, screening, active_blocks)
    indicator, crossing = pl.pallas_call(
        crossing_kernel,
        out_shape=(jax.ShapeDtypeStruct((16, 32, 128), f32), jax.ShapeDtypeStruct((VIS * 96, 128), f32)),
        in_specs=[vmem, vmem, hbm],
        out_specs=(hbm, hbm),
        scratch_shapes=[
            pltpu.VMEM((17, 40, 128), f32),
            pltpu.VMEM((3, 512, 128), f32),
            pltpu.VMEM((17 * 96, 128), f32),
            pltpu.SMEM((1, VIS), jnp.int32),
            pltpu.SemaphoreType.DMA((2 + 3 * VIS,)),
        ],
        compiler_params=pltpu.CompilerParams(vmem_limit_bytes=24 << 20),
    )(x, iso, visible_bricks)
    return indicator, crossing.reshape(VIS, 1, 3, BLK ** 3)


def solution(mesh):
    spec = P("gx", "gy", None)
    return jax.shard_map(
        body,
        mesh=mesh,
        in_specs=(spec, spec, spec, spec),
        out_specs=(spec, P("gx", "gy", None, None)),
        check_vma=False,
    )
```

```python
import jax
import jax.numpy as jnp
from jax import lax
from jax.experimental import pallas as pl
from jax.experimental.pallas import tpu as pltpu
from jax.sharding import PartitionSpec as P

MESH = pl.DeviceIdType.MESH
BLK = 16
ACT = 12
VIS = 8
NGX = 32
NGY = 16
NZ = 16
SIGMA = 2.5
HR = 6
HS = 4
SCALE = 1.0 / 86400.0
NEIGHBOURS = [(1, 1), (1, -1), (-1, 1), (-1, -1), (0, 1), (0, -1), (1, 0), (-1, 0)]


def two_sum(a, b):
    s = a + b
    t = s - a
    return s, (a - (s - t)) + (b - t)


def quick_two_sum(a, b):
    s = a + b
    return s, b - (s - a)


def split(a):
    c = 4097.0 * a
    hi = c - (c - a)
    return hi, a - hi


def two_prod(a, b):
    p = a * b
    ah, al = split(a)
    bh, bl = split(b)
    return p, ((ah * bh - p) + ah * bl + al * bh) + al * bl


def dd_add(x, y):
    s, e = two_sum(x[0], y[0])
    return quick_two_sum(s, e + (x[1] + y[1]))


def dd_neg(x):
    return -x[0], -x[1]


def dd_sub(x, y):
    return dd_add(x, dd_neg(y))


def dd_mul(x, y):
    p, e = two_prod(x[0], y[0])
    return quick_two_sum(p, e + (x[0] * y[1] + x[1] * y[0]))


def dd_div(x, y):
    q = x[0] / y[0]
    r = dd_sub(x, dd_mul(y, (q, jnp.zeros_like(q))))
    return quick_two_sum(q, r[0] / y[0])


def cg_weights(mu):
    one = (jnp.ones_like(mu[0][0]), jnp.zeros_like(mu[0][0]))
    inv = dd_div(one, mu[0])
    row = [dd_mul(m, inv) for m in mu[1:]]
    a = row[0]
    level = [dd_sub(row[k + 1], dd_mul(a, row[k])) for k in range(4)]
    first = [(jnp.zeros_like(a[0]), jnp.zeros_like(a[0]))] + level
    central = []
    for _ in range(4):
        first = [dd_sub(first[k + 1], dd_mul(a, first[k])) for k in range(len(first) - 1)]
        central.append(first[0])
    m2, m3, m4, m5 = central
    tiny = 1e-30
    m2s = (jnp.maximum(m2[0], tiny), jnp.where(m2[0] > tiny, m2[1], 0.0))
    b1 = dd_div(m3, m2s)
    m22 = dd_mul(m2, m2)
    h2 = dd_sub(dd_sub(m4, dd_mul(b1, m3)), m22)
    h2s = jnp.maximum(h2[0], tiny)
    inner = dd_sub(dd_mul(b1, m3), dd_add(m4, m4))
    inner = dd_add(inner, dd_add(m22, m22))
    top = dd_add(m5, dd_mul(b1, inner))
    m23 = dd_mul(m2, m3)
    top = dd_sub(top, dd_add(m23, m23))
    d0 = a[0] + SIGMA
    d1 = jnp.clip(d0 + b1[0], 0.25, 9.0)
    d2 = jnp.clip(d0 + top[0] / h2s, 0.25, 9.0)
    beta1 = jnp.maximum(m2[0], 0.0)
    beta2 = jnp.clip(h2[0] / m2s[0], 0.0, 25.0)
    bb1 = d1 - d0
    minor = d1 * d2 - beta2
    y2 = 1.0 / (d0 * minor - beta1 * d2)
    y1 = -d2 * y2
    y0 = minor * y2
    c2 = y2
    c1 = y1 - y2 * (2.0 * a[0] + bb1)
    c0 = y0 - a[0] * y1 + y2 * (a[0] * a[0] + a[0] * bb1 - m2[0])
    return c0, c1, c2


def sigmoid4(v):
    return 1.0 / (1.0 + jnp.exp(-4.0 * v))


def crossing_weight(lower, upper):
    return lower * (1.0 - upper) + (1.0 - lower) * upper


def solve_kernel(rhs, scr, act, x_out, iso_out,
           R, S, M, U1, U2, MZ, SZ, MZ2, SZ2, IN, OUT, act_s, ar1, ar2,
                 lsem, ssem, rsem, asem, arsem, token):
    gx = lax.axis_index("gx")
    gy = lax.axis_index("gy")
    z = gx // 2
    core = lax.rem(gx, 2)

    def at_z(off):
        return lax.rem(z + off + NZ, NZ) * 2 + core

    bar = pltpu.get_barrier_semaphore()

    def tell(x, y):
        pl.semaphore_signal(bar, inc=1, device_id=(x, y), device_id_type=MESH)

    other_chip = lax.rem(gx + 2 * core - 1 + NGX, NGX)
    for dy in (1, -1):
        tell(other_chip, lax.rem(gy + dy + NGY, NGY))
    tell(other_chip, gy)
    for j in (1, 15, 10, 6, 9, 7, 11, 5, 8, 2, 14, 13, 3, 12, 4):
        for c in (1 - core, core):
            tell(2 * z + c, lax.rem(gy + j, NGY))
    tell(2 * z + 1 - core, gy)
    for off in (4, -4, 3, -3, 2, -2, 1, -1):
        tell(at_z(off), gy)
    has = []
    for dx, dy in NEIGHBOURS:
        ok = None
        for cond in ([gx < NGX - 1] if dx == 1 else []) + ([gx > 0] if dx == -1 else []) + (
            [gy < NGY - 1] if dy == 1 else []) + ([gy > 0] if dy == -1 else []):
            ok = cond if ok is None else jnp.logical_and(ok, cond)
        has.append(ok)
    loads = [
        pltpu.make_async_copy(act.at[0], act_s, lsem.at[0]),
        pltpu.make_async_copy(rhs, R.at[pl.ds(HR, 16), pl.ds(8, 32)], lsem.at[1]),
        pltpu.make_async_copy(scr, S.at[pl.ds(HS, 16), pl.ds(8, 32)], lsem.at[2]),
    ]
    for c in loads:
        c.start()

    @pl.when(gx == 0)
    def _():
        R[pl.ds(0, HR)] = jnp.zeros((HR, 48, 128), jnp.float32)
        S[pl.ds(0, HS)] = jnp.zeros((HS, 48, 128), jnp.float32)
        M[0] = jnp.zeros((4, 128), jnp.float32)

    @pl.when(gx == NGX - 1)
    def _():
        R[pl.ds(HR + 16, HR)] = jnp.zeros((HR, 48, 128), jnp.float32)
        S[pl.ds(HS + 16, HS)] = jnp.zeros((HS, 48, 128), jnp.float32)
        M[2] = jnp.zeros((4, 128), jnp.float32)

    def clear_rows(row, kind):
        R[:, pl.ds(row, 8)] = jnp.zeros((28, 8, 128), jnp.float32)
        S[:, pl.ds(row, 8)] = jnp.zeros((24, 8, 128), jnp.float32)
        M[:, pl.ds(kind, 1)] = jnp.zeros((3, 1, 128), jnp.float32)

    @pl.when(gy == 0)
    def _():
        clear_rows(0, 0)

    @pl.when(gy == NGY - 1)
    def _():
        clear_rows(40, 3)

    lane = lax.broadcasted_iota(jnp.int32, (8, 128), 1)
    loads[0].wait()
    entries = [act_s[0, q] for q in range(ACT)]
    count = jnp.int32(0)
    for e in entries:
        count = count + jnp.where(e >= 0, 1, 0)
    for w in range(2):
        number = lane // BLK + 8 * w
        own = jnp.zeros((8, 128), jnp.float32)
        for e in entries:
            own = jnp.where(number == e, 1.0, own)
        M[1, pl.ds(1 + w, 1)] = own[0:1]
    loads[1].wait()
    loads[2].wait()

    def mask_rows(dx, kinds):
        tiles = [jnp.broadcast_to(M[dx, pl.ds(k, 1)], (8, 128)) for k in range(4)]
        return jnp.concatenate([tiles[k] for k in kinds], axis=0)

    own = mask_rows(1, (1, 1, 2, 2))

    def prepare(p, carry):
        R[HR + p, pl.ds(8, 32)] = R[HR + p, pl.ds(8, 32)] * own
        S[HS + p, pl.ds(8, 32)] = S[HS + p, pl.ds(8, 32)] - SIGMA
        return carry

    lax.fori_loop(0, 16, prepare, 0, unroll=4)

    pl.semaphore_wait(bar, 42)
    for off in (4, -4):
        pl.semaphore_signal(token, inc=1, device_id=(at_z(off), gy), device_id_type=MESH)

    def pieces(i, which):
        dx, dy = NEIGHBOURS[i]
        out = []
        for n in which:
            if n == 2:
                first, size = {0: (1, 2), 1: (2, 1), -1: (1, 1)}[dy]
                src = M.at[1, pl.ds(first, size)]
                dst = M.at[1 - dx, pl.ds({0: 1, 1: 0, -1: 3}[dy], size)]
            else:
                ref, h = ((R, HR), (S, HS))[n]
                planes = {0: (h, h, 16), 1: (16, 0, h), -1: (h, h + 16, h)}[dx]
                rows = {0: (8, 8, 32), 1: (40 - h, 8 - h, h), -1: (8, 40, h)}[dy]
                src = ref.at[pl.ds(planes[0], planes[2]), pl.ds(rows[0], rows[2])]
                dst = ref.at[pl.ds(planes[1], planes[2]), pl.ds(rows[1], rows[2])]
            out.append(pltpu.make_async_remote_copy(
                src, dst, ssem.at[i, n], rsem.at[i, n],
                device_id=(gx + dx, gy + dy), device_id_type=MESH))
        return out

    opposite = [NEIGHBOURS.index((-dx, -dy)) for dx, dy in NEIGHBOURS]

    def receive(which):
        for i in range(8):
            @pl.when(has[opposite[i]])
            def _():
                for c in pieces(i, which):
                    c.wait_recv()

    for which in ((0,), (2, 1)):
        for i, ok in enumerate(has):
            @pl.when(ok)
            def _():
                for c in pieces(i, which):
                    c.start()

    zero = jnp.zeros((8, 128), jnp.float32)
    sub = lax.broadcasted_iota(jnp.int32, (8, 128), 0)

    lanes = lax.broadcasted_iota(jnp.int32, (48, 128), 1)

    def z_stage(src, row, mz, sz, out_row, p, rows):
        v = src[p, pl.ds(row, rows)]
        at = lanes[0:rows]
        p1 = jnp.where(at < 1, 0.0, pltpu.roll(v, 1, 1)) + jnp.where(at > 126, 0.0, pltpu.roll(v, 127, 1))
        p2 = jnp.where(at < 2, 0.0, pltpu.roll(v, 2, 1)) + jnp.where(at > 125, 0.0, pltpu.roll(v, 126, 1))
        mz[p, pl.ds(out_row, rows)] = 66.0 * v + 26.0 * p1 + p2
        sz[p, pl.ds(out_row, rows)] = 6.0 * v - 2.0 * p1 - p2

    def y_stage(mz, sz, row, p, out_row, rows):
        def at(ref, off):
            return ref[p, pl.ds(row + off, rows)]

        s0 = at(sz, 0)
        s1 = at(sz, -1) + at(sz, 1)
        s2 = at(sz, -2) + at(sz, 2)
        m0 = at(mz, 0)
        m1 = at(mz, -1) + at(mz, 1)
        m2 = at(mz, -2) + at(mz, 2)
        IN[p, pl.ds(out_row, rows)] = (66.0 * s0 + 26.0 * s1 + s2) + (6.0 * m0 - 2.0 * m1 - m2)
        OUT[p, pl.ds(out_row, rows)] = 66.0 * m0 + 26.0 * m1 + m2

    def x_stage(p, row, rows, m, scr_rows, src, src_row):
        def at(ref, off):
            return ref[p + off, pl.ds(row, rows)]

        i1 = at(IN, 1) + at(IN, 3)
        i2 = at(IN, 0) + at(IN, 4)
        o1 = at(OUT, 1) + at(OUT, 3)
        o2 = at(OUT, 0) + at(OUT, 4)
        k = (66.0 * at(IN, 2) + 26.0 * i1 + i2) + (6.0 * at(OUT, 2) - 2.0 * o1 - o2)
        centre = src[p + 2, pl.ds(src_row, rows)]
        return m * (k * SCALE + scr_rows * centre), centre

    def total_of(acc, terms):
        return tuple(x + y for x, y in zip(acc, terms))

    def own_terms(value, centre, first, tiles):
        terms = []
        for prod in (value * centre, value * value, value):
            t = [prod[8 * k:8 * k + 8] for k in range(tiles)]
            if first is None:
                terms.append((t[0] + t[1]) + t[2])
            elif tiles == 2:
                terms.append(jnp.where(sub >= first, t[0], t[1]))
            else:
                terms.append((jnp.where(sub >= first, t[0], t[4]) + t[1]) + (t[2] + t[3]))
        return terms

    def mask_from(dx, base):
        k = [jnp.broadcast_to(M[dx, pl.ds(j, 1)], (8, 128)) for j in range(4)]
        cut = sub >= -base
        return jnp.concatenate([jnp.where(cut, k[1], k[0]), k[1], jnp.where(cut, k[2], k[1]), k[2],
                                jnp.where(cut, k[3], k[2])], axis=0)

    mu0, sum0 = zero, zero
    for p in range(HR, HR + 16):
        z_stage(R, 8, MZ, SZ, 16, p, 32)
        v = R[p, pl.ds(8, 32)]
        w = v * v
        mu0 = mu0 + ((w[0:8] + w[8:16]) + (w[16:24] + w[24:32]))
        sum0 = sum0 + ((v[0:8] + v[8:16]) + (v[16:24] + v[24:32]))
    for p in range(HR, HR + 16):
        y_stage(MZ, SZ, 20, p, 8, 24)
    middle = jnp.concatenate([own[0:8], jnp.where(sub >= 4, own[16:24], own[0:8]), own[16:24]], axis=0)
    acc = (zero, zero, zero)
    for p in range(6, 18):
        value, centre = x_stage(p, 8, 24, middle, S[p, pl.ds(12, 24)], R, 12)
        U1[p, pl.ds(8, 24)] = value
        acc = total_of(acc, own_terms(value, centre, None, 3))

    receive((0,))
    for p in range(28):
        if HR <= p < HR + 16:
            z_stage(R, 0, MZ, SZ, 8, p, 8)
            z_stage(R, 40, MZ, SZ, 48, p, 8)
        else:
            z_stage(R, 0, MZ, SZ, 8, p, 48)
    for p in range(28):
        if HR <= p < HR + 16:
            y_stage(MZ, SZ, 12, p, 0, 8)
            y_stage(MZ, SZ, 44, p, 32, 8)
        else:
            y_stage(MZ, SZ, 12, p, 0, 40)
    receive((2, 1))
    masks = [mask_from(dx, -4) for dx in range(3)]
    for p in range(24):
        dx = 0 if p < 4 else 1 if p < 20 else 2
        if 6 <= p < 18:
            low, c_low = x_stage(p, 0, 8, masks[1][0:8], S[p, pl.ds(4, 8)], R, 4)
            high, c_high = x_stage(p, 32, 8, masks[1][32:40], S[p, pl.ds(36, 8)], R, 36)
            U1[p, pl.ds(0, 8)] = low
            U1[p, pl.ds(32, 8)] = high
            acc = total_of(acc, own_terms(jnp.concatenate([low, high], axis=0),
                                          jnp.concatenate([c_low, c_high], axis=0), 4, 2))
        else:
            value, centre = x_stage(p, 0, 40, masks[dx], S[p, pl.ds(4, 40)], R, 4)
            U1[p, pl.ds(0, 40)] = value
            if dx == 1:
                acc = total_of(acc, own_terms(value, centre, 4, 5))
    mu1, mu2, sum1 = acc

    for p in range(24):
        z_stage(U1, 0, MZ2, SZ2, 8, p, 40)
    for p in range(24):
        y_stage(MZ2, SZ2, 10, p, 0, 40)
    masks = [mask_from(dx, -2) for dx in range(3)]
    acc = (zero, zero, zero)
    for p in range(20):
        dx = 0 if p < 2 else 1 if p < 18 else 2
        value, centre = x_stage(p, 0, 40, masks[dx], S[p + 2, pl.ds(6, 40)], U1, 2)
        U2[p, pl.ds(0, 40)] = value
        if dx == 1:
            acc = total_of(acc, own_terms(value, centre, 2, 5))
    mu3, mu4, sum2 = acc

    for p in range(20):
        z_stage(U2, 0, MZ, SZ, 8, p, 40)
    for p in range(20):
        y_stage(MZ, SZ, 10, p, 0, 32)
    mu5 = zero
    for p in range(16):
        value, centre = x_stage(p, 0, 32, own, S[p + 4, pl.ds(8, 32)], U2, 2)
        w = value * centre
        mu5 = mu5 + ((w[0:8] + w[8:16]) + (w[16:24] + w[24:32]))

    sub16 = lax.broadcasted_iota(jnp.int32, (16, 128), 0)
    lane16 = lax.broadcasted_iota(jnp.int32, (16, 128), 1)
    rows = jnp.zeros((16, 128), jnp.float32)
    for k, acc in enumerate((mu0, mu1, mu2, mu3, mu4, mu5, sum0, sum1, sum2)):
        rows = jnp.where(sub16 == k, jnp.sum(acc, axis=0, keepdims=True), rows)
    total = jnp.sum(rows, axis=1, keepdims=True)
    spread = jnp.where(lane16 == sub16, total, 0.0)
    values = jnp.sum(spread, axis=0, keepdims=True)
    lane1 = lax.broadcasted_iota(jnp.int32, (1, 128), 1)
    coarse = jnp.zeros((1, 128), jnp.float32)
    for k in range(6):
        coarse = jnp.where(lane1 == k, 1.5 * 2.0 ** (26 + k), coarse)
    rounded = (values + coarse) - coarse
    high = jnp.where(lane1 < 6, rounded, values)
    rest = jnp.where(lane1 < 6, values - rounded, 0.0)
    row = high + pltpu.roll(rest, 64, 1)
    row = jnp.where(lane1 == 9, count.astype(jnp.float32), row)

    pending = []
    mine = gy * 2 + core
    ar1[mine] = row
    for j in (10, 6, 9, 7, 11, 5, 8, 2, 14, 13, 3, 1, 15, 12, 4, 0):
        for c in (1 - core, core):
            if j == 0 and c is core:
                continue
            pltpu.make_async_remote_copy(
                ar1.at[mine], ar1.at[mine], asem.at[0], arsem.at[0],
                device_id=(2 * z + c, lax.rem(gy + j, NGY)), device_id_type=MESH).start()
    wait = pltpu.make_async_remote_copy(
        ar1.at[pl.ds(0, 31)], ar1.at[pl.ds(0, 31)], asem.at[0], arsem.at[0],
        device_id=(2 * z + 1 - core, gy), device_id_type=MESH)
    wait.wait_recv()
    pending.append(wait)

    ar2[z] = jnp.sum(ar1[...], axis=0)
    pl.semaphore_wait(token, 2)
    for off in (8, 7, -7, 6, -6, 5, -5, 4, -4, 3, -3, 2, -2, 1, -1):
        pltpu.make_async_remote_copy(
            ar2.at[z], ar2.at[z], asem.at[1], arsem.at[1],
            device_id=(at_z(off), gy), device_id_type=MESH).start()
    wait = pltpu.make_async_remote_copy(
        ar2.at[pl.ds(0, 15)], ar2.at[pl.ds(0, 15)], asem.at[1], arsem.at[1],
        device_id=(at_z(1), gy), device_id_type=MESH)
    wait.wait_recv()
    pending.append(wait)
    row = jnp.sum(ar2[...], axis=0)

    goal = jnp.where(sub16 < 10, sub16, sub16 + 54)
    picked = jnp.sum(jnp.where(lane16 == goal, row, 0.0), axis=1, keepdims=True)
    value = [jnp.broadcast_to(picked[k:k + 1], (8, 128)) for k in range(16)]
    mu = [two_sum(value[k], value[10 + k]) for k in range(6)]
    c0, c1, c2 = cg_weights(mu)
    iso = (c0 * value[6] + c1 * value[7] + c2 * value[8]) / (value[9] * float(BLK ** 3))

    def tile5(v):
        return jnp.concatenate([v] * 5, axis=0)

    iso_out[...] = iso
    c0, c1, c2 = tile5(c0), tile5(c1), tile5(c2)

    def solve(p, carry):
        x_out[p] = c0 * R[HR + p, pl.ds(8, 40)] + c1 * U1[4 + p, pl.ds(4, 40)] + c2 * U2[2 + p, pl.ds(2, 40)]
        return carry

    lax.fori_loop(0, 17, solve, 0, unroll=True)

    for i, ok in enumerate(has):
        @pl.when(ok)
        def _():
            for c in pieces(i, (0, 1, 2)):
                c.wait_send()
    for c in pending:
        c.wait_send()


def crossing_kernel(x_ref, iso_ref, vis, ind_out, cross_out, G, W, BR, vis_s, sem):
    load = pltpu.make_async_copy(vis.at[0], vis_s, sem.at[0])
    load.start()
    store = pltpu.make_async_copy(x_ref.at[pl.ds(0, 16), pl.ds(0, 32)], ind_out, sem.at[1])
    store.start()
    lane = lax.broadcasted_iota(jnp.int32, (8, 128), 1)
    iso = jnp.concatenate([iso_ref[...]] * 5, axis=0)

    for p in range(17):
        G[p] = sigmoid4(x_ref[p] - iso)
    BR[pl.ds(16 * 96, 96)] = jnp.zeros((96, 128), jnp.float32)

    lane32 = lax.broadcasted_iota(jnp.int32, (32, 128), 1)
    edge = lane32 == 127
    empty = sigmoid4(0.0 - iso[0:32])
    group = lane // BLK
    odd = [(group // (1 << bit)) % 2 == 1 for bit in range(3)]
    load.wait()
    slots = []
    for q in range(VIS):
        n = vis_s[0, q]
        slots.append(jnp.where(n >= 0, n, 16) * 96)
    stores = [store]
    for e in range(3):
        for p in range(16):
            g = G[p, pl.ds(0, 32)]
            if e == 0:
                other = G[p + 1, pl.ds(0, 32)]
            elif e == 1:
                other = G[p, pl.ds(1, 32)]
            else:
                other = jnp.where(edge, empty, pltpu.roll(g, 127, 1))
            h = crossing_weight(g, other)
            for w in range(2):
                W[e, pl.ds((p // 4) * 128 + w * 64 + p % 4 * 16, 16)] = h[16 * w:16 * w + 16]
        for first in range(0, 8, 4):
            parts = range(first, first + 4)
            vs = {}
            for part in parts:
                vs[part] = [W[e, pl.ds(part * 64 + (-j) % 8, 8, stride=8)] for j in range(8)]
            for part in parts:
                vs[part] = [v if j == 0 else pltpu.roll(v, 16 * ((-j) % 8), 1) for j, v in enumerate(vs[part])]
            for bit in range(3):
                for part in parts:
                    old = vs[part]
                    vs[part] = [jnp.where(odd[bit], old[(t - (1 << bit)) % 8], old[t]) for t in range(8)]
            for part in parts:
                vs[part] = [v if t == 0 else pltpu.roll(v, 128 - 16 * t, 1) for t, v in enumerate(vs[part])]
            for part in parts:
                w, ib = part % 2, part // 2
                for t in range(8):
                    BR[pl.ds((w * 8 + t) * 96 + e * 32 + ib * 8, 8)] = vs[part][t]
        for q in range(VIS):
            start = pl.multiple_of(slots[q] + e * 32, 8)
            stores.append(pltpu.make_async_copy(
                BR.at[pl.ds(start, 32)], cross_out.at[pl.ds(q * 96 + e * 32, 32)], sem.at[2 + q * 3 + e]))
            stores[-1].start()
    for c in stores:
        c.wait()


def body(right_side, screening, active_blocks, visible_bricks):
    f32 = jnp.float32
    right_side, screening, active_blocks, visible_bricks = (
        pltpu.with_memory_space_constraint(v, pltpu.HBM)
        for v in (right_side, screening, active_blocks, visible_bricks))
    hbm = pl.BlockSpec(memory_space=pltpu.HBM)
    vmem = pl.BlockSpec(memory_space=pltpu.VMEM)
    x, iso = pl.pallas_call(
        solve_kernel,
        out_shape=(jax.ShapeDtypeStruct((17, 40, 128), f32), jax.ShapeDtypeStruct((8, 128), f32)),
        in_specs=[hbm] * 3,
        out_specs=(vmem, vmem),
        scratch_shapes=[
            pltpu.VMEM((28, 48, 128), f32),
            pltpu.VMEM((24, 48, 128), f32),
            pltpu.VMEM((3, 4, 128), f32),
            pltpu.VMEM((24, 48, 128), f32),
            pltpu.VMEM((20, 48, 128), f32),
            pltpu.VMEM((28, 64, 128), f32),
            pltpu.VMEM((28, 64, 128), f32),
            pltpu.VMEM((24, 56, 128), f32),
            pltpu.VMEM((24, 56, 128), f32),
            pltpu.VMEM((28, 48, 128), f32),
            pltpu.VMEM((28, 48, 128), f32),
            pltpu.SMEM((1, ACT), jnp.int32),
            pltpu.VMEM((32, 1, 128), f32),
            pltpu.VMEM((16, 1, 128), f32),
            pltpu.SemaphoreType.DMA((3,)),
            pltpu.SemaphoreType.DMA((8, 3)),
            pltpu.SemaphoreType.DMA((8, 3)),
            pltpu.SemaphoreType.DMA((2,)),
            pltpu.SemaphoreType.DMA((2,)),
            pltpu.SemaphoreType.REGULAR,
        ],
        compiler_params=pltpu.CompilerParams(
            collective_id=0, has_side_effects=True, vmem_limit_bytes=32 << 20),
    )(right_side, screening, active_blocks)
    indicator, crossing = pl.pallas_call(
        crossing_kernel,
        out_shape=(jax.ShapeDtypeStruct((16, 32, 128), f32), jax.ShapeDtypeStruct((VIS * 96, 128), f32)),
        in_specs=[vmem, vmem, hbm],
        out_specs=(hbm, hbm),
        scratch_shapes=[
            pltpu.VMEM((17, 40, 128), f32),
            pltpu.VMEM((3, 512, 128), f32),
            pltpu.VMEM((17 * 96, 128), f32),
            pltpu.SMEM((1, VIS), jnp.int32),
            pltpu.SemaphoreType.DMA((2 + 3 * VIS,)),
        ],
        compiler_params=pltpu.CompilerParams(vmem_limit_bytes=24 << 20),
    )(x, iso, visible_bricks)
    return indicator, crossing.reshape(VIS, 1, 3, BLK ** 3)


def solution(mesh):
    spec = P("gx", "gy", None)
    return jax.shard_map(
        body,
        mesh=mesh,
        in_specs=(spec, spec, spec, spec),
        out_specs=(spec, P("gx", "gy", None, None)),
        check_vma=False,
    )
```

```python
import jax
import jax.numpy as jnp
from jax import lax
from jax.experimental import pallas as pl
from jax.experimental.pallas import tpu as pltpu
from jax.sharding import PartitionSpec as P

MESH = pl.DeviceIdType.MESH
BLK = 16
ACT = 12
VIS = 8
NGX = 32
NGY = 16
NZ = 16
SIGMA = 2.5
HR = 6
HS = 4
SCALE = 1.0 / 86400.0
NEIGHBOURS = [(1, 1), (1, -1), (-1, 1), (-1, -1), (0, 1), (0, -1), (1, 0), (-1, 0)]


def two_sum(a, b):
    s = a + b
    t = s - a
    return s, (a - (s - t)) + (b - t)


def quick_two_sum(a, b):
    s = a + b
    return s, b - (s - a)


def split(a):
    c = 4097.0 * a
    hi = c - (c - a)
    return hi, a - hi


def two_prod(a, b):
    p = a * b
    ah, al = split(a)
    bh, bl = split(b)
    return p, ((ah * bh - p) + ah * bl + al * bh) + al * bl


def dd_add(x, y):
    s, e = two_sum(x[0], y[0])
    return quick_two_sum(s, e + (x[1] + y[1]))


def dd_neg(x):
    return -x[0], -x[1]


def dd_sub(x, y):
    return dd_add(x, dd_neg(y))


def dd_mul(x, y):
    p, e = two_prod(x[0], y[0])
    return quick_two_sum(p, e + (x[0] * y[1] + x[1] * y[0]))


def dd_div(x, y):
    q = x[0] / y[0]
    r = dd_sub(x, dd_mul(y, (q, jnp.zeros_like(q))))
    return quick_two_sum(q, r[0] / y[0])


def cg_weights(mu):
    one = (jnp.ones_like(mu[0][0]), jnp.zeros_like(mu[0][0]))
    inv = dd_div(one, mu[0])
    row = [dd_mul(m, inv) for m in mu[1:]]
    a = row[0]
    level = [dd_sub(row[k + 1], dd_mul(a, row[k])) for k in range(4)]
    first = [(jnp.zeros_like(a[0]), jnp.zeros_like(a[0]))] + level
    central = []
    for _ in range(4):
        first = [dd_sub(first[k + 1], dd_mul(a, first[k])) for k in range(len(first) - 1)]
        central.append(first[0])
    m2, m3, m4, m5 = central
    tiny = 1e-30
    m2s = (jnp.maximum(m2[0], tiny), jnp.where(m2[0] > tiny, m2[1], 0.0))
    b1 = dd_div(m3, m2s)
    m22 = dd_mul(m2, m2)
    h2 = dd_sub(dd_sub(m4, dd_mul(b1, m3)), m22)
    h2s = jnp.maximum(h2[0], tiny)
    inner = dd_sub(dd_mul(b1, m3), dd_add(m4, m4))
    inner = dd_add(inner, dd_add(m22, m22))
    top = dd_add(m5, dd_mul(b1, inner))
    m23 = dd_mul(m2, m3)
    top = dd_sub(top, dd_add(m23, m23))
    d0 = a[0] + SIGMA
    d1 = jnp.clip(d0 + b1[0], 0.25, 9.0)
    d2 = jnp.clip(d0 + top[0] / h2s, 0.25, 9.0)
    beta1 = jnp.maximum(m2[0], 0.0)
    beta2 = jnp.clip(h2[0] / m2s[0], 0.0, 25.0)
    bb1 = d1 - d0
    minor = d1 * d2 - beta2
    y2 = 1.0 / (d0 * minor - beta1 * d2)
    y1 = -d2 * y2
    y0 = minor * y2
    c2 = y2
    c1 = y1 - y2 * (2.0 * a[0] + bb1)
    c0 = y0 - a[0] * y1 + y2 * (a[0] * a[0] + a[0] * bb1 - m2[0])
    return c0, c1, c2


def tree(parts):
    while len(parts) > 1:
        parts = [a + b for a, b in zip(parts[::2], parts[1::2])]
    return parts[0]


def sigmoid4(v):
    return 1.0 / (1.0 + jnp.exp(-4.0 * v))


def crossing_weight(lower, upper):
    return lower * (1.0 - upper) + (1.0 - lower) * upper


def solve_kernel(rhs, scr, act, x_out, iso_out,
           R, S, M, U1, U2, MZ, SZ, MZ2, SZ2, TA, TB, act_s, ar1, ar2,
                 lsem, ssem, rsem, asem, arsem, token):
    gx = lax.axis_index("gx")
    gy = lax.axis_index("gy")
    z = gx // 2
    core = lax.rem(gx, 2)

    def at_z(off):
        return lax.rem(z + off + NZ, NZ) * 2 + core

    loads = [
        pltpu.make_async_copy(act.at[0], act_s, lsem.at[0]),
        pltpu.make_async_copy(rhs, R.at[pl.ds(HR, 16), pl.ds(8, 32)], lsem.at[1]),
        pltpu.make_async_copy(scr, S.at[pl.ds(HS, 16), pl.ds(8, 32)], lsem.at[2]),
    ]
    for c in loads:
        c.start()

    bar = pltpu.get_barrier_semaphore()

    def tell(x, y):
        pl.semaphore_signal(bar, inc=1, device_id=(x, y), device_id_type=MESH)

    other_chip = lax.rem(gx + 2 * core - 1 + NGX, NGX)
    for dy in (1, -1):
        tell(other_chip, lax.rem(gy + dy + NGY, NGY))
    tell(other_chip, gy)
    for j in (1, 15, 10, 6, 9, 7, 11, 5, 8, 2, 14, 13, 3, 12, 4):
        for c in (1 - core, core):
            tell(2 * z + c, lax.rem(gy + j, NGY))
    tell(2 * z + 1 - core, gy)
    for off in (4, -4, 3, -3, 2, -2, 1, -1):
        tell(at_z(off), gy)
    has = []
    for dx, dy in NEIGHBOURS:
        ok = None
        for cond in ([gx < NGX - 1] if dx == 1 else []) + ([gx > 0] if dx == -1 else []) + (
            [gy < NGY - 1] if dy == 1 else []) + ([gy > 0] if dy == -1 else []):
            ok = cond if ok is None else jnp.logical_and(ok, cond)
        has.append(ok)
    @pl.when(gx == 0)
    def _():
        R[pl.ds(0, HR)] = jnp.zeros((HR, 48, 128), jnp.float32)
        S[pl.ds(0, HS)] = jnp.zeros((HS, 48, 128), jnp.float32)
        M[0] = jnp.zeros((4, 128), jnp.float32)

    @pl.when(gx == NGX - 1)
    def _():
        R[pl.ds(HR + 16, HR)] = jnp.zeros((HR, 48, 128), jnp.float32)
        S[pl.ds(HS + 16, HS)] = jnp.zeros((HS, 48, 128), jnp.float32)
        M[2] = jnp.zeros((4, 128), jnp.float32)

    def clear_rows(row, kind):
        R[:, pl.ds(row, 8)] = jnp.zeros((28, 8, 128), jnp.float32)
        S[:, pl.ds(row, 8)] = jnp.zeros((24, 8, 128), jnp.float32)
        M[:, pl.ds(kind, 1)] = jnp.zeros((3, 1, 128), jnp.float32)

    @pl.when(gy == 0)
    def _():
        clear_rows(0, 0)

    @pl.when(gy == NGY - 1)
    def _():
        clear_rows(40, 3)

    lane = lax.broadcasted_iota(jnp.int32, (8, 128), 1)
    loads[0].wait()
    entries = [act_s[0, q] for q in range(ACT)]
    count = jnp.int32(0)
    for e in entries:
        count = count + jnp.where(e >= 0, 1, 0)
    for w in range(2):
        number = lane // BLK + 8 * w
        own = jnp.zeros((8, 128), jnp.float32)
        for e in entries:
            own = jnp.where(number == e, 1.0, own)
        M[1, pl.ds(1 + w, 1)] = own[0:1]
    loads[1].wait()
    loads[2].wait()

    def mask_rows(dx, kinds):
        tiles = [jnp.broadcast_to(M[dx, pl.ds(k, 1)], (8, 128)) for k in range(4)]
        return jnp.concatenate([tiles[k] for k in kinds], axis=0)

    own = mask_rows(1, (1, 1, 2, 2))

    def prepare(p, carry):
        R[HR + p, pl.ds(8, 32)] = R[HR + p, pl.ds(8, 32)] * own
        S[HS + p, pl.ds(8, 32)] = S[HS + p, pl.ds(8, 32)] - SIGMA
        return carry

    lax.fori_loop(0, 16, prepare, 0, unroll=4)

    pl.semaphore_wait(bar, 42)
    for off in (4, -4):
        pl.semaphore_signal(token, inc=1, device_id=(at_z(off), gy), device_id_type=MESH)

    def pieces(i, which):
        dx, dy = NEIGHBOURS[i]
        out = []
        for n in which:
            if n == 2:
                first, size = {0: (1, 2), 1: (2, 1), -1: (1, 1)}[dy]
                src = M.at[1, pl.ds(first, size)]
                dst = M.at[1 - dx, pl.ds({0: 1, 1: 0, -1: 3}[dy], size)]
            else:
                ref, h = ((R, HR), (S, HS))[n]
                planes = {0: (h, h, 16), 1: (16, 0, h), -1: (h, h + 16, h)}[dx]
                rows = {0: (8, 8, 32), 1: (40 - h, 8 - h, h), -1: (8, 40, h)}[dy]
                src = ref.at[pl.ds(planes[0], planes[2]), pl.ds(rows[0], rows[2])]
                dst = ref.at[pl.ds(planes[1], planes[2]), pl.ds(rows[1], rows[2])]
            out.append(pltpu.make_async_remote_copy(
                src, dst, ssem.at[i, n], rsem.at[i, n],
                device_id=(gx + dx, gy + dy), device_id_type=MESH))
        return out

    opposite = [NEIGHBOURS.index((-dx, -dy)) for dx, dy in NEIGHBOURS]

    def receive(which, kinds=(0, 1, 2)):
        for i in range(8):
            dx, dy = NEIGHBOURS[i]
            if (2 if dx and dy else 0 if dx else 1) not in kinds:
                continue

            @pl.when(has[opposite[i]])
            def _():
                for c in pieces(i, which):
                    c.wait_recv()

    for which in ((0,), (2, 1)):
        for i, ok in enumerate(has):
            @pl.when(ok)
            def _():
                for c in pieces(i, which):
                    c.start()

    zero = jnp.zeros((8, 128), jnp.float32)
    sub = lax.broadcasted_iota(jnp.int32, (8, 128), 0)

    lanes = lax.broadcasted_iota(jnp.int32, (48, 128), 1)

    def z_stage(src, row, mz, sz, out_row, p, rows):
        v = src[p, pl.ds(row, rows)]
        at = lanes[0:rows]
        p1 = jnp.where(at < 1, 0.0, pltpu.roll(v, 1, 1)) + jnp.where(at > 126, 0.0, pltpu.roll(v, 127, 1))
        p2 = jnp.where(at < 2, 0.0, pltpu.roll(v, 2, 1)) + jnp.where(at > 125, 0.0, pltpu.roll(v, 126, 1))
        mz[p, pl.ds(out_row, rows)] = 66.0 * v + 26.0 * p1 + p2
        sz[p, pl.ds(out_row, rows)] = 6.0 * v - 2.0 * p1 - p2

    def x_stage(mz, sz, to, p, row, rows):
        def at(ref, off):
            return ref[p + off, pl.ds(row, rows)]

        s1 = at(sz, 1) + at(sz, 3)
        s2 = at(sz, 0) + at(sz, 4)
        m1 = at(mz, 1) + at(mz, 3)
        m2 = at(mz, 0) + at(mz, 4)
        m0 = at(mz, 2)
        one = (66.0 * at(sz, 2) + 26.0 * s1 + s2) + (6.0 * m0 - 2.0 * m1 - m2)
        two = 66.0 * m0 + 26.0 * m1 + m2
        to[0, p, pl.ds(row, rows)] = (66.0 * SCALE) * one + (6.0 * SCALE) * two
        to[1, p, pl.ds(row, rows)] = (26.0 * SCALE) * one - (2.0 * SCALE) * two
        to[2, p, pl.ds(row, rows)] = SCALE * (one - two)

    def y_stage(to, p, row, rows, m, scr_rows, src, src_row):
        def at(k, off):
            return to[k, p, pl.ds(row + off, rows)]

        k = at(0, 0) + ((at(1, -1) + at(1, 1)) + (at(2, -2) + at(2, 2)))
        centre = src[p + 2, pl.ds(src_row, rows)]
        return m * (k + scr_rows * centre), centre

    def total_of(acc, terms):
        return tuple(x + y for x, y in zip(acc, terms))

    def own_terms(value, centre, first, tiles):
        terms = []
        for prod in (value * centre, value * value, value):
            t = [prod[8 * k:8 * k + 8] for k in range(tiles)]
            if first is None:
                terms.append((t[0] + t[1]) + t[2])
            elif tiles == 2:
                terms.append(jnp.where(sub >= first, t[0], t[1]))
            else:
                terms.append((jnp.where(sub >= first, t[0], t[4]) + t[1]) + (t[2] + t[3]))
        return terms

    def mask_from(dx, base):
        k = [jnp.broadcast_to(M[dx, pl.ds(j, 1)], (8, 128)) for j in range(4)]
        cut = sub >= -base
        return jnp.concatenate([jnp.where(cut, k[1], k[0]), k[1], jnp.where(cut, k[2], k[1]), k[2],
                                jnp.where(cut, k[3], k[2])], axis=0)

    mu0, sum0 = zero, zero
    for p in range(HR, HR + 16):
        z_stage(R, 8, MZ, SZ, 16, p, 32)
        v = R[p, pl.ds(8, 32)]
        w = v * v
        mu0 = mu0 + ((w[0:8] + w[8:16]) + (w[16:24] + w[24:32]))
        sum0 = sum0 + ((v[0:8] + v[8:16]) + (v[16:24] + v[24:32]))
    for p in range(6, 18):
        x_stage(MZ, SZ, TA, p, 16, 32)
    middle = jnp.concatenate([own[0:8], jnp.where(sub >= 4, own[16:24], own[0:8]), own[16:24]], axis=0)
    acc = (zero, zero, zero)
    for p in range(6, 18):
        value, centre = y_stage(TA, p, 20, 24, middle, S[p, pl.ds(12, 24)], R, 12)
        U1[p, pl.ds(8, 24)] = value
        acc = total_of(acc, own_terms(value, centre, None, 3))

    halo = [p for p in range(28) if not HR <= p < HR + 16]
    outer = [p for p in range(24) if not 6 <= p < 18]
    receive((0,), (0,))
    for p in halo:
        z_stage(R, 8, MZ, SZ, 16, p, 32)
    for p in outer:
        x_stage(MZ, SZ, TA, p, 16, 32)
    receive((0,), (1,))
    for p in range(HR, HR + 16):
        z_stage(R, 0, MZ, SZ, 8, p, 8)
        z_stage(R, 40, MZ, SZ, 48, p, 8)
    for p in range(6, 18):
        x_stage(MZ, SZ, TA, p, 8, 8)
        x_stage(MZ, SZ, TA, p, 48, 8)
    receive((0,), (2,))
    for p in halo:
        z_stage(R, 0, MZ, SZ, 8, p, 8)
        z_stage(R, 40, MZ, SZ, 48, p, 8)
    for p in outer:
        x_stage(MZ, SZ, TA, p, 8, 8)
        x_stage(MZ, SZ, TA, p, 48, 8)
    receive((2, 1))
    masks = [mask_from(dx, -4) for dx in range(3)]
    for p in range(24):
        dx = 0 if p < 4 else 1 if p < 20 else 2
        if 6 <= p < 18:
            low, c_low = y_stage(TA, p, 12, 8, masks[1][0:8], S[p, pl.ds(4, 8)], R, 4)
            high, c_high = y_stage(TA, p, 44, 8, masks[1][32:40], S[p, pl.ds(36, 8)], R, 36)
            U1[p, pl.ds(0, 8)] = low
            U1[p, pl.ds(32, 8)] = high
            acc = total_of(acc, own_terms(jnp.concatenate([low, high], axis=0),
                                          jnp.concatenate([c_low, c_high], axis=0), 4, 2))
        else:
            value, centre = y_stage(TA, p, 12, 40, masks[dx], S[p, pl.ds(4, 40)], R, 4)
            U1[p, pl.ds(0, 40)] = value
            if dx == 1:
                acc = total_of(acc, own_terms(value, centre, 4, 5))
    mu1, mu2, sum1 = acc

    for p in range(0, 24):
        z_stage(U1, 0, MZ2, SZ2, 8, p, 40)
    for p in range(20):
        x_stage(MZ2, SZ2, TB, p, 8, 40)
    masks = [mask_from(dx, -2) for dx in range(3)]
    acc = (zero, zero, zero)
    for p in range(20):
        dx = 0 if p < 2 else 1 if p < 18 else 2
        value, centre = y_stage(TB, p, 10, 40, masks[dx], S[p + 2, pl.ds(6, 40)], U1, 2)
        U2[p, pl.ds(0, 40)] = value
        if dx == 1:
            acc = total_of(acc, own_terms(value, centre, 2, 5))
    mu3, mu4, sum2 = acc

    for p in range(0, 20):
        z_stage(U2, 0, MZ, SZ, 8, p, 40)
    for p in range(16):
        x_stage(MZ, SZ, TA, p, 8, 40)
    sub16 = lax.broadcasted_iota(jnp.int32, (16, 128), 0)
    lane16 = lax.broadcasted_iota(jnp.int32, (16, 128), 1)
    lane1 = lax.broadcasted_iota(jnp.int32, (1, 128), 1)
    rows = jnp.zeros((16, 128), jnp.float32)
    for k, acc in ((0, mu0), (1, mu1), (2, mu2), (3, mu3), (4, mu4), (6, sum0), (7, sum1), (8, sum2)):
        rows = jnp.where(sub16 == k, jnp.sum(acc, axis=0, keepdims=True), rows)
    total = jnp.sum(rows, axis=1, keepdims=True)
    spread = jnp.where(lane16 == sub16, total, 0.0)
    values = jnp.sum(spread, axis=0, keepdims=True)
    coarse = jnp.zeros((1, 128), jnp.float32)
    for k in range(6):
        coarse = jnp.where(lane1 == k, 1.5 * 2.0 ** (26 + k), coarse)
    mu5 = zero
    for p in range(16):
        value, centre = y_stage(TA, p, 10, 32, own, S[p + 4, pl.ds(8, 32)], U2, 2)
        w = value * centre
        mu5 = mu5 + ((w[0:8] + w[8:16]) + (w[16:24] + w[24:32]))

    last = jnp.sum(jnp.sum(mu5, axis=0, keepdims=True), axis=1, keepdims=True)
    values = jnp.where(lane1 == 5, last, values)
    rounded = (values + coarse) - coarse
    high = jnp.where(lane1 < 6, rounded, values)
    rest = jnp.where(lane1 < 6, values - rounded, 0.0)
    row = high + pltpu.roll(rest, 64, 1)
    row = jnp.where(lane1 == 9, count.astype(jnp.float32), row)

    pending = []
    mine = gy * 2 + core
    ar1[mine] = row
    for j in (10, 6, 9, 7, 11, 5, 8, 2, 14, 13, 3, 1, 15, 12, 4, 0):
        for c in (1 - core, core):
            if j == 0 and c is core:
                continue
            pltpu.make_async_remote_copy(
                ar1.at[mine], ar1.at[mine], asem.at[0], arsem.at[0],
                device_id=(2 * z + c, lax.rem(gy + j, NGY)), device_id_type=MESH).start()
    wait = pltpu.make_async_remote_copy(
        ar1.at[pl.ds(0, 31)], ar1.at[pl.ds(0, 31)], asem.at[0], arsem.at[0],
        device_id=(2 * z + 1 - core, gy), device_id_type=MESH)
    wait.wait_recv()
    pending.append(wait)

    ar2[z] = tree([ar1[j] for j in range(32)])
    pl.semaphore_wait(token, 2)
    for off in (8, 7, -7, 6, -6, 5, -5, 4, -4, 3, -3, 2, -2, 1, -1):
        pltpu.make_async_remote_copy(
            ar2.at[z], ar2.at[z], asem.at[1], arsem.at[1],
            device_id=(at_z(off), gy), device_id_type=MESH).start()
    wait = pltpu.make_async_remote_copy(
        ar2.at[pl.ds(0, 15)], ar2.at[pl.ds(0, 15)], asem.at[1], arsem.at[1],
        device_id=(at_z(1), gy), device_id_type=MESH)
    wait.wait_recv()
    pending.append(wait)
    row = tree([ar2[j] for j in range(16)])

    goal = jnp.where(sub16 < 10, sub16, sub16 + 54)
    picked = jnp.sum(jnp.where(lane16 == goal, row, 0.0), axis=1, keepdims=True)
    value = [jnp.broadcast_to(picked[k:k + 1], (8, 128)) for k in range(16)]
    mu = [two_sum(value[k], value[10 + k]) for k in range(6)]
    c0, c1, c2 = cg_weights(mu)
    iso = (c0 * value[6] + c1 * value[7] + c2 * value[8]) / (value[9] * float(BLK ** 3))

    def tile5(v):
        return jnp.concatenate([v] * 5, axis=0)

    iso_out[...] = iso
    c0, c1, c2 = tile5(c0), tile5(c1), tile5(c2)

    def solve(p, carry):
        x_out[p] = c0 * R[HR + p, pl.ds(8, 40)] + c1 * U1[4 + p, pl.ds(4, 40)] + c2 * U2[2 + p, pl.ds(2, 40)]
        return carry

    lax.fori_loop(0, 17, solve, 0, unroll=True)

    for i, ok in enumerate(has):
        @pl.when(ok)
        def _():
            for c in pieces(i, (0, 1, 2)):
                c.wait_send()
    for c in pending:
        c.wait_send()


def crossing_kernel(x_ref, iso_ref, vis, ind_out, cross_out, G, W, BR, vis_s, sem):
    load = pltpu.make_async_copy(vis.at[0], vis_s, sem.at[0])
    load.start()
    store = pltpu.make_async_copy(x_ref.at[pl.ds(0, 16), pl.ds(0, 32)], ind_out, sem.at[1])
    store.start()
    lane = lax.broadcasted_iota(jnp.int32, (8, 128), 1)
    iso = jnp.concatenate([iso_ref[...]] * 5, axis=0)

    for p in range(17):
        G[p] = sigmoid4(x_ref[p] - iso)
    BR[pl.ds(16 * 96, 96)] = jnp.zeros((96, 128), jnp.float32)

    lane32 = lax.broadcasted_iota(jnp.int32, (32, 128), 1)
    edge = lane32 == 127
    empty = sigmoid4(0.0 - iso[0:32])
    group = lane // BLK
    odd = [(group // (1 << bit)) % 2 == 1 for bit in range(3)]
    load.wait()
    slots = []
    for q in range(VIS):
        n = vis_s[0, q]
        slots.append(jnp.where(n >= 0, n, 16) * 96)
    stores = [store]
    for e in range(3):
        for p in range(16):
            g = G[p, pl.ds(0, 32)]
            if e == 0:
                other = G[p + 1, pl.ds(0, 32)]
            elif e == 1:
                other = G[p, pl.ds(1, 32)]
            else:
                other = jnp.where(edge, empty, pltpu.roll(g, 127, 1))
            h = crossing_weight(g, other)
            for w in range(2):
                W[e, pl.ds((p // 4) * 128 + w * 64 + p % 4 * 16, 16)] = h[16 * w:16 * w + 16]
        for first in range(0, 8, 4):
            parts = range(first, first + 4)
            vs = {}
            for part in parts:
                vs[part] = [W[e, pl.ds(part * 64 + (-j) % 8, 8, stride=8)] for j in range(8)]
            for part in parts:
                vs[part] = [v if j == 0 else pltpu.roll(v, 16 * ((-j) % 8), 1) for j, v in enumerate(vs[part])]
            for bit in range(3):
                for part in parts:
                    old = vs[part]
                    vs[part] = [jnp.where(odd[bit], old[(t - (1 << bit)) % 8], old[t]) for t in range(8)]
            for part in parts:
                vs[part] = [v if t == 0 else pltpu.roll(v, 128 - 16 * t, 1) for t, v in enumerate(vs[part])]
            for part in parts:
                w, ib = part % 2, part // 2
                for t in range(8):
                    BR[pl.ds((w * 8 + t) * 96 + e * 32 + ib * 8, 8)] = vs[part][t]
        for q in range(VIS):
            start = pl.multiple_of(slots[q] + e * 32, 8)
            stores.append(pltpu.make_async_copy(
                BR.at[pl.ds(start, 32)], cross_out.at[pl.ds(q * 96 + e * 32, 32)], sem.at[2 + q * 3 + e]))
            stores[-1].start()
    for c in stores:
        c.wait()


def body(right_side, screening, active_blocks, visible_bricks):
    f32 = jnp.float32
    right_side, screening, active_blocks, visible_bricks = (
        pltpu.with_memory_space_constraint(v, pltpu.HBM)
        for v in (right_side, screening, active_blocks, visible_bricks))
    hbm = pl.BlockSpec(memory_space=pltpu.HBM)
    vmem = pl.BlockSpec(memory_space=pltpu.VMEM)
    x, iso = pl.pallas_call(
        solve_kernel,
        out_shape=(jax.ShapeDtypeStruct((17, 40, 128), f32), jax.ShapeDtypeStruct((8, 128), f32)),
        in_specs=[hbm] * 3,
        out_specs=(vmem, vmem),
        scratch_shapes=[
            pltpu.VMEM((28, 48, 128), f32),
            pltpu.VMEM((24, 48, 128), f32),
            pltpu.VMEM((3, 4, 128), f32),
            pltpu.VMEM((24, 48, 128), f32),
            pltpu.VMEM((20, 48, 128), f32),
            pltpu.VMEM((28, 64, 128), f32),
            pltpu.VMEM((28, 64, 128), f32),
            pltpu.VMEM((24, 56, 128), f32),
            pltpu.VMEM((24, 56, 128), f32),
            pltpu.VMEM((3, 24, 64, 128), f32),
            pltpu.VMEM((3, 20, 56, 128), f32),
            pltpu.SMEM((1, ACT), jnp.int32),
            pltpu.VMEM((32, 1, 128), f32),
            pltpu.VMEM((16, 1, 128), f32),
            pltpu.SemaphoreType.DMA((3,)),
            pltpu.SemaphoreType.DMA((8, 3)),
            pltpu.SemaphoreType.DMA((8, 3)),
            pltpu.SemaphoreType.DMA((2,)),
            pltpu.SemaphoreType.DMA((2,)),
            pltpu.SemaphoreType.REGULAR,
        ],
        compiler_params=pltpu.CompilerParams(
            collective_id=0, has_side_effects=True, vmem_limit_bytes=32 << 20),
    )(right_side, screening, active_blocks)
    indicator, crossing = pl.pallas_call(
        crossing_kernel,
        out_shape=(jax.ShapeDtypeStruct((16, 32, 128), f32), jax.ShapeDtypeStruct((VIS * 96, 128), f32)),
        in_specs=[vmem, vmem, hbm],
        out_specs=(hbm, hbm),
        scratch_shapes=[
            pltpu.VMEM((17, 40, 128), f32),
            pltpu.VMEM((3, 512, 128), f32),
            pltpu.VMEM((17 * 96, 128), f32),
            pltpu.SMEM((1, VIS), jnp.int32),
            pltpu.SemaphoreType.DMA((2 + 3 * VIS,)),
        ],
        compiler_params=pltpu.CompilerParams(vmem_limit_bytes=24 << 20),
    )(x, iso, visible_bricks)
    return indicator, crossing.reshape(VIS, 1, 3, BLK ** 3)


def solution(mesh):
    spec = P("gx", "gy", None)
    return jax.shard_map(
        body,
        mesh=mesh,
        in_specs=(spec, spec, spec, spec),
        out_specs=(spec, P("gx", "gy", None, None)),
        check_vma=False,
    )
```

```python
import jax
import jax.numpy as jnp
from jax import lax
from jax.experimental import pallas as pl
from jax.experimental.pallas import tpu as pltpu
from jax.sharding import PartitionSpec as P

MESH = pl.DeviceIdType.MESH
BLK = 16
ACT = 12
VIS = 8
NGX = 32
NGY = 16
NZ = 16
SIGMA = 2.5
HR = 6
HS = 4
SCALE = 1.0 / 86400.0
NEIGHBOURS = [(1, 1), (1, -1), (-1, 1), (-1, -1), (0, 1), (0, -1), (1, 0), (-1, 0)]


def two_sum(a, b):
    s = a + b
    t = s - a
    return s, (a - (s - t)) + (b - t)


def quick_two_sum(a, b):
    s = a + b
    return s, b - (s - a)


def split(a):
    c = 4097.0 * a
    hi = c - (c - a)
    return hi, a - hi


def two_prod(a, b):
    p = a * b
    ah, al = split(a)
    bh, bl = split(b)
    return p, ((ah * bh - p) + ah * bl + al * bh) + al * bl


def dd_add(x, y):
    s, e = two_sum(x[0], y[0])
    return quick_two_sum(s, e + (x[1] + y[1]))


def dd_neg(x):
    return -x[0], -x[1]


def dd_sub(x, y):
    return dd_add(x, dd_neg(y))


def dd_mul(x, y):
    p, e = two_prod(x[0], y[0])
    return quick_two_sum(p, e + (x[0] * y[1] + x[1] * y[0]))


def dd_div(x, y):
    q = x[0] / y[0]
    r = dd_sub(x, dd_mul(y, (q, jnp.zeros_like(q))))
    return quick_two_sum(q, r[0] / y[0])


def cg_weights(mu):
    one = (jnp.ones_like(mu[0][0]), jnp.zeros_like(mu[0][0]))
    inv = dd_div(one, mu[0])
    row = [dd_mul(m, inv) for m in mu[1:]]
    a = row[0]
    level = [dd_sub(row[k + 1], dd_mul(a, row[k])) for k in range(4)]
    first = [(jnp.zeros_like(a[0]), jnp.zeros_like(a[0]))] + level
    central = []
    for _ in range(4):
        first = [dd_sub(first[k + 1], dd_mul(a, first[k])) for k in range(len(first) - 1)]
        central.append(first[0])
    m2, m3, m4, m5 = central
    tiny = 1e-30
    m2s = (jnp.maximum(m2[0], tiny), jnp.where(m2[0] > tiny, m2[1], 0.0))
    b1 = dd_div(m3, m2s)
    m22 = dd_mul(m2, m2)
    h2 = dd_sub(dd_sub(m4, dd_mul(b1, m3)), m22)
    h2s = jnp.maximum(h2[0], tiny)
    inner = dd_sub(dd_mul(b1, m3), dd_add(m4, m4))
    inner = dd_add(inner, dd_add(m22, m22))
    top = dd_add(m5, dd_mul(b1, inner))
    m23 = dd_mul(m2, m3)
    top = dd_sub(top, dd_add(m23, m23))
    d0 = a[0] + SIGMA
    d1 = jnp.clip(d0 + b1[0], 0.25, 9.0)
    d2 = jnp.clip(d0 + top[0] / h2s, 0.25, 9.0)
    beta1 = jnp.maximum(m2[0], 0.0)
    beta2 = jnp.clip(h2[0] / m2s[0], 0.0, 25.0)
    bb1 = d1 - d0
    minor = d1 * d2 - beta2
    y2 = 1.0 / (d0 * minor - beta1 * d2)
    y1 = -d2 * y2
    y0 = minor * y2
    c2 = y2
    c1 = y1 - y2 * (2.0 * a[0] + bb1)
    c0 = y0 - a[0] * y1 + y2 * (a[0] * a[0] + a[0] * bb1 - m2[0])
    return c0, c1, c2


def tree(parts):
    while len(parts) > 1:
        parts = [a + b for a, b in zip(parts[::2], parts[1::2])]
    return parts[0]


def sigmoid4(v):
    return 1.0 / (1.0 + jnp.exp(-4.0 * v))


def crossing_weight(lower, upper):
    return lower * (1.0 - upper) + (1.0 - lower) * upper


def solve_kernel(rhs, scr, act, x_out, iso_out,
           R, S, M, U1, U2, MZ, SZ, MZ2, SZ2, TA, TB, act_s, ar1, ar2,
                 lsem, ssem, rsem, asem, arsem, token):
    gx = lax.axis_index("gx")
    gy = lax.axis_index("gy")
    z = gx // 2
    core = lax.rem(gx, 2)

    def at_z(off):
        return lax.rem(z + off + NZ, NZ) * 2 + core

    loads = [
        pltpu.make_async_copy(act.at[0], act_s, lsem.at[0]),
        pltpu.make_async_copy(rhs, R.at[pl.ds(HR, 16), pl.ds(8, 32)], lsem.at[1]),
        pltpu.make_async_copy(scr, S.at[pl.ds(HS, 16), pl.ds(8, 32)], lsem.at[2]),
    ]
    for c in loads:
        c.start()

    bar = pltpu.get_barrier_semaphore()

    def tell(x, y):
        pl.semaphore_signal(bar, inc=1, device_id=(x, y), device_id_type=MESH)

    def along_x(off):
        return lax.rem(gx + off + NGX, NGX)

    def along_y(off):
        return lax.rem(gy + off + NGY, NGY)

    for dx, dy in NEIGHBOURS:
        tell(along_x(dx), along_y(dy))
    has = []
    for dx, dy in NEIGHBOURS:
        ok = None
        for cond in ([gx < NGX - 1] if dx == 1 else []) + ([gx > 0] if dx == -1 else []) + (
            [gy < NGY - 1] if dy == 1 else []) + ([gy > 0] if dy == -1 else []):
            ok = cond if ok is None else jnp.logical_and(ok, cond)
        has.append(ok)
    @pl.when(gx == 0)
    def _():
        R[pl.ds(0, HR)] = jnp.zeros((HR, 48, 128), jnp.float32)
        S[pl.ds(0, HS)] = jnp.zeros((HS, 48, 128), jnp.float32)
        M[0] = jnp.zeros((4, 128), jnp.float32)

    @pl.when(gx == NGX - 1)
    def _():
        R[pl.ds(HR + 16, HR)] = jnp.zeros((HR, 48, 128), jnp.float32)
        S[pl.ds(HS + 16, HS)] = jnp.zeros((HS, 48, 128), jnp.float32)
        M[2] = jnp.zeros((4, 128), jnp.float32)

    def clear_rows(row, kind):
        R[:, pl.ds(row, 8)] = jnp.zeros((28, 8, 128), jnp.float32)
        S[:, pl.ds(row, 8)] = jnp.zeros((24, 8, 128), jnp.float32)
        M[:, pl.ds(kind, 1)] = jnp.zeros((3, 1, 128), jnp.float32)

    @pl.when(gy == 0)
    def _():
        clear_rows(0, 0)

    @pl.when(gy == NGY - 1)
    def _():
        clear_rows(40, 3)

    lane = lax.broadcasted_iota(jnp.int32, (8, 128), 1)
    loads[0].wait()
    entries = [act_s[0, q] for q in range(ACT)]
    count = jnp.int32(0)
    for e in entries:
        count = count + jnp.where(e >= 0, 1, 0)
    for w in range(2):
        number = lane // BLK + 8 * w
        own = jnp.zeros((8, 128), jnp.float32)
        for e in entries:
            own = jnp.where(number == e, 1.0, own)
        M[1, pl.ds(1 + w, 1)] = own[0:1]
    loads[1].wait()
    loads[2].wait()

    def mask_rows(dx, kinds):
        tiles = [jnp.broadcast_to(M[dx, pl.ds(k, 1)], (8, 128)) for k in range(4)]
        return jnp.concatenate([tiles[k] for k in kinds], axis=0)

    own = mask_rows(1, (1, 1, 2, 2))

    def prepare(p, carry):
        R[HR + p, pl.ds(8, 32)] = R[HR + p, pl.ds(8, 32)] * own
        S[HS + p, pl.ds(8, 32)] = S[HS + p, pl.ds(8, 32)] - SIGMA
        return carry

    lax.fori_loop(0, 16, prepare, 0, unroll=4)

    pl.semaphore_wait(bar, 8)

    def vouch(k):
        for off in (1 << k, -(1 << k)):
            pl.semaphore_signal(token.at[k], inc=1, device_id=(along_x(off), gy), device_id_type=MESH)
            if k < 3:
                pl.semaphore_signal(token.at[k], inc=1, device_id=(gx, along_y(off)), device_id_type=MESH)

    vouch(0)

    def pieces(i, which):
        dx, dy = NEIGHBOURS[i]
        out = []
        for n in which:
            if n == 2:
                first, size = {0: (1, 2), 1: (2, 1), -1: (1, 1)}[dy]
                src = M.at[1, pl.ds(first, size)]
                dst = M.at[1 - dx, pl.ds({0: 1, 1: 0, -1: 3}[dy], size)]
            else:
                ref, h = ((R, HR), (S, HS))[n]
                planes = {0: (h, h, 16), 1: (16, 0, h), -1: (h, h + 16, h)}[dx]
                rows = {0: (8, 8, 32), 1: (40 - h, 8 - h, h), -1: (8, 40, h)}[dy]
                src = ref.at[pl.ds(planes[0], planes[2]), pl.ds(rows[0], rows[2])]
                dst = ref.at[pl.ds(planes[1], planes[2]), pl.ds(rows[1], rows[2])]
            out.append(pltpu.make_async_remote_copy(
                src, dst, ssem.at[i, n], rsem.at[i, n],
                device_id=(gx + dx, gy + dy), device_id_type=MESH))
        return out

    opposite = [NEIGHBOURS.index((-dx, -dy)) for dx, dy in NEIGHBOURS]

    def receive(which, kinds=(0, 1, 2)):
        for i in range(8):
            dx, dy = NEIGHBOURS[i]
            if (2 if dx and dy else 0 if dx else 1) not in kinds:
                continue

            @pl.when(has[opposite[i]])
            def _():
                for c in pieces(i, which):
                    c.wait_recv()

    for which in ((0,), (2, 1)):
        for i, ok in enumerate(has):
            @pl.when(ok)
            def _():
                for c in pieces(i, which):
                    c.start()

    zero = jnp.zeros((8, 128), jnp.float32)
    sub = lax.broadcasted_iota(jnp.int32, (8, 128), 0)

    lanes = lax.broadcasted_iota(jnp.int32, (48, 128), 1)

    def z_stage(src, row, mz, sz, out_row, p, rows):
        v = src[p, pl.ds(row, rows)]
        at = lanes[0:rows]
        p1 = jnp.where(at < 1, 0.0, pltpu.roll(v, 1, 1)) + jnp.where(at > 126, 0.0, pltpu.roll(v, 127, 1))
        p2 = jnp.where(at < 2, 0.0, pltpu.roll(v, 2, 1)) + jnp.where(at > 125, 0.0, pltpu.roll(v, 126, 1))
        mz[p, pl.ds(out_row, rows)] = 66.0 * v + 26.0 * p1 + p2
        sz[p, pl.ds(out_row, rows)] = 6.0 * v - 2.0 * p1 - p2

    def x_stage(mz, sz, to, p, row, rows):
        def at(ref, off):
            return ref[p + off, pl.ds(row, rows)]

        s1 = at(sz, 1) + at(sz, 3)
        s2 = at(sz, 0) + at(sz, 4)
        m1 = at(mz, 1) + at(mz, 3)
        m2 = at(mz, 0) + at(mz, 4)
        m0 = at(mz, 2)
        one = (66.0 * at(sz, 2) + 26.0 * s1 + s2) + (6.0 * m0 - 2.0 * m1 - m2)
        two = 66.0 * m0 + 26.0 * m1 + m2
        to[0, p, pl.ds(row, rows)] = (66.0 * SCALE) * one + (6.0 * SCALE) * two
        to[1, p, pl.ds(row, rows)] = (26.0 * SCALE) * one - (2.0 * SCALE) * two
        to[2, p, pl.ds(row, rows)] = SCALE * (one - two)

    def y_stage(to, p, row, rows, m, scr_rows, src, src_row):
        def at(k, off):
            return to[k, p, pl.ds(row + off, rows)]

        k = at(0, 0) + ((at(1, -1) + at(1, 1)) + (at(2, -2) + at(2, 2)))
        centre = src[p + 2, pl.ds(src_row, rows)]
        return m * (k + scr_rows * centre), centre

    def total_of(acc, terms):
        return tuple(x + y for x, y in zip(acc, terms))

    def own_terms(value, centre, first, tiles):
        terms = []
        for prod in (value * centre, value * value, value):
            t = [prod[8 * k:8 * k + 8] for k in range(tiles)]
            if first is None:
                terms.append((t[0] + t[1]) + t[2])
            elif tiles == 2:
                terms.append(jnp.where(sub >= first, t[0], t[1]))
            else:
                terms.append((jnp.where(sub >= first, t[0], t[4]) + t[1]) + (t[2] + t[3]))
        return terms

    def mask_from(dx, base):
        k = [jnp.broadcast_to(M[dx, pl.ds(j, 1)], (8, 128)) for j in range(4)]
        cut = sub >= -base
        return jnp.concatenate([jnp.where(cut, k[1], k[0]), k[1], jnp.where(cut, k[2], k[1]), k[2],
                                jnp.where(cut, k[3], k[2])], axis=0)

    mu0, sum0 = zero, zero
    for p in range(HR, HR + 16):
        z_stage(R, 8, MZ, SZ, 16, p, 32)
        v = R[p, pl.ds(8, 32)]
        w = v * v
        mu0 = mu0 + ((w[0:8] + w[8:16]) + (w[16:24] + w[24:32]))
        sum0 = sum0 + ((v[0:8] + v[8:16]) + (v[16:24] + v[24:32]))
    for p in range(6, 18):
        x_stage(MZ, SZ, TA, p, 16, 32)
    middle = jnp.concatenate([own[0:8], jnp.where(sub >= 4, own[16:24], own[0:8]), own[16:24]], axis=0)
    acc = (zero, zero, zero)
    for p in range(6, 18):
        value, centre = y_stage(TA, p, 20, 24, middle, S[p, pl.ds(12, 24)], R, 12)
        U1[p, pl.ds(8, 24)] = value
        acc = total_of(acc, own_terms(value, centre, None, 3))

    halo = [p for p in range(28) if not HR <= p < HR + 16]
    outer = [p for p in range(24) if not 6 <= p < 18]
    for p in range(6, 18):
        z_stage(U1, 8, MZ2, SZ2, 16, p, 24)
    for p in range(6, 14):
        x_stage(MZ2, SZ2, TB, p, 16, 24)
    pl.semaphore_wait(token.at[0], 4)
    vouch(1)
    receive((0,), (0,))
    for p in halo:
        z_stage(R, 8, MZ, SZ, 16, p, 32)
    for p in outer:
        x_stage(MZ, SZ, TA, p, 16, 32)
    receive((0,), (1,))
    for p in range(HR, HR + 16):
        z_stage(R, 0, MZ, SZ, 8, p, 8)
        z_stage(R, 40, MZ, SZ, 48, p, 8)
    for p in range(6, 18):
        x_stage(MZ, SZ, TA, p, 8, 8)
        x_stage(MZ, SZ, TA, p, 48, 8)
    receive((0,), (2,))
    pl.semaphore_wait(token.at[1], 4)
    vouch(2)
    for p in halo:
        z_stage(R, 0, MZ, SZ, 8, p, 8)
        z_stage(R, 40, MZ, SZ, 48, p, 8)
    for p in outer:
        x_stage(MZ, SZ, TA, p, 8, 8)
        x_stage(MZ, SZ, TA, p, 48, 8)
    receive((2, 1))
    masks = [mask_from(dx, -4) for dx in range(3)]
    for p in range(24):
        dx = 0 if p < 4 else 1 if p < 20 else 2
        if 6 <= p < 18:
            low, c_low = y_stage(TA, p, 12, 8, masks[1][0:8], S[p, pl.ds(4, 8)], R, 4)
            high, c_high = y_stage(TA, p, 44, 8, masks[1][32:40], S[p, pl.ds(36, 8)], R, 36)
            U1[p, pl.ds(0, 8)] = low
            U1[p, pl.ds(32, 8)] = high
            acc = total_of(acc, own_terms(jnp.concatenate([low, high], axis=0),
                                          jnp.concatenate([c_low, c_high], axis=0), 4, 2))
        else:
            value, centre = y_stage(TA, p, 12, 40, masks[dx], S[p, pl.ds(4, 40)], R, 4)
            U1[p, pl.ds(0, 40)] = value
            if dx == 1:
                acc = total_of(acc, own_terms(value, centre, 4, 5))
    mu1, mu2, sum1 = acc

    for p in range(24):
        if 6 <= p < 18:
            z_stage(U1, 0, MZ2, SZ2, 8, p, 8)
            z_stage(U1, 32, MZ2, SZ2, 40, p, 8)
        else:
            z_stage(U1, 0, MZ2, SZ2, 8, p, 40)
    for p in range(20):
        if 6 <= p < 14:
            x_stage(MZ2, SZ2, TB, p, 8, 8)
            x_stage(MZ2, SZ2, TB, p, 40, 8)
        else:
            x_stage(MZ2, SZ2, TB, p, 8, 40)
    masks = [mask_from(dx, -2) for dx in range(3)]
    acc = (zero, zero, zero)
    for p in range(20):
        dx = 0 if p < 2 else 1 if p < 18 else 2
        value, centre = y_stage(TB, p, 10, 40, masks[dx], S[p + 2, pl.ds(6, 40)], U1, 2)
        U2[p, pl.ds(0, 40)] = value
        if dx == 1:
            acc = total_of(acc, own_terms(value, centre, 2, 5))
    mu3, mu4, sum2 = acc

    for p in range(0, 20):
        z_stage(U2, 0, MZ, SZ, 8, p, 40)
    for p in range(16):
        x_stage(MZ, SZ, TA, p, 8, 40)
    sub16 = lax.broadcasted_iota(jnp.int32, (16, 128), 0)
    lane16 = lax.broadcasted_iota(jnp.int32, (16, 128), 1)
    lane1 = lax.broadcasted_iota(jnp.int32, (1, 128), 1)
    rows = jnp.zeros((16, 128), jnp.float32)
    for k, acc in ((0, mu0), (1, mu1), (2, mu2), (3, mu3), (4, mu4), (6, sum0), (7, sum1), (8, sum2)):
        rows = jnp.where(sub16 == k, jnp.sum(acc, axis=0, keepdims=True), rows)
    total = jnp.sum(rows, axis=1, keepdims=True)
    spread = jnp.where(lane16 == sub16, total, 0.0)
    values = jnp.sum(spread, axis=0, keepdims=True)
    coarse = jnp.zeros((1, 128), jnp.float32)
    for k in range(6):
        coarse = jnp.where(lane1 == k, 1.5 * 2.0 ** (26 + k), coarse)
    mu5 = zero
    for p in range(16):
        value, centre = y_stage(TA, p, 10, 32, own, S[p + 4, pl.ds(8, 32)], U2, 2)
        w = value * centre
        mu5 = mu5 + ((w[0:8] + w[8:16]) + (w[16:24] + w[24:32]))

    last = jnp.sum(jnp.sum(mu5, axis=0, keepdims=True), axis=1, keepdims=True)
    values = jnp.where(lane1 == 5, last, values)
    rounded = (values + coarse) - coarse
    high = jnp.where(lane1 < 6, rounded, values)
    rest = jnp.where(lane1 < 6, values - rounded, 0.0)
    row = high + pltpu.roll(rest, 64, 1)
    row = jnp.where(lane1 == 9, count.astype(jnp.float32), row)

    pending = []
    mine = gy * 2 + core
    pl.semaphore_wait(token.at[2], 4)
    ar1[mine] = row
    for j in (10, 6, 9, 7, 11, 5, 8, 2, 14, 13, 3, 1, 15, 12, 4, 0):
        for c in (1 - core, core):
            if j == 0 and c is core:
                continue
            pltpu.make_async_remote_copy(
                ar1.at[mine], ar1.at[mine], asem.at[0], arsem.at[0],
                device_id=(2 * z + c, lax.rem(gy + j, NGY)), device_id_type=MESH).start()
    wait = pltpu.make_async_remote_copy(
        ar1.at[pl.ds(0, 31)], ar1.at[pl.ds(0, 31)], asem.at[0], arsem.at[0],
        device_id=(2 * z + 1 - core, gy), device_id_type=MESH)
    vouch(3)
    for i, ok in enumerate(has):
        @pl.when(ok)
        def _():
            for c in pieces(i, (0, 1, 2)):
                c.wait_send()
    wait.wait_recv()
    pending.append(wait)

    ar2[z] = tree([ar1[j] for j in range(32)])
    pl.semaphore_wait(token.at[3], 2)
    for off in (8, 7, -7, 6, -6, 5, -5, 4, -4, 3, -3, 2, -2, 1, -1):
        pltpu.make_async_remote_copy(
            ar2.at[z], ar2.at[z], asem.at[1], arsem.at[1],
            device_id=(at_z(off), gy), device_id_type=MESH).start()
    pending.pop().wait_send()
    wait = pltpu.make_async_remote_copy(
        ar2.at[pl.ds(0, 15)], ar2.at[pl.ds(0, 15)], asem.at[1], arsem.at[1],
        device_id=(at_z(1), gy), device_id_type=MESH)
    wait.wait_recv()
    pending.append(wait)
    row = tree([ar2[j] for j in range(16)])

    goal = jnp.where(sub16 < 10, sub16, sub16 + 54)
    picked = jnp.sum(jnp.where(lane16 == goal, row, 0.0), axis=1, keepdims=True)
    value = [jnp.broadcast_to(picked[k:k + 1], (8, 128)) for k in range(16)]
    mu = [two_sum(value[k], value[10 + k]) for k in range(6)]
    c0, c1, c2 = cg_weights(mu)
    iso = (c0 * value[6] + c1 * value[7] + c2 * value[8]) / (value[9] * float(BLK ** 3))

    def tile5(v):
        return jnp.concatenate([v] * 5, axis=0)

    iso_out[...] = iso
    c0, c1, c2 = tile5(c0), tile5(c1), tile5(c2)

    def solve(p, carry):
        x_out[p] = c0 * R[HR + p, pl.ds(8, 40)] + c1 * U1[4 + p, pl.ds(4, 40)] + c2 * U2[2 + p, pl.ds(2, 40)]
        return carry

    lax.fori_loop(0, 17, solve, 0, unroll=True)

    for c in pending:
        c.wait_send()


def crossing_kernel(x_ref, iso_ref, vis, ind_out, cross_out, G, W, BR, vis_s, sem):
    load = pltpu.make_async_copy(vis.at[0], vis_s, sem.at[0])
    load.start()
    store = pltpu.make_async_copy(x_ref.at[pl.ds(0, 16), pl.ds(0, 32)], ind_out, sem.at[1])
    store.start()
    lane = lax.broadcasted_iota(jnp.int32, (8, 128), 1)
    iso = jnp.concatenate([iso_ref[...]] * 5, axis=0)

    for p in range(17):
        G[p] = sigmoid4(x_ref[p] - iso)
    BR[pl.ds(16 * 96, 96)] = jnp.zeros((96, 128), jnp.float32)

    lane32 = lax.broadcasted_iota(jnp.int32, (32, 128), 1)
    edge = lane32 == 127
    empty = sigmoid4(0.0 - iso[0:32])
    group = lane // BLK
    odd = [(group // (1 << bit)) % 2 == 1 for bit in range(3)]
    load.wait()
    slots = []
    for q in range(VIS):
        n = vis_s[0, q]
        slots.append(jnp.where(n >= 0, n, 16) * 96)
    stores = [store]
    for e in range(3):
        for p in range(16):
            g = G[p, pl.ds(0, 32)]
            if e == 0:
                other = G[p + 1, pl.ds(0, 32)]
            elif e == 1:
                other = G[p, pl.ds(1, 32)]
            else:
                other = jnp.where(edge, empty, pltpu.roll(g, 127, 1))
            h = crossing_weight(g, other)
            for w in range(2):
                W[e, pl.ds((p // 4) * 128 + w * 64 + p % 4 * 16, 16)] = h[16 * w:16 * w + 16]
        for first in range(0, 8, 4):
            parts = range(first, first + 4)
            vs = {}
            for part in parts:
                vs[part] = [W[e, pl.ds(part * 64 + (-j) % 8, 8, stride=8)] for j in range(8)]
            for part in parts:
                vs[part] = [v if j == 0 else pltpu.roll(v, 16 * ((-j) % 8), 1) for j, v in enumerate(vs[part])]
            for bit in range(3):
                for part in parts:
                    old = vs[part]
                    vs[part] = [jnp.where(odd[bit], old[(t - (1 << bit)) % 8], old[t]) for t in range(8)]
            for part in parts:
                vs[part] = [v if t == 0 else pltpu.roll(v, 128 - 16 * t, 1) for t, v in enumerate(vs[part])]
            for part in parts:
                w, ib = part % 2, part // 2
                for t in range(8):
                    BR[pl.ds((w * 8 + t) * 96 + e * 32 + ib * 8, 8)] = vs[part][t]
        for q in range(VIS):
            start = pl.multiple_of(slots[q] + e * 32, 8)
            stores.append(pltpu.make_async_copy(
                BR.at[pl.ds(start, 32)], cross_out.at[pl.ds(q * 96 + e * 32, 32)], sem.at[2 + q * 3 + e]))
            stores[-1].start()
    for c in stores:
        c.wait()


def body(right_side, screening, active_blocks, visible_bricks):
    f32 = jnp.float32
    right_side, screening, active_blocks, visible_bricks = (
        pltpu.with_memory_space_constraint(v, pltpu.HBM)
        for v in (right_side, screening, active_blocks, visible_bricks))
    hbm = pl.BlockSpec(memory_space=pltpu.HBM)
    vmem = pl.BlockSpec(memory_space=pltpu.VMEM)
    x, iso = pl.pallas_call(
        solve_kernel,
        out_shape=(jax.ShapeDtypeStruct((17, 40, 128), f32), jax.ShapeDtypeStruct((8, 128), f32)),
        in_specs=[hbm] * 3,
        out_specs=(vmem, vmem),
        scratch_shapes=[
            pltpu.VMEM((28, 48, 128), f32),
            pltpu.VMEM((24, 48, 128), f32),
            pltpu.VMEM((3, 4, 128), f32),
            pltpu.VMEM((24, 48, 128), f32),
            pltpu.VMEM((20, 48, 128), f32),
            pltpu.VMEM((28, 64, 128), f32),
            pltpu.VMEM((28, 64, 128), f32),
            pltpu.VMEM((24, 56, 128), f32),
            pltpu.VMEM((24, 56, 128), f32),
            pltpu.VMEM((3, 24, 64, 128), f32),
            pltpu.VMEM((3, 20, 56, 128), f32),
            pltpu.SMEM((1, ACT), jnp.int32),
            pltpu.VMEM((32, 1, 128), f32),
            pltpu.VMEM((16, 1, 128), f32),
            pltpu.SemaphoreType.DMA((3,)),
            pltpu.SemaphoreType.DMA((8, 3)),
            pltpu.SemaphoreType.DMA((8, 3)),
            pltpu.SemaphoreType.DMA((2,)),
            pltpu.SemaphoreType.DMA((2,)),
            pltpu.SemaphoreType.REGULAR((4,)),
        ],
        compiler_params=pltpu.CompilerParams(
            collective_id=0, has_side_effects=True, vmem_limit_bytes=32 << 20),
    )(right_side, screening, active_blocks)
    indicator, crossing = pl.pallas_call(
        crossing_kernel,
        out_shape=(jax.ShapeDtypeStruct((16, 32, 128), f32), jax.ShapeDtypeStruct((VIS * 96, 128), f32)),
        in_specs=[vmem, vmem, hbm],
        out_specs=(hbm, hbm),
        scratch_shapes=[
            pltpu.VMEM((17, 40, 128), f32),
            pltpu.VMEM((3, 512, 128), f32),
            pltpu.VMEM((17 * 96, 128), f32),
            pltpu.SMEM((1, VIS), jnp.int32),
            pltpu.SemaphoreType.DMA((2 + 3 * VIS,)),
        ],
        compiler_params=pltpu.CompilerParams(vmem_limit_bytes=24 << 20),
    )(x, iso, visible_bricks)
    return indicator, crossing.reshape(VIS, 1, 3, BLK ** 3)


def solution(mesh):
    spec = P("gx", "gy", None)
    return jax.shard_map(
        body,
        mesh=mesh,
        in_specs=(spec, spec, spec, spec),
        out_specs=(spec, P("gx", "gy", None, None)),
        check_vma=False,
    )
```

```python
import jax
import jax.numpy as jnp
from jax import lax
from jax.experimental import pallas as pl
from jax.experimental.pallas import tpu as pltpu
from jax.sharding import PartitionSpec as P

MESH = pl.DeviceIdType.MESH
BLK = 16
ACT = 12
VIS = 8
NGX = 32
NGY = 16
NZ = 16
SIGMA = 2.5
HR = 6
HS = 4
SCALE = 1.0 / 86400.0
NEIGHBOURS = [(1, 1), (1, -1), (-1, 1), (-1, -1), (0, 1), (0, -1), (1, 0), (-1, 0)]


def two_sum(a, b):
    s = a + b
    t = s - a
    return s, (a - (s - t)) + (b - t)


def quick_two_sum(a, b):
    s = a + b
    return s, b - (s - a)


def split(a):
    c = 4097.0 * a
    hi = c - (c - a)
    return hi, a - hi


def two_prod(a, b):
    p = a * b
    ah, al = split(a)
    bh, bl = split(b)
    return p, ((ah * bh - p) + ah * bl + al * bh) + al * bl


def dd_add(x, y):
    s, e = two_sum(x[0], y[0])
    return quick_two_sum(s, e + (x[1] + y[1]))


def dd_neg(x):
    return -x[0], -x[1]


def dd_sub(x, y):
    return dd_add(x, dd_neg(y))


def dd_mul(x, y):
    p, e = two_prod(x[0], y[0])
    return quick_two_sum(p, e + (x[0] * y[1] + x[1] * y[0]))


def dd_div(x, y):
    q = x[0] / y[0]
    r = dd_sub(x, dd_mul(y, (q, jnp.zeros_like(q))))
    return quick_two_sum(q, r[0] / y[0])


def cg_weights(mu):
    one = (jnp.ones_like(mu[0][0]), jnp.zeros_like(mu[0][0]))
    inv = dd_div(one, mu[0])
    row = [dd_mul(m, inv) for m in mu[1:]]
    a = row[0]
    level = [dd_sub(row[k + 1], dd_mul(a, row[k])) for k in range(4)]
    first = [(jnp.zeros_like(a[0]), jnp.zeros_like(a[0]))] + level
    central = []
    for _ in range(4):
        first = [dd_sub(first[k + 1], dd_mul(a, first[k])) for k in range(len(first) - 1)]
        central.append(first[0])
    m2, m3, m4, m5 = central
    tiny = 1e-30
    m2s = (jnp.maximum(m2[0], tiny), jnp.where(m2[0] > tiny, m2[1], 0.0))
    b1 = dd_div(m3, m2s)
    m22 = dd_mul(m2, m2)
    h2 = dd_sub(dd_sub(m4, dd_mul(b1, m3)), m22)
    h2s = jnp.maximum(h2[0], tiny)
    inner = dd_sub(dd_mul(b1, m3), dd_add(m4, m4))
    inner = dd_add(inner, dd_add(m22, m22))
    top = dd_add(m5, dd_mul(b1, inner))
    m23 = dd_mul(m2, m3)
    top = dd_sub(top, dd_add(m23, m23))
    d0 = a[0] + SIGMA
    d1 = jnp.clip(d0 + b1[0], 0.25, 9.0)
    d2 = jnp.clip(d0 + top[0] / h2s, 0.25, 9.0)
    beta1 = jnp.maximum(m2[0], 0.0)
    beta2 = jnp.clip(h2[0] / m2s[0], 0.0, 25.0)
    bb1 = d1 - d0
    minor = d1 * d2 - beta2
    y2 = 1.0 / (d0 * minor - beta1 * d2)
    y1 = -d2 * y2
    y0 = minor * y2
    c2 = y2
    c1 = y1 - y2 * (2.0 * a[0] + bb1)
    c0 = y0 - a[0] * y1 + y2 * (a[0] * a[0] + a[0] * bb1 - m2[0])
    return c0, c1, c2


def tree(parts):
    while len(parts) > 1:
        parts = [a + b for a, b in zip(parts[::2], parts[1::2])]
    return parts[0]


def sigmoid4(v):
    return 1.0 / (1.0 + jnp.exp(-4.0 * v))


def crossing_weight(lower, upper):
    return lower * (1.0 - upper) + (1.0 - lower) * upper


def solve_kernel(rhs, scr, act, x_out, iso_out,
           R, S, M, U1, U2, MZ, SZ, MZ2, SZ2, MZ3, SZ3, TA, TB, TC, act_s, ar1, ar2,
                 lsem, ssem, rsem, asem, arsem, token):
    gx = lax.axis_index("gx")
    gy = lax.axis_index("gy")
    z = gx // 2
    core = lax.rem(gx, 2)

    def at_z(off):
        return lax.rem(z + off + NZ, NZ) * 2 + core

    loads = [
        pltpu.make_async_copy(act.at[0], act_s, lsem.at[0]),
        pltpu.make_async_copy(rhs, R.at[pl.ds(HR, 16), pl.ds(8, 32)], lsem.at[1]),
        pltpu.make_async_copy(scr, S.at[pl.ds(HS, 16), pl.ds(8, 32)], lsem.at[2]),
    ]
    for c in loads:
        c.start()

    bar = pltpu.get_barrier_semaphore()

    def tell(x, y):
        pl.semaphore_signal(bar, inc=1, device_id=(x, y), device_id_type=MESH)

    other_chip = lax.rem(gx + 2 * core - 1 + NGX, NGX)
    for dy in (1, -1):
        tell(other_chip, lax.rem(gy + dy + NGY, NGY))
    tell(other_chip, gy)
    for j in (1, 15, 10, 6, 9, 7, 11, 5, 8, 2, 14, 13, 3, 12, 4):
        for c in (1 - core, core):
            tell(2 * z + c, lax.rem(gy + j, NGY))
    tell(2 * z + 1 - core, gy)
    for off in (4, -4, 3, -3, 2, -2, 1, -1):
        tell(at_z(off), gy)
    has = []
    for dx, dy in NEIGHBOURS:
        ok = None
        for cond in ([gx < NGX - 1] if dx == 1 else []) + ([gx > 0] if dx == -1 else []) + (
            [gy < NGY - 1] if dy == 1 else []) + ([gy > 0] if dy == -1 else []):
            ok = cond if ok is None else jnp.logical_and(ok, cond)
        has.append(ok)
    @pl.when(gx == 0)
    def _():
        R[pl.ds(0, HR)] = jnp.zeros((HR, 48, 128), jnp.float32)
        S[pl.ds(0, HS)] = jnp.zeros((HS, 48, 128), jnp.float32)
        M[0] = jnp.zeros((4, 128), jnp.float32)

    @pl.when(gx == NGX - 1)
    def _():
        R[pl.ds(HR + 16, HR)] = jnp.zeros((HR, 48, 128), jnp.float32)
        S[pl.ds(HS + 16, HS)] = jnp.zeros((HS, 48, 128), jnp.float32)
        M[2] = jnp.zeros((4, 128), jnp.float32)

    def clear_rows(row, kind):
        R[:, pl.ds(row, 8)] = jnp.zeros((28, 8, 128), jnp.float32)
        S[:, pl.ds(row, 8)] = jnp.zeros((24, 8, 128), jnp.float32)
        M[:, pl.ds(kind, 1)] = jnp.zeros((3, 1, 128), jnp.float32)

    @pl.when(gy == 0)
    def _():
        clear_rows(0, 0)

    @pl.when(gy == NGY - 1)
    def _():
        clear_rows(40, 3)

    lane = lax.broadcasted_iota(jnp.int32, (8, 128), 1)
    loads[0].wait()
    entries = [act_s[0, q] for q in range(ACT)]
    count = jnp.int32(0)
    for e in entries:
        count = count + jnp.where(e >= 0, 1, 0)
    for w in range(2):
        number = lane // BLK + 8 * w
        own = jnp.zeros((8, 128), jnp.float32)
        for e in entries:
            own = jnp.where(number == e, 1.0, own)
        M[1, pl.ds(1 + w, 1)] = own[0:1]
    loads[1].wait()
    loads[2].wait()

    def mask_rows(dx, kinds):
        tiles = [jnp.broadcast_to(M[dx, pl.ds(k, 1)], (8, 128)) for k in range(4)]
        return jnp.concatenate([tiles[k] for k in kinds], axis=0)

    own = mask_rows(1, (1, 1, 2, 2))

    def prepare(p, carry):
        R[HR + p, pl.ds(8, 32)] = R[HR + p, pl.ds(8, 32)] * own
        S[HS + p, pl.ds(8, 32)] = S[HS + p, pl.ds(8, 32)] - SIGMA
        return carry

    lax.fori_loop(0, 16, prepare, 0, unroll=4)

    pl.semaphore_wait(bar, 42)
    for off in (4, -4):
        pl.semaphore_signal(token, inc=1, device_id=(at_z(off), gy), device_id_type=MESH)

    def pieces(i, which):
        dx, dy = NEIGHBOURS[i]
        out = []
        for n in which:
            if n == 2:
                first, size = {0: (1, 2), 1: (2, 1), -1: (1, 1)}[dy]
                src = M.at[1, pl.ds(first, size)]
                dst = M.at[1 - dx, pl.ds({0: 1, 1: 0, -1: 3}[dy], size)]
            else:
                ref, h = ((R, HR), (S, HS))[n]
                planes = {0: (h, h, 16), 1: (16, 0, h), -1: (h, h + 16, h)}[dx]
                rows = {0: (8, 8, 32), 1: (40 - h, 8 - h, h), -1: (8, 40, h)}[dy]
                src = ref.at[pl.ds(planes[0], planes[2]), pl.ds(rows[0], rows[2])]
                dst = ref.at[pl.ds(planes[1], planes[2]), pl.ds(rows[1], rows[2])]
            out.append(pltpu.make_async_remote_copy(
                src, dst, ssem.at[i, n], rsem.at[i, n],
                device_id=(gx + dx, gy + dy), device_id_type=MESH))
        return out

    opposite = [NEIGHBOURS.index((-dx, -dy)) for dx, dy in NEIGHBOURS]

    def receive(which, kinds=(0, 1, 2)):
        for i in range(8):
            dx, dy = NEIGHBOURS[i]
            if (2 if dx and dy else 0 if dx else 1) not in kinds:
                continue

            @pl.when(has[opposite[i]])
            def _():
                for c in pieces(i, which):
                    c.wait_recv()

    for which in ((0,), (2, 1)):
        for i, ok in enumerate(has):
            @pl.when(ok)
            def _():
                for c in pieces(i, which):
                    c.start()

    zero = jnp.zeros((8, 128), jnp.float32)
    sub = lax.broadcasted_iota(jnp.int32, (8, 128), 0)

    lanes = lax.broadcasted_iota(jnp.int32, (48, 128), 1)

    def z_stage(src, row, mz, sz, out_row, p, rows):
        v = src[p, pl.ds(row, rows)]
        at = lanes[0:rows]
        p1 = jnp.where(at < 1, 0.0, pltpu.roll(v, 1, 1)) + jnp.where(at > 126, 0.0, pltpu.roll(v, 127, 1))
        p2 = jnp.where(at < 2, 0.0, pltpu.roll(v, 2, 1)) + jnp.where(at > 125, 0.0, pltpu.roll(v, 126, 1))
        mz[p, pl.ds(out_row, rows)] = 66.0 * v + 26.0 * p1 + p2
        sz[p, pl.ds(out_row, rows)] = 6.0 * v - 2.0 * p1 - p2

    def x_stage(mz, sz, to, p, row, rows):
        def at(ref, off):
            return ref[p + off, pl.ds(row, rows)]

        s1 = at(sz, 1) + at(sz, 3)
        s2 = at(sz, 0) + at(sz, 4)
        m1 = at(mz, 1) + at(mz, 3)
        m2 = at(mz, 0) + at(mz, 4)
        m0 = at(mz, 2)
        one = (66.0 * at(sz, 2) + 26.0 * s1 + s2) + (6.0 * m0 - 2.0 * m1 - m2)
        two = 66.0 * m0 + 26.0 * m1 + m2
        to[0, p, pl.ds(row, rows)] = (66.0 * SCALE) * one + (6.0 * SCALE) * two
        to[1, p, pl.ds(row, rows)] = (26.0 * SCALE) * one - (2.0 * SCALE) * two
        to[2, p, pl.ds(row, rows)] = SCALE * (one - two)

    def y_stage(to, p, row, rows, m, scr_rows, src, src_row):
        def at(k, off):
            return to[k, p, pl.ds(row + off, rows)]

        k = at(0, 0) + ((at(1, -1) + at(1, 1)) + (at(2, -2) + at(2, 2)))
        centre = src[p + 2, pl.ds(src_row, rows)]
        return m * (k + scr_rows * centre), centre

    def total_of(acc, terms):
        return tuple(x + y for x, y in zip(acc, terms))

    def own_terms(value, centre, keep):
        terms = []
        for prod in (value * centre, value * value, value):
            t = [prod[8 * k:8 * k + 8] for k in range(len(keep))]
            t = [x if c is None else jnp.where(c, x, 0.0) for x, c in zip(t, keep)]
            while len(t) > 1:
                t = [x + y for x, y in zip(t[::2], t[1::2])] + t[len(t) - len(t) % 2:]
            terms.append(t[0])
        return terms

    def mask_from(dx, base):
        k = [jnp.broadcast_to(M[dx, pl.ds(j, 1)], (8, 128)) for j in range(4)]
        cut = sub >= -base
        return jnp.concatenate([jnp.where(cut, k[1], k[0]), k[1], jnp.where(cut, k[2], k[1]), k[2],
                                jnp.where(cut, k[3], k[2])], axis=0)

    mu0, sum0 = zero, zero
    for p in range(HR, HR + 16):
        z_stage(R, 8, MZ, SZ, 16, p, 32)
        v = R[p, pl.ds(8, 32)]
        w = v * v
        mu0 = mu0 + ((w[0:8] + w[8:16]) + (w[16:24] + w[24:32]))
        sum0 = sum0 + ((v[0:8] + v[8:16]) + (v[16:24] + v[24:32]))
    for p in range(6, 18):
        x_stage(MZ, SZ, TA, p, 16, 32)
    def middle1(dx):
        k = [jnp.broadcast_to(M[dx, pl.ds(j, 1)], (8, 128)) for j in (1, 2)]
        return jnp.concatenate([k[0], jnp.where(sub >= 4, k[1], k[0]), k[1]], axis=0)

    def middle2(dx):
        k = [jnp.broadcast_to(M[dx, pl.ds(j, 1)], (8, 128)) for j in (1, 2)]
        return jnp.concatenate([k[0], jnp.where(sub >= 2, k[1], k[0])], axis=0)

    def side(p, width):
        return 0 if p < width else 1 if p < width + 16 else 2

    def first_middle(p, m, acc):
        value, centre = y_stage(TA, p, 20, 24, m, S[p, pl.ds(12, 24)], R, 12)
        U1[p, pl.ds(8, 24)] = value
        return total_of(acc, own_terms(value, centre, [None] * 3)) if 4 <= p < 20 else acc

    acc = (zero, zero, zero)
    m = middle1(1)
    for p in range(6, 18):
        acc = first_middle(p, m, acc)

    halo = [p for p in range(28) if not HR <= p < HR + 16]
    outer = [p for p in range(24) if not 6 <= p < 18]
    receive((0,), (0,))
    for p in halo:
        z_stage(R, 8, MZ, SZ, 16, p, 32)
    for p in outer:
        x_stage(MZ, SZ, TA, p, 16, 32)
    receive((2, 1), (0,))
    m = [middle1(dx) for dx in range(3)]
    for p in outer:
        acc = first_middle(p, m[side(p, 4)], acc)
    for p in range(24):
        z_stage(U1, 8, MZ2, SZ2, 16, p, 24)
    for p in range(20):
        x_stage(MZ2, SZ2, TB, p, 16, 24)
    m = [middle2(dx) for dx in range(3)]
    acc2 = (zero, zero, zero)
    for p in range(20):
        value, centre = y_stage(TB, p, 18, 16, m[side(p, 2)], S[p + 2, pl.ds(14, 16)], U1, 10)
        U2[p, pl.ds(8, 16)] = value
        if 2 <= p < 18:
            acc2 = total_of(acc2, own_terms(value, centre, [None] * 2))
    for p in range(20):
        z_stage(U2, 8, MZ3, SZ3, 16, p, 16)
    for p in range(16):
        x_stage(MZ3, SZ3, TC, p, 16, 16)

    receive((0,), (1,))
    for p in range(HR, HR + 16):
        z_stage(R, 0, MZ, SZ, 8, p, 8)
        z_stage(R, 40, MZ, SZ, 48, p, 8)
    for p in range(6, 18):
        x_stage(MZ, SZ, TA, p, 8, 8)
        x_stage(MZ, SZ, TA, p, 48, 8)
    receive((0,), (2,))
    for p in halo:
        z_stage(R, 0, MZ, SZ, 8, p, 8)
        z_stage(R, 40, MZ, SZ, 48, p, 8)
    for p in outer:
        x_stage(MZ, SZ, TA, p, 8, 8)
        x_stage(MZ, SZ, TA, p, 48, 8)
    receive((2, 1), (1, 2))
    masks = [mask_from(dx, -4) for dx in range(3)]
    for p in range(24):
        m = masks[side(p, 4)]
        for row, first, keep in ((0, 4, sub >= 4), (32, 36, sub < 4)):
            value, centre = y_stage(TA, p, row + 12, 8, m[row:row + 8], S[p, pl.ds(first, 8)], R, first)
            U1[p, pl.ds(row, 8)] = value
            if 4 <= p < 20:
                acc = total_of(acc, own_terms(value, centre, [keep]))
    mu1, mu2, sum1 = acc

    for p in range(24):
        z_stage(U1, 0, MZ2, SZ2, 8, p, 8)
        z_stage(U1, 32, MZ2, SZ2, 40, p, 8)
    for p in range(20):
        x_stage(MZ2, SZ2, TB, p, 8, 8)
        x_stage(MZ2, SZ2, TB, p, 40, 8)
    masks = [mask_from(dx, -2) for dx in range(3)]
    for p in range(20):
        m = masks[side(p, 2)]
        for row, rows, keep in ((0, 8, [sub >= 2]), (24, 16, [None, sub < 2])):
            value, centre = y_stage(TB, p, row + 10, rows, m[row:row + rows],
                                    S[p + 2, pl.ds(row + 6, rows)], U1, row + 2)
            U2[p, pl.ds(row, rows)] = value
            if 2 <= p < 18:
                acc2 = total_of(acc2, own_terms(value, centre, keep))
    mu3, mu4, sum2 = acc2

    for p in range(20):
        z_stage(U2, 0, MZ3, SZ3, 8, p, 8)
        z_stage(U2, 24, MZ3, SZ3, 32, p, 16)
    for p in range(16):
        x_stage(MZ3, SZ3, TC, p, 8, 8)
        x_stage(MZ3, SZ3, TC, p, 32, 16)
    sub16 = lax.broadcasted_iota(jnp.int32, (16, 128), 0)
    lane16 = lax.broadcasted_iota(jnp.int32, (16, 128), 1)
    lane1 = lax.broadcasted_iota(jnp.int32, (1, 128), 1)
    rows = jnp.zeros((16, 128), jnp.float32)
    for k, acc in ((0, mu0), (1, mu1), (2, mu2), (3, mu3), (4, mu4), (6, sum0), (7, sum1), (8, sum2)):
        rows = jnp.where(sub16 == k, jnp.sum(acc, axis=0, keepdims=True), rows)
    total = jnp.sum(rows, axis=1, keepdims=True)
    spread = jnp.where(lane16 == sub16, total, 0.0)
    values = jnp.sum(spread, axis=0, keepdims=True)
    coarse = jnp.zeros((1, 128), jnp.float32)
    for k in range(6):
        coarse = jnp.where(lane1 == k, 1.5 * 2.0 ** (26 + k), coarse)
    mu5 = zero
    for p in range(16):
        value, centre = y_stage(TC, p, 10, 32, own, S[p + 4, pl.ds(8, 32)], U2, 2)
        w = value * centre
        mu5 = mu5 + ((w[0:8] + w[8:16]) + (w[16:24] + w[24:32]))

    last = jnp.sum(jnp.sum(mu5, axis=0, keepdims=True), axis=1, keepdims=True)
    values = jnp.where(lane1 == 5, last, values)
    rounded = (values + coarse) - coarse
    high = jnp.where(lane1 < 6, rounded, values)
    rest = jnp.where(lane1 < 6, values - rounded, 0.0)
    row = high + pltpu.roll(rest, 64, 1)
    row = jnp.where(lane1 == 9, count.astype(jnp.float32), row)

    pending = []
    mine = gy * 2 + core
    ar1[mine] = row
    for j in (10, 6, 9, 7, 11, 5, 8, 2, 14, 13, 3, 1, 15, 12, 4, 0):
        for c in (1 - core, core):
            if j == 0 and c is core:
                continue
            pltpu.make_async_remote_copy(
                ar1.at[mine], ar1.at[mine], asem.at[0], arsem.at[0],
                device_id=(2 * z + c, lax.rem(gy + j, NGY)), device_id_type=MESH).start()
    wait = pltpu.make_async_remote_copy(
        ar1.at[pl.ds(0, 31)], ar1.at[pl.ds(0, 31)], asem.at[0], arsem.at[0],
        device_id=(2 * z + 1 - core, gy), device_id_type=MESH)
    for i, ok in enumerate(has):
        @pl.when(ok)
        def _():
            for c in pieces(i, (0, 1, 2)):
                c.wait_send()
    wait.wait_recv()
    pending.append(wait)

    ar2[z] = tree([ar1[j] for j in range(32)])
    pl.semaphore_wait(token, 2)
    for off in (8, 7, -7, 6, -6, 5, -5, 4, -4, 3, -3, 2, -2, 1, -1):
        pltpu.make_async_remote_copy(
            ar2.at[z], ar2.at[z], asem.at[1], arsem.at[1],
            device_id=(at_z(off), gy), device_id_type=MESH).start()
    pending.pop().wait_send()
    wait = pltpu.make_async_remote_copy(
        ar2.at[pl.ds(0, 15)], ar2.at[pl.ds(0, 15)], asem.at[1], arsem.at[1],
        device_id=(at_z(1), gy), device_id_type=MESH)
    wait.wait_recv()
    pending.append(wait)
    row = tree([ar2[j] for j in range(16)])

    goal = jnp.where(sub16 < 10, sub16, sub16 + 54)
    picked = jnp.sum(jnp.where(lane16 == goal, row, 0.0), axis=1, keepdims=True)
    value = [jnp.broadcast_to(picked[k:k + 1], (8, 128)) for k in range(16)]
    mu = [two_sum(value[k], value[10 + k]) for k in range(6)]
    c0, c1, c2 = cg_weights(mu)
    iso = (c0 * value[6] + c1 * value[7] + c2 * value[8]) / (value[9] * float(BLK ** 3))

    def tile5(v):
        return jnp.concatenate([v] * 5, axis=0)

    iso_out[...] = iso
    c0, c1, c2 = tile5(c0), tile5(c1), tile5(c2)

    def solve(p, carry):
        x_out[p] = c0 * R[HR + p, pl.ds(8, 40)] + c1 * U1[4 + p, pl.ds(4, 40)] + c2 * U2[2 + p, pl.ds(2, 40)]
        return carry

    lax.fori_loop(0, 17, solve, 0, unroll=True)

    for c in pending:
        c.wait_send()


def crossing_kernel(x_ref, iso_ref, vis, ind_out, cross_out, G, W, BR, vis_s, sem):
    load = pltpu.make_async_copy(vis.at[0], vis_s, sem.at[0])
    load.start()
    store = pltpu.make_async_copy(x_ref.at[pl.ds(0, 16), pl.ds(0, 32)], ind_out, sem.at[1])
    store.start()
    lane = lax.broadcasted_iota(jnp.int32, (8, 128), 1)
    iso = jnp.concatenate([iso_ref[...]] * 5, axis=0)

    for p in range(17):
        G[p] = sigmoid4(x_ref[p] - iso)
    BR[pl.ds(16 * 96, 96)] = jnp.zeros((96, 128), jnp.float32)

    lane32 = lax.broadcasted_iota(jnp.int32, (32, 128), 1)
    edge = lane32 == 127
    empty = sigmoid4(0.0 - iso[0:32])
    group = lane // BLK
    odd = [(group // (1 << bit)) % 2 == 1 for bit in range(3)]
    load.wait()
    slots = []
    for q in range(VIS):
        n = vis_s[0, q]
        slots.append(jnp.where(n >= 0, n, 16) * 96)
    stores = [store]
    for e in range(3):
        for p in range(16):
            g = G[p, pl.ds(0, 32)]
            if e == 0:
                other = G[p + 1, pl.ds(0, 32)]
            elif e == 1:
                other = G[p, pl.ds(1, 32)]
            else:
                other = jnp.where(edge, empty, pltpu.roll(g, 127, 1))
            h = crossing_weight(g, other)
            for w in range(2):
                W[e, pl.ds((p // 4) * 128 + w * 64 + p % 4 * 16, 16)] = h[16 * w:16 * w + 16]
        for first in range(0, 8, 4):
            parts = range(first, first + 4)
            vs = {}
            for part in parts:
                vs[part] = [W[e, pl.ds(part * 64 + (-j) % 8, 8, stride=8)] for j in range(8)]
            for part in parts:
                vs[part] = [v if j == 0 else pltpu.roll(v, 16 * ((-j) % 8), 1) for j, v in enumerate(vs[part])]
            for bit in range(3):
                for part in parts:
                    old = vs[part]
                    vs[part] = [jnp.where(odd[bit], old[(t - (1 << bit)) % 8], old[t]) for t in range(8)]
            for part in parts:
                vs[part] = [v if t == 0 else pltpu.roll(v, 128 - 16 * t, 1) for t, v in enumerate(vs[part])]
            for part in parts:
                w, ib = part % 2, part // 2
                for t in range(8):
                    BR[pl.ds((w * 8 + t) * 96 + e * 32 + ib * 8, 8)] = vs[part][t]
        for q in range(VIS):
            start = pl.multiple_of(slots[q] + e * 32, 8)
            stores.append(pltpu.make_async_copy(
                BR.at[pl.ds(start, 32)], cross_out.at[pl.ds(q * 96 + e * 32, 32)], sem.at[2 + q * 3 + e]))
            stores[-1].start()
    for c in stores:
        c.wait()


def body(right_side, screening, active_blocks, visible_bricks):
    f32 = jnp.float32
    right_side, screening, active_blocks, visible_bricks = (
        pltpu.with_memory_space_constraint(v, pltpu.HBM)
        for v in (right_side, screening, active_blocks, visible_bricks))
    hbm = pl.BlockSpec(memory_space=pltpu.HBM)
    vmem = pl.BlockSpec(memory_space=pltpu.VMEM)
    x, iso = pl.pallas_call(
        solve_kernel,
        out_shape=(jax.ShapeDtypeStruct((17, 40, 128), f32), jax.ShapeDtypeStruct((8, 128), f32)),
        in_specs=[hbm] * 3,
        out_specs=(vmem, vmem),
        scratch_shapes=[
            pltpu.VMEM((28, 48, 128), f32),
            pltpu.VMEM((24, 48, 128), f32),
            pltpu.VMEM((3, 4, 128), f32),
            pltpu.VMEM((24, 48, 128), f32),
            pltpu.VMEM((20, 48, 128), f32),
            pltpu.VMEM((28, 64, 128), f32),
            pltpu.VMEM((28, 64, 128), f32),
            pltpu.VMEM((24, 56, 128), f32),
            pltpu.VMEM((24, 56, 128), f32),
            pltpu.VMEM((20, 56, 128), f32),
            pltpu.VMEM((20, 56, 128), f32),
            pltpu.VMEM((3, 24, 64, 128), f32),
            pltpu.VMEM((3, 20, 56, 128), f32),
            pltpu.VMEM((3, 16, 56, 128), f32),
            pltpu.SMEM((1, ACT), jnp.int32),
            pltpu.VMEM((32, 1, 128), f32),
            pltpu.VMEM((16, 1, 128), f32),
            pltpu.SemaphoreType.DMA((3,)),
            pltpu.SemaphoreType.DMA((8, 3)),
            pltpu.SemaphoreType.DMA((8, 3)),
            pltpu.SemaphoreType.DMA((2,)),
            pltpu.SemaphoreType.DMA((2,)),
            pltpu.SemaphoreType.REGULAR,
        ],
        compiler_params=pltpu.CompilerParams(
            collective_id=0, has_side_effects=True, vmem_limit_bytes=32 << 20),
    )(right_side, screening, active_blocks)
    indicator, crossing = pl.pallas_call(
        crossing_kernel,
        out_shape=(jax.ShapeDtypeStruct((16, 32, 128), f32), jax.ShapeDtypeStruct((VIS * 96, 128), f32)),
        in_specs=[vmem, vmem, hbm],
        out_specs=(hbm, hbm),
        scratch_shapes=[
            pltpu.VMEM((17, 40, 128), f32),
            pltpu.VMEM((3, 512, 128), f32),
            pltpu.VMEM((17 * 96, 128), f32),
            pltpu.SMEM((1, VIS), jnp.int32),
            pltpu.SemaphoreType.DMA((2 + 3 * VIS,)),
        ],
        compiler_params=pltpu.CompilerParams(vmem_limit_bytes=24 << 20),
    )(x, iso, visible_bricks)
    return indicator, crossing.reshape(VIS, 1, 3, BLK ** 3)


def solution(mesh):
    spec = P("gx", "gy", None)
    return jax.shard_map(
        body,
        mesh=mesh,
        in_specs=(spec, spec, spec, spec),
        out_specs=(spec, P("gx", "gy", None, None)),
        check_vma=False,
    )
```

```python
import jax
import jax.numpy as jnp
from jax import lax
from jax.experimental import pallas as pl
from jax.experimental.pallas import tpu as pltpu
from jax.sharding import PartitionSpec as P

MESH = pl.DeviceIdType.MESH
BLK = 16
ACT = 12
VIS = 8
NGX = 32
NGY = 16
NZ = 16
SIGMA = 2.5
HR = 6
HS = 4
SCALE = 1.0 / 86400.0
NEIGHBOURS = [(1, 1), (1, -1), (-1, 1), (-1, -1), (0, 1), (0, -1), (1, 0), (-1, 0)]


def two_sum(a, b):
    s = a + b
    t = s - a
    return s, (a - (s - t)) + (b - t)


def quick_two_sum(a, b):
    s = a + b
    return s, b - (s - a)


def split(a):
    c = 4097.0 * a
    hi = c - (c - a)
    return hi, a - hi


def two_prod(a, b):
    p = a * b
    ah, al = split(a)
    bh, bl = split(b)
    return p, ((ah * bh - p) + ah * bl + al * bh) + al * bl


def dd_add(x, y):
    s, e = two_sum(x[0], y[0])
    return quick_two_sum(s, e + (x[1] + y[1]))


def dd_neg(x):
    return -x[0], -x[1]


def dd_sub(x, y):
    return dd_add(x, dd_neg(y))


def dd_mul(x, y):
    p, e = two_prod(x[0], y[0])
    return quick_two_sum(p, e + (x[0] * y[1] + x[1] * y[0]))


def dd_div(x, y):
    q = x[0] / y[0]
    r = dd_sub(x, dd_mul(y, (q, jnp.zeros_like(q))))
    return quick_two_sum(q, r[0] / y[0])


def cg_weights(mu):
    one = (jnp.ones_like(mu[0][0]), jnp.zeros_like(mu[0][0]))
    inv = dd_div(one, mu[0])
    row = [dd_mul(m, inv) for m in mu[1:]]
    a = row[0]
    level = [dd_sub(row[k + 1], dd_mul(a, row[k])) for k in range(4)]
    first = [(jnp.zeros_like(a[0]), jnp.zeros_like(a[0]))] + level
    central = []
    for _ in range(4):
        first = [dd_sub(first[k + 1], dd_mul(a, first[k])) for k in range(len(first) - 1)]
        central.append(first[0])
    m2, m3, m4, m5 = central
    tiny = 1e-30
    m2s = (jnp.maximum(m2[0], tiny), jnp.where(m2[0] > tiny, m2[1], 0.0))
    b1 = dd_div(m3, m2s)
    m22 = dd_mul(m2, m2)
    h2 = dd_sub(dd_sub(m4, dd_mul(b1, m3)), m22)
    h2s = jnp.maximum(h2[0], tiny)
    inner = dd_sub(dd_mul(b1, m3), dd_add(m4, m4))
    inner = dd_add(inner, dd_add(m22, m22))
    top = dd_add(m5, dd_mul(b1, inner))
    m23 = dd_mul(m2, m3)
    top = dd_sub(top, dd_add(m23, m23))
    d0 = a[0] + SIGMA
    d1 = jnp.clip(d0 + b1[0], 0.25, 9.0)
    d2 = jnp.clip(d0 + top[0] / h2s, 0.25, 9.0)
    beta1 = jnp.maximum(m2[0], 0.0)
    beta2 = jnp.clip(h2[0] / m2s[0], 0.0, 25.0)
    bb1 = d1 - d0
    minor = d1 * d2 - beta2
    y2 = 1.0 / (d0 * minor - beta1 * d2)
    y1 = -d2 * y2
    y0 = minor * y2
    c2 = y2
    c1 = y1 - y2 * (2.0 * a[0] + bb1)
    c0 = y0 - a[0] * y1 + y2 * (a[0] * a[0] + a[0] * bb1 - m2[0])
    return c0, c1, c2


def tree(parts):
    while len(parts) > 1:
        parts = [a + b for a, b in zip(parts[::2], parts[1::2])]
    return parts[0]


def sigmoid4(v):
    return 1.0 / (1.0 + jnp.exp(-4.0 * v))


def crossing_weight(lower, upper):
    return lower * (1.0 - upper) + (1.0 - lower) * upper


def solve_kernel(rhs, scr, act, x_out, iso_out,
           R, S, M, U1, U2, MZ, SZ, MZ2, SZ2, MZ3, SZ3, TA, TB, TC, act_s, ar1, ar2,
                 lsem, ssem, rsem, asem, arsem, token):
    gx = lax.axis_index("gx")
    gy = lax.axis_index("gy")
    z = gx // 2
    core = lax.rem(gx, 2)

    def at_z(off):
        return lax.rem(z + off + NZ, NZ) * 2 + core

    loads = [
        pltpu.make_async_copy(act.at[0], act_s, lsem.at[0]),
        pltpu.make_async_copy(rhs, R.at[pl.ds(HR, 16), pl.ds(8, 32)], lsem.at[1]),
        pltpu.make_async_copy(scr, S.at[pl.ds(HS, 16), pl.ds(8, 32)], lsem.at[2]),
    ]
    for c in loads:
        c.start()

    bar = pltpu.get_barrier_semaphore()

    def tell(x, y):
        pl.semaphore_signal(bar, inc=1, device_id=(x, y), device_id_type=MESH)

    def along_x(off):
        return lax.rem(gx + off + NGX, NGX)

    def along_y(off):
        return lax.rem(gy + off + NGY, NGY)

    for dx, dy in NEIGHBOURS:
        tell(along_x(dx), along_y(dy))
    has = []
    for dx, dy in NEIGHBOURS:
        ok = None
        for cond in ([gx < NGX - 1] if dx == 1 else []) + ([gx > 0] if dx == -1 else []) + (
            [gy < NGY - 1] if dy == 1 else []) + ([gy > 0] if dy == -1 else []):
            ok = cond if ok is None else jnp.logical_and(ok, cond)
        has.append(ok)
    @pl.when(gx == 0)
    def _():
        R[pl.ds(0, HR)] = jnp.zeros((HR, 48, 128), jnp.float32)
        S[pl.ds(0, HS)] = jnp.zeros((HS, 48, 128), jnp.float32)
        M[0] = jnp.zeros((4, 128), jnp.float32)

    @pl.when(gx == NGX - 1)
    def _():
        R[pl.ds(HR + 16, HR)] = jnp.zeros((HR, 48, 128), jnp.float32)
        S[pl.ds(HS + 16, HS)] = jnp.zeros((HS, 48, 128), jnp.float32)
        M[2] = jnp.zeros((4, 128), jnp.float32)

    def clear_rows(row, kind):
        R[:, pl.ds(row, 8)] = jnp.zeros((28, 8, 128), jnp.float32)
        S[:, pl.ds(row, 8)] = jnp.zeros((24, 8, 128), jnp.float32)
        M[:, pl.ds(kind, 1)] = jnp.zeros((3, 1, 128), jnp.float32)

    @pl.when(gy == 0)
    def _():
        clear_rows(0, 0)

    @pl.when(gy == NGY - 1)
    def _():
        clear_rows(40, 3)

    lane = lax.broadcasted_iota(jnp.int32, (8, 128), 1)
    loads[0].wait()
    entries = [act_s[0, q] for q in range(ACT)]
    count = jnp.int32(0)
    for e in entries:
        count = count + jnp.where(e >= 0, 1, 0)
    for w in range(2):
        number = lane // BLK + 8 * w
        own = jnp.zeros((8, 128), jnp.float32)
        for e in entries:
            own = jnp.where(number == e, 1.0, own)
        M[1, pl.ds(1 + w, 1)] = own[0:1]
    loads[1].wait()
    loads[2].wait()

    def mask_rows(dx, kinds):
        tiles = [jnp.broadcast_to(M[dx, pl.ds(k, 1)], (8, 128)) for k in range(4)]
        return jnp.concatenate([tiles[k] for k in kinds], axis=0)

    own = mask_rows(1, (1, 1, 2, 2))

    def prepare(p, carry):
        R[HR + p, pl.ds(8, 32)] = R[HR + p, pl.ds(8, 32)] * own
        S[HS + p, pl.ds(8, 32)] = S[HS + p, pl.ds(8, 32)] - SIGMA
        return carry

    lax.fori_loop(0, 16, prepare, 0, unroll=4)

    pl.semaphore_wait(bar, 8)

    def vouch(k):
        for off in (1 << k, -(1 << k)):
            pl.semaphore_signal(token.at[k], inc=1, device_id=(along_x(off), gy), device_id_type=MESH)
            if k < 3:
                pl.semaphore_signal(token.at[k], inc=1, device_id=(gx, along_y(off)), device_id_type=MESH)

    vouch(0)

    def pieces(i, which):
        dx, dy = NEIGHBOURS[i]
        out = []
        for n in which:
            if n == 2:
                first, size = {0: (1, 2), 1: (2, 1), -1: (1, 1)}[dy]
                src = M.at[1, pl.ds(first, size)]
                dst = M.at[1 - dx, pl.ds({0: 1, 1: 0, -1: 3}[dy], size)]
            else:
                ref, h = ((R, HR), (S, HS))[n]
                planes = {0: (h, h, 16), 1: (16, 0, h), -1: (h, h + 16, h)}[dx]
                rows = {0: (8, 8, 32), 1: (40 - h, 8 - h, h), -1: (8, 40, h)}[dy]
                src = ref.at[pl.ds(planes[0], planes[2]), pl.ds(rows[0], rows[2])]
                dst = ref.at[pl.ds(planes[1], planes[2]), pl.ds(rows[1], rows[2])]
            out.append(pltpu.make_async_remote_copy(
                src, dst, ssem.at[i, n], rsem.at[i, n],
                device_id=(gx + dx, gy + dy), device_id_type=MESH))
        return out

    opposite = [NEIGHBOURS.index((-dx, -dy)) for dx, dy in NEIGHBOURS]

    def receive(which, kinds=(0, 1, 2)):
        for i in range(8):
            dx, dy = NEIGHBOURS[i]
            if (2 if dx and dy else 0 if dx else 1) not in kinds:
                continue

            @pl.when(has[opposite[i]])
            def _():
                for c in pieces(i, which):
                    c.wait_recv()

    for which in ((0,), (2, 1)):
        for i, ok in enumerate(has):
            @pl.when(ok)
            def _():
                for c in pieces(i, which):
                    c.start()

    zero = jnp.zeros((8, 128), jnp.float32)
    sub = lax.broadcasted_iota(jnp.int32, (8, 128), 0)

    lanes = lax.broadcasted_iota(jnp.int32, (48, 128), 1)

    def z_stage(src, row, mz, sz, out_row, p, rows):
        v = src[p, pl.ds(row, rows)]
        at = lanes[0:rows]
        p1 = jnp.where(at < 1, 0.0, pltpu.roll(v, 1, 1)) + jnp.where(at > 126, 0.0, pltpu.roll(v, 127, 1))
        p2 = jnp.where(at < 2, 0.0, pltpu.roll(v, 2, 1)) + jnp.where(at > 125, 0.0, pltpu.roll(v, 126, 1))
        mz[p, pl.ds(out_row, rows)] = 66.0 * v + 26.0 * p1 + p2
        sz[p, pl.ds(out_row, rows)] = 6.0 * v - 2.0 * p1 - p2

    def x_stage(mz, sz, to, p, row, rows):
        def at(ref, off):
            return ref[p + off, pl.ds(row, rows)]

        s1 = at(sz, 1) + at(sz, 3)
        s2 = at(sz, 0) + at(sz, 4)
        m1 = at(mz, 1) + at(mz, 3)
        m2 = at(mz, 0) + at(mz, 4)
        m0 = at(mz, 2)
        one = (66.0 * at(sz, 2) + 26.0 * s1 + s2) + (6.0 * m0 - 2.0 * m1 - m2)
        two = 66.0 * m0 + 26.0 * m1 + m2
        to[0, p, pl.ds(row, rows)] = (66.0 * SCALE) * one + (6.0 * SCALE) * two
        to[1, p, pl.ds(row, rows)] = (26.0 * SCALE) * one - (2.0 * SCALE) * two
        to[2, p, pl.ds(row, rows)] = SCALE * (one - two)

    def y_stage(to, p, row, rows, m, scr_rows, src, src_row):
        def at(k, off):
            return to[k, p, pl.ds(row + off, rows)]

        k = at(0, 0) + ((at(1, -1) + at(1, 1)) + (at(2, -2) + at(2, 2)))
        centre = src[p + 2, pl.ds(src_row, rows)]
        return m * (k + scr_rows * centre), centre

    def total_of(acc, terms):
        return tuple(x + y for x, y in zip(acc, terms))

    def own_terms(value, centre, keep):
        terms = []
        for prod in (value * centre, value * value, value):
            t = [prod[8 * k:8 * k + 8] for k in range(len(keep))]
            t = [x if c is None else jnp.where(c, x, 0.0) for x, c in zip(t, keep)]
            while len(t) > 1:
                t = [x + y for x, y in zip(t[::2], t[1::2])] + t[len(t) - len(t) % 2:]
            terms.append(t[0])
        return terms

    def mask_from(dx, base):
        k = [jnp.broadcast_to(M[dx, pl.ds(j, 1)], (8, 128)) for j in range(4)]
        cut = sub >= -base
        return jnp.concatenate([jnp.where(cut, k[1], k[0]), k[1], jnp.where(cut, k[2], k[1]), k[2],
                                jnp.where(cut, k[3], k[2])], axis=0)

    mu0, sum0 = zero, zero
    for p in range(HR, HR + 16):
        z_stage(R, 8, MZ, SZ, 16, p, 32)
        v = R[p, pl.ds(8, 32)]
        w = v * v
        mu0 = mu0 + ((w[0:8] + w[8:16]) + (w[16:24] + w[24:32]))
        sum0 = sum0 + ((v[0:8] + v[8:16]) + (v[16:24] + v[24:32]))
    for p in range(6, 18):
        x_stage(MZ, SZ, TA, p, 16, 32)
    def middle1(dx):
        k = [jnp.broadcast_to(M[dx, pl.ds(j, 1)], (8, 128)) for j in (1, 2)]
        return jnp.concatenate([k[0], jnp.where(sub >= 4, k[1], k[0]), k[1]], axis=0)

    def middle2(dx):
        k = [jnp.broadcast_to(M[dx, pl.ds(j, 1)], (8, 128)) for j in (1, 2)]
        return jnp.concatenate([k[0], jnp.where(sub >= 2, k[1], k[0])], axis=0)

    def side(p, width):
        return 0 if p < width else 1 if p < width + 16 else 2

    def first_middle(p, m, acc):
        value, centre = y_stage(TA, p, 20, 24, m, S[p, pl.ds(12, 24)], R, 12)
        U1[p, pl.ds(8, 24)] = value
        return total_of(acc, own_terms(value, centre, [None] * 3)) if 4 <= p < 20 else acc

    acc = (zero, zero, zero)
    m = middle1(1)
    for p in range(6, 18):
        acc = first_middle(p, m, acc)

    halo = [p for p in range(28) if not HR <= p < HR + 16]
    outer = [p for p in range(24) if not 6 <= p < 18]
    receive((0,), (0,))
    for p in halo:
        z_stage(R, 8, MZ, SZ, 16, p, 32)
    for p in outer:
        x_stage(MZ, SZ, TA, p, 16, 32)
    receive((2, 1), (0,))
    pl.semaphore_wait(token.at[0], 4)
    vouch(1)
    m = [middle1(dx) for dx in range(3)]
    for p in outer:
        acc = first_middle(p, m[side(p, 4)], acc)
    for p in range(24):
        z_stage(U1, 8, MZ2, SZ2, 16, p, 24)
    for p in range(20):
        x_stage(MZ2, SZ2, TB, p, 16, 24)
    m = [middle2(dx) for dx in range(3)]
    acc2 = (zero, zero, zero)
    for p in range(20):
        value, centre = y_stage(TB, p, 18, 16, m[side(p, 2)], S[p + 2, pl.ds(14, 16)], U1, 10)
        U2[p, pl.ds(8, 16)] = value
        if 2 <= p < 18:
            acc2 = total_of(acc2, own_terms(value, centre, [None] * 2))
    for p in range(20):
        z_stage(U2, 8, MZ3, SZ3, 16, p, 16)
    for p in range(16):
        x_stage(MZ3, SZ3, TC, p, 16, 16)

    pl.semaphore_wait(token.at[1], 4)
    vouch(2)
    receive((0,), (1,))
    for p in range(HR, HR + 16):
        z_stage(R, 0, MZ, SZ, 8, p, 8)
        z_stage(R, 40, MZ, SZ, 48, p, 8)
    for p in range(6, 18):
        x_stage(MZ, SZ, TA, p, 8, 8)
        x_stage(MZ, SZ, TA, p, 48, 8)
    receive((0,), (2,))
    for p in halo:
        z_stage(R, 0, MZ, SZ, 8, p, 8)
        z_stage(R, 40, MZ, SZ, 48, p, 8)
    for p in outer:
        x_stage(MZ, SZ, TA, p, 8, 8)
        x_stage(MZ, SZ, TA, p, 48, 8)
    receive((2, 1), (1, 2))
    masks = [mask_from(dx, -4) for dx in range(3)]
    for p in range(24):
        m = masks[side(p, 4)]
        for row, first, keep in ((0, 4, sub >= 4), (32, 36, sub < 4)):
            value, centre = y_stage(TA, p, row + 12, 8, m[row:row + 8], S[p, pl.ds(first, 8)], R, first)
            U1[p, pl.ds(row, 8)] = value
            if 4 <= p < 20:
                acc = total_of(acc, own_terms(value, centre, [keep]))
    mu1, mu2, sum1 = acc

    for p in range(24):
        z_stage(U1, 0, MZ2, SZ2, 8, p, 8)
        z_stage(U1, 32, MZ2, SZ2, 40, p, 8)
    for p in range(20):
        x_stage(MZ2, SZ2, TB, p, 8, 8)
        x_stage(MZ2, SZ2, TB, p, 40, 8)
    masks = [mask_from(dx, -2) for dx in range(3)]
    for p in range(20):
        m = masks[side(p, 2)]
        for row, rows, keep in ((0, 8, [sub >= 2]), (24, 16, [None, sub < 2])):
            value, centre = y_stage(TB, p, row + 10, rows, m[row:row + rows],
                                    S[p + 2, pl.ds(row + 6, rows)], U1, row + 2)
            U2[p, pl.ds(row, rows)] = value
            if 2 <= p < 18:
                acc2 = total_of(acc2, own_terms(value, centre, keep))
    mu3, mu4, sum2 = acc2

    for p in range(20):
        z_stage(U2, 0, MZ3, SZ3, 8, p, 8)
        z_stage(U2, 24, MZ3, SZ3, 32, p, 16)
    for p in range(16):
        x_stage(MZ3, SZ3, TC, p, 8, 8)
        x_stage(MZ3, SZ3, TC, p, 32, 16)
    sub16 = lax.broadcasted_iota(jnp.int32, (16, 128), 0)
    lane16 = lax.broadcasted_iota(jnp.int32, (16, 128), 1)
    lane1 = lax.broadcasted_iota(jnp.int32, (1, 128), 1)
    rows = jnp.zeros((16, 128), jnp.float32)
    for k, acc in ((0, mu0), (1, mu1), (2, mu2), (3, mu3), (4, mu4), (6, sum0), (7, sum1), (8, sum2)):
        rows = jnp.where(sub16 == k, jnp.sum(acc, axis=0, keepdims=True), rows)
    total = jnp.sum(rows, axis=1, keepdims=True)
    spread = jnp.where(lane16 == sub16, total, 0.0)
    values = jnp.sum(spread, axis=0, keepdims=True)
    coarse = jnp.zeros((1, 128), jnp.float32)
    for k in range(6):
        coarse = jnp.where(lane1 == k, 1.5 * 2.0 ** (26 + k), coarse)
    mu5 = zero
    for p in range(16):
        value, centre = y_stage(TC, p, 10, 32, own, S[p + 4, pl.ds(8, 32)], U2, 2)
        w = value * centre
        mu5 = mu5 + ((w[0:8] + w[8:16]) + (w[16:24] + w[24:32]))

    last = jnp.sum(jnp.sum(mu5, axis=0, keepdims=True), axis=1, keepdims=True)
    values = jnp.where(lane1 == 5, last, values)
    rounded = (values + coarse) - coarse
    high = jnp.where(lane1 < 6, rounded, values)
    rest = jnp.where(lane1 < 6, values - rounded, 0.0)
    row = high + pltpu.roll(rest, 64, 1)
    row = jnp.where(lane1 == 9, count.astype(jnp.float32), row)

    pending = []
    mine = gy * 2 + core
    pl.semaphore_wait(token.at[2], 4)
    ar1[mine] = row
    for j in (10, 6, 9, 7, 11, 5, 8, 2, 14, 13, 3, 1, 15, 12, 4, 0):
        for c in (1 - core, core):
            if j == 0 and c is core:
                continue
            pltpu.make_async_remote_copy(
                ar1.at[mine], ar1.at[mine], asem.at[0], arsem.at[0],
                device_id=(2 * z + c, lax.rem(gy + j, NGY)), device_id_type=MESH).start()
    wait = pltpu.make_async_remote_copy(
        ar1.at[pl.ds(0, 31)], ar1.at[pl.ds(0, 31)], asem.at[0], arsem.at[0],
        device_id=(2 * z + 1 - core, gy), device_id_type=MESH)
    vouch(3)
    for i, ok in enumerate(has):
        @pl.when(ok)
        def _():
            for c in pieces(i, (0, 1, 2)):
                c.wait_send()
    wait.wait_recv()
    pending.append(wait)

    ar2[z] = tree([ar1[j] for j in range(32)])
    pl.semaphore_wait(token.at[3], 2)
    for off in (8, 7, -7, 6, -6, 5, -5, 4, -4, 3, -3, 2, -2, 1, -1):
        pltpu.make_async_remote_copy(
            ar2.at[z], ar2.at[z], asem.at[1], arsem.at[1],
            device_id=(at_z(off), gy), device_id_type=MESH).start()
    pending.pop().wait_send()
    wait = pltpu.make_async_remote_copy(
        ar2.at[pl.ds(0, 15)], ar2.at[pl.ds(0, 15)], asem.at[1], arsem.at[1],
        device_id=(at_z(1), gy), device_id_type=MESH)
    wait.wait_recv()
    pending.append(wait)
    row = tree([ar2[j] for j in range(16)])

    goal = jnp.where(sub16 < 10, sub16, sub16 + 54)
    picked = jnp.sum(jnp.where(lane16 == goal, row, 0.0), axis=1, keepdims=True)
    value = [jnp.broadcast_to(picked[k:k + 1], (8, 128)) for k in range(16)]
    mu = [two_sum(value[k], value[10 + k]) for k in range(6)]
    c0, c1, c2 = cg_weights(mu)
    iso = (c0 * value[6] + c1 * value[7] + c2 * value[8]) / (value[9] * float(BLK ** 3))

    def tile5(v):
        return jnp.concatenate([v] * 5, axis=0)

    iso_out[...] = iso
    c0, c1, c2 = tile5(c0), tile5(c1), tile5(c2)

    def solve(p, carry):
        x_out[p] = c0 * R[HR + p, pl.ds(8, 40)] + c1 * U1[4 + p, pl.ds(4, 40)] + c2 * U2[2 + p, pl.ds(2, 40)]
        return carry

    lax.fori_loop(0, 17, solve, 0, unroll=True)

    for c in pending:
        c.wait_send()


def crossing_kernel(x_ref, iso_ref, vis, ind_out, cross_out, G, W, BR, vis_s, sem):
    load = pltpu.make_async_copy(vis.at[0], vis_s, sem.at[0])
    load.start()
    store = pltpu.make_async_copy(x_ref.at[pl.ds(0, 16), pl.ds(0, 32)], ind_out, sem.at[1])
    store.start()
    lane = lax.broadcasted_iota(jnp.int32, (8, 128), 1)
    iso = jnp.concatenate([iso_ref[...]] * 5, axis=0)

    for p in range(17):
        G[p] = sigmoid4(x_ref[p] - iso)
    BR[pl.ds(16 * 96, 96)] = jnp.zeros((96, 128), jnp.float32)

    lane32 = lax.broadcasted_iota(jnp.int32, (32, 128), 1)
    edge = lane32 == 127
    empty = sigmoid4(0.0 - iso[0:32])
    group = lane // BLK
    odd = [(group // (1 << bit)) % 2 == 1 for bit in range(3)]
    load.wait()
    slots = []
    for q in range(VIS):
        n = vis_s[0, q]
        slots.append(jnp.where(n >= 0, n, 16) * 96)
    stores = [store]
    for e in range(3):
        for p in range(16):
            g = G[p, pl.ds(0, 32)]
            if e == 0:
                other = G[p + 1, pl.ds(0, 32)]
            elif e == 1:
                other = G[p, pl.ds(1, 32)]
            else:
                other = jnp.where(edge, empty, pltpu.roll(g, 127, 1))
            h = crossing_weight(g, other)
            for w in range(2):
                W[e, pl.ds((p // 4) * 128 + w * 64 + p % 4 * 16, 16)] = h[16 * w:16 * w + 16]
        for first in range(0, 8, 4):
            parts = range(first, first + 4)
            vs = {}
            for part in parts:
                vs[part] = [W[e, pl.ds(part * 64 + (-j) % 8, 8, stride=8)] for j in range(8)]
            for part in parts:
                vs[part] = [v if j == 0 else pltpu.roll(v, 16 * ((-j) % 8), 1) for j, v in enumerate(vs[part])]
            for bit in range(3):
                for part in parts:
                    old = vs[part]
                    vs[part] = [jnp.where(odd[bit], old[(t - (1 << bit)) % 8], old[t]) for t in range(8)]
            for part in parts:
                vs[part] = [v if t == 0 else pltpu.roll(v, 128 - 16 * t, 1) for t, v in enumerate(vs[part])]
            for part in parts:
                w, ib = part % 2, part // 2
                for t in range(8):
                    BR[pl.ds((w * 8 + t) * 96 + e * 32 + ib * 8, 8)] = vs[part][t]
        for q in range(VIS):
            start = pl.multiple_of(slots[q] + e * 32, 8)
            stores.append(pltpu.make_async_copy(
                BR.at[pl.ds(start, 32)], cross_out.at[pl.ds(q * 96 + e * 32, 32)], sem.at[2 + q * 3 + e]))
            stores[-1].start()
    for c in stores:
        c.wait()


def body(right_side, screening, active_blocks, visible_bricks):
    f32 = jnp.float32
    right_side, screening, active_blocks, visible_bricks = (
        pltpu.with_memory_space_constraint(v, pltpu.HBM)
        for v in (right_side, screening, active_blocks, visible_bricks))
    hbm = pl.BlockSpec(memory_space=pltpu.HBM)
    vmem = pl.BlockSpec(memory_space=pltpu.VMEM)
    x, iso = pl.pallas_call(
        solve_kernel,
        out_shape=(jax.ShapeDtypeStruct((17, 40, 128), f32), jax.ShapeDtypeStruct((8, 128), f32)),
        in_specs=[hbm] * 3,
        out_specs=(vmem, vmem),
        scratch_shapes=[
            pltpu.VMEM((28, 48, 128), f32),
            pltpu.VMEM((24, 48, 128), f32),
            pltpu.VMEM((3, 4, 128), f32),
            pltpu.VMEM((24, 48, 128), f32),
            pltpu.VMEM((20, 48, 128), f32),
            pltpu.VMEM((28, 64, 128), f32),
            pltpu.VMEM((28, 64, 128), f32),
            pltpu.VMEM((24, 56, 128), f32),
            pltpu.VMEM((24, 56, 128), f32),
            pltpu.VMEM((20, 56, 128), f32),
            pltpu.VMEM((20, 56, 128), f32),
            pltpu.VMEM((3, 24, 64, 128), f32),
            pltpu.VMEM((3, 20, 56, 128), f32),
            pltpu.VMEM((3, 16, 56, 128), f32),
            pltpu.SMEM((1, ACT), jnp.int32),
            pltpu.VMEM((32, 1, 128), f32),
            pltpu.VMEM((16, 1, 128), f32),
            pltpu.SemaphoreType.DMA((3,)),
            pltpu.SemaphoreType.DMA((8, 3)),
            pltpu.SemaphoreType.DMA((8, 3)),
            pltpu.SemaphoreType.DMA((2,)),
            pltpu.SemaphoreType.DMA((2,)),
            pltpu.SemaphoreType.REGULAR((4,)),
        ],
        compiler_params=pltpu.CompilerParams(
            collective_id=0, has_side_effects=True, vmem_limit_bytes=32 << 20),
    )(right_side, screening, active_blocks)
    indicator, crossing = pl.pallas_call(
        crossing_kernel,
        out_shape=(jax.ShapeDtypeStruct((16, 32, 128), f32), jax.ShapeDtypeStruct((VIS * 96, 128), f32)),
        in_specs=[vmem, vmem, hbm],
        out_specs=(hbm, hbm),
        scratch_shapes=[
            pltpu.VMEM((17, 40, 128), f32),
            pltpu.VMEM((3, 512, 128), f32),
            pltpu.VMEM((17 * 96, 128), f32),
            pltpu.SMEM((1, VIS), jnp.int32),
            pltpu.SemaphoreType.DMA((2 + 3 * VIS,)),
        ],
        compiler_params=pltpu.CompilerParams(vmem_limit_bytes=24 << 20),
    )(x, iso, visible_bricks)
    return indicator, crossing.reshape(VIS, 1, 3, BLK ** 3)


def solution(mesh):
    spec = P("gx", "gy", None)
    return jax.shard_map(
        body,
        mesh=mesh,
        in_specs=(spec, spec, spec, spec),
        out_specs=(spec, P("gx", "gy", None, None)),
        check_vma=False,
    )
```

```python
import jax
import jax.numpy as jnp
from jax import lax
from jax.experimental import pallas as pl
from jax.experimental.pallas import tpu as pltpu
from jax.sharding import PartitionSpec as P

MESH = pl.DeviceIdType.MESH
BLK = 16
ACT = 12
VIS = 8
NGX = 32
NGY = 16
NZ = 16
SIGMA = 2.5
HR = 6
HS = 4
SCALE = 1.0 / 86400.0
NEIGHBOURS = [(1, 1), (1, -1), (-1, 1), (-1, -1), (0, 1), (0, -1), (1, 0), (-1, 0)]


def two_sum(a, b):
    s = a + b
    t = s - a
    return s, (a - (s - t)) + (b - t)


def quick_two_sum(a, b):
    s = a + b
    return s, b - (s - a)


def split(a):
    c = 4097.0 * a
    hi = c - (c - a)
    return hi, a - hi


def two_prod(a, b):
    p = a * b
    ah, al = split(a)
    bh, bl = split(b)
    return p, ((ah * bh - p) + ah * bl + al * bh) + al * bl


def dd_add(x, y):
    s, e = two_sum(x[0], y[0])
    return quick_two_sum(s, e + (x[1] + y[1]))


def dd_neg(x):
    return -x[0], -x[1]


def dd_sub(x, y):
    return dd_add(x, dd_neg(y))


def dd_mul(x, y):
    p, e = two_prod(x[0], y[0])
    return quick_two_sum(p, e + (x[0] * y[1] + x[1] * y[0]))


def dd_div(x, y):
    q = x[0] / y[0]
    r = dd_sub(x, dd_mul(y, (q, jnp.zeros_like(q))))
    return quick_two_sum(q, r[0] / y[0])


def cg_weights(mu):
    one = (jnp.ones_like(mu[0][0]), jnp.zeros_like(mu[0][0]))
    inv = dd_div(one, mu[0])
    row = [dd_mul(m, inv) for m in mu[1:]]
    a = row[0]
    level = [dd_sub(row[k + 1], dd_mul(a, row[k])) for k in range(4)]
    first = [(jnp.zeros_like(a[0]), jnp.zeros_like(a[0]))] + level
    central = []
    for _ in range(4):
        first = [dd_sub(first[k + 1], dd_mul(a, first[k])) for k in range(len(first) - 1)]
        central.append(first[0])
    m2, m3, m4, m5 = central
    tiny = 1e-30
    m2s = (jnp.maximum(m2[0], tiny), jnp.where(m2[0] > tiny, m2[1], 0.0))
    b1 = dd_div(m3, m2s)
    m22 = dd_mul(m2, m2)
    h2 = dd_sub(dd_sub(m4, dd_mul(b1, m3)), m22)
    h2s = jnp.maximum(h2[0], tiny)
    inner = dd_sub(dd_mul(b1, m3), dd_add(m4, m4))
    inner = dd_add(inner, dd_add(m22, m22))
    top = dd_add(m5, dd_mul(b1, inner))
    m23 = dd_mul(m2, m3)
    top = dd_sub(top, dd_add(m23, m23))
    d0 = a[0] + SIGMA
    d1 = jnp.clip(d0 + b1[0], 0.25, 9.0)
    d2 = jnp.clip(d0 + top[0] / h2s, 0.25, 9.0)
    beta1 = jnp.maximum(m2[0], 0.0)
    beta2 = jnp.clip(h2[0] / m2s[0], 0.0, 25.0)
    bb1 = d1 - d0
    minor = d1 * d2 - beta2
    y2 = 1.0 / (d0 * minor - beta1 * d2)
    y1 = -d2 * y2
    y0 = minor * y2
    c2 = y2
    c1 = y1 - y2 * (2.0 * a[0] + bb1)
    c0 = y0 - a[0] * y1 + y2 * (a[0] * a[0] + a[0] * bb1 - m2[0])
    return c0, c1, c2


def tree(parts):
    while len(parts) > 1:
        parts = [a + b for a, b in zip(parts[::2], parts[1::2])]
    return parts[0]


def sigmoid4(v):
    return 1.0 / (1.0 + jnp.exp(-4.0 * v))


def crossing_weight(lower, upper):
    return lower * (1.0 - upper) + (1.0 - lower) * upper


def solve_kernel(rhs, scr, act, x_out, iso_out,
           R, S, M, U1, U2, MZ, SZ, MZ2, SZ2, MZ3, SZ3, TA, TB, TC, act_s, ar1, ar2,
                 lsem, ssem, rsem, asem, arsem, token):
    gx = lax.axis_index("gx")
    gy = lax.axis_index("gy")
    z = gx // 2
    core = lax.rem(gx, 2)

    def at_z(off):
        return lax.rem(z + off + NZ, NZ) * 2 + core

    loads = [
        pltpu.make_async_copy(act.at[0], act_s, lsem.at[0]),
        pltpu.make_async_copy(rhs, R.at[pl.ds(HR, 16), pl.ds(8, 32)], lsem.at[1]),
        pltpu.make_async_copy(scr, S.at[pl.ds(HS, 16), pl.ds(8, 32)], lsem.at[2]),
    ]
    for c in loads:
        c.start()

    bar = pltpu.get_barrier_semaphore()

    def tell(x, y):
        pl.semaphore_signal(bar, inc=1, device_id=(x, y), device_id_type=MESH)

    other_chip = lax.rem(gx + 2 * core - 1 + NGX, NGX)
    for dy in (1, -1):
        tell(other_chip, lax.rem(gy + dy + NGY, NGY))
    tell(other_chip, gy)
    for j in (1, 15, 10, 6, 9, 7, 11, 5, 8, 2, 14, 13, 3, 12, 4):
        for c in (1 - core, core):
            tell(2 * z + c, lax.rem(gy + j, NGY))
    tell(2 * z + 1 - core, gy)
    for off in (4, -4, 3, -3, 2, -2, 1, -1):
        tell(at_z(off), gy)
    has = []
    for dx, dy in NEIGHBOURS:
        ok = None
        for cond in ([gx < NGX - 1] if dx == 1 else []) + ([gx > 0] if dx == -1 else []) + (
            [gy < NGY - 1] if dy == 1 else []) + ([gy > 0] if dy == -1 else []):
            ok = cond if ok is None else jnp.logical_and(ok, cond)
        has.append(ok)
    @pl.when(gx == 0)
    def _():
        R[pl.ds(0, HR)] = jnp.zeros((HR, 48, 128), jnp.float32)
        S[pl.ds(0, HS)] = jnp.zeros((HS, 48, 128), jnp.float32)
        M[0] = jnp.zeros((4, 128), jnp.float32)

    @pl.when(gx == NGX - 1)
    def _():
        R[pl.ds(HR + 16, HR)] = jnp.zeros((HR, 48, 128), jnp.float32)
        S[pl.ds(HS + 16, HS)] = jnp.zeros((HS, 48, 128), jnp.float32)
        M[2] = jnp.zeros((4, 128), jnp.float32)

    def clear_rows(row, kind):
        R[:, pl.ds(row, 8)] = jnp.zeros((28, 8, 128), jnp.float32)
        S[:, pl.ds(row, 8)] = jnp.zeros((24, 8, 128), jnp.float32)
        M[:, pl.ds(kind, 1)] = jnp.zeros((3, 1, 128), jnp.float32)

    @pl.when(gy == 0)
    def _():
        clear_rows(0, 0)

    @pl.when(gy == NGY - 1)
    def _():
        clear_rows(40, 3)

    lane = lax.broadcasted_iota(jnp.int32, (8, 128), 1)
    loads[0].wait()
    entries = [act_s[0, q] for q in range(ACT)]
    count = jnp.int32(0)
    for e in entries:
        count = count + jnp.where(e >= 0, 1, 0)
    for w in range(2):
        number = lane // BLK + 8 * w
        own = jnp.zeros((8, 128), jnp.float32)
        for e in entries:
            own = jnp.where(number == e, 1.0, own)
        M[1, pl.ds(1 + w, 1)] = own[0:1]
    loads[1].wait()
    loads[2].wait()

    def mask_rows(dx, kinds):
        tiles = [jnp.broadcast_to(M[dx, pl.ds(k, 1)], (8, 128)) for k in range(4)]
        return jnp.concatenate([tiles[k] for k in kinds], axis=0)

    own = mask_rows(1, (1, 1, 2, 2))

    def prepare(p, carry):
        R[HR + p, pl.ds(8, 32)] = R[HR + p, pl.ds(8, 32)] * own
        S[HS + p, pl.ds(8, 32)] = S[HS + p, pl.ds(8, 32)] - SIGMA
        return carry

    lax.fori_loop(0, 16, prepare, 0, unroll=4)

    pl.semaphore_wait(bar, 42)
    for off in (4, -4):
        pl.semaphore_signal(token, inc=1, device_id=(at_z(off), gy), device_id_type=MESH)

    def pieces(i, which):
        dx, dy = NEIGHBOURS[i]
        out = []
        for n in which:
            if n == 2:
                first, size = {0: (1, 2), 1: (2, 1), -1: (1, 1)}[dy]
                src = M.at[1, pl.ds(first, size)]
                dst = M.at[1 - dx, pl.ds({0: 1, 1: 0, -1: 3}[dy], size)]
            else:
                ref, h = ((R, HR), (S, HS))[n]
                planes = {0: (h, h, 16), 1: (16, 0, h), -1: (h, h + 16, h)}[dx]
                rows = {0: (8, 8, 32), 1: (40 - h, 8 - h, h), -1: (8, 40, h)}[dy]
                src = ref.at[pl.ds(planes[0], planes[2]), pl.ds(rows[0], rows[2])]
                dst = ref.at[pl.ds(planes[1], planes[2]), pl.ds(rows[1], rows[2])]
            out.append(pltpu.make_async_remote_copy(
                src, dst, ssem.at[i, n], rsem.at[i, n],
                device_id=(gx + dx, gy + dy), device_id_type=MESH))
        return out

    opposite = [NEIGHBOURS.index((-dx, -dy)) for dx, dy in NEIGHBOURS]

    def receive(which, kinds=(0, 1, 2)):
        for i in range(8):
            dx, dy = NEIGHBOURS[i]
            if (2 if dx and dy else 0 if dx else 1) not in kinds:
                continue

            @pl.when(has[opposite[i]])
            def _():
                for c in pieces(i, which):
                    c.wait_recv()

    for which, order in (((0,), range(8)), ((2, 1), (6, 7, 4, 5, 0, 1, 2, 3))):
        for i in order:
            @pl.when(has[i])
            def _():
                for c in pieces(i, which):
                    c.start()

    zero = jnp.zeros((8, 128), jnp.float32)
    sub = lax.broadcasted_iota(jnp.int32, (8, 128), 0)

    lanes = lax.broadcasted_iota(jnp.int32, (48, 128), 1)

    def z_stage(src, row, mz, sz, out_row, p, rows):
        v = src[p, pl.ds(row, rows)]
        at = lanes[0:rows]
        p1 = jnp.where(at < 1, 0.0, pltpu.roll(v, 1, 1)) + jnp.where(at > 126, 0.0, pltpu.roll(v, 127, 1))
        p2 = jnp.where(at < 2, 0.0, pltpu.roll(v, 2, 1)) + jnp.where(at > 125, 0.0, pltpu.roll(v, 126, 1))
        mz[p, pl.ds(out_row, rows)] = 66.0 * v + 26.0 * p1 + p2
        sz[p, pl.ds(out_row, rows)] = 6.0 * v - 2.0 * p1 - p2

    def x_stage(mz, sz, to, p, row, rows):
        def at(ref, off):
            return ref[p + off, pl.ds(row, rows)]

        s1 = at(sz, 1) + at(sz, 3)
        s2 = at(sz, 0) + at(sz, 4)
        m1 = at(mz, 1) + at(mz, 3)
        m2 = at(mz, 0) + at(mz, 4)
        m0 = at(mz, 2)
        one = (66.0 * at(sz, 2) + 26.0 * s1 + s2) + (6.0 * m0 - 2.0 * m1 - m2)
        two = 66.0 * m0 + 26.0 * m1 + m2
        to[0, p, pl.ds(row, rows)] = (66.0 * SCALE) * one + (6.0 * SCALE) * two
        to[1, p, pl.ds(row, rows)] = (26.0 * SCALE) * one - (2.0 * SCALE) * two
        to[2, p, pl.ds(row, rows)] = SCALE * (one - two)

    def y_stage(to, p, row, rows, m, scr_rows, src, src_row):
        def at(k, off):
            return to[k, p, pl.ds(row + off, rows)]

        k = at(0, 0) + ((at(1, -1) + at(1, 1)) + (at(2, -2) + at(2, 2)))
        centre = src[p + 2, pl.ds(src_row, rows)]
        return m * (k + scr_rows * centre), centre

    def total_of(acc, terms):
        return tuple(x + y for x, y in zip(acc, terms))

    def own_terms(value, centre, keep):
        terms = []
        for prod in (value * centre, value * value, value):
            t = [prod[8 * k:8 * k + 8] for k in range(len(keep))]
            t = [x if c is None else jnp.where(c, x, 0.0) for x, c in zip(t, keep)]
            while len(t) > 1:
                t = [x + y for x, y in zip(t[::2], t[1::2])] + t[len(t) - len(t) % 2:]
            terms.append(t[0])
        return terms

    def mask_from(dx, base):
        k = [jnp.broadcast_to(M[dx, pl.ds(j, 1)], (8, 128)) for j in range(4)]
        cut = sub >= -base
        return jnp.concatenate([jnp.where(cut, k[1], k[0]), k[1], jnp.where(cut, k[2], k[1]), k[2],
                                jnp.where(cut, k[3], k[2])], axis=0)

    mu0, sum0 = zero, zero
    for p in range(HR, HR + 16):
        z_stage(R, 8, MZ, SZ, 16, p, 32)
        v = R[p, pl.ds(8, 32)]
        w = v * v
        mu0 = mu0 + ((w[0:8] + w[8:16]) + (w[16:24] + w[24:32]))
        sum0 = sum0 + ((v[0:8] + v[8:16]) + (v[16:24] + v[24:32]))
    for p in range(6, 18):
        x_stage(MZ, SZ, TA, p, 16, 32)
    def middle1(dx):
        k = [jnp.broadcast_to(M[dx, pl.ds(j, 1)], (8, 128)) for j in (1, 2)]
        return jnp.concatenate([k[0], jnp.where(sub >= 4, k[1], k[0]), k[1]], axis=0)

    def middle2(dx):
        k = [jnp.broadcast_to(M[dx, pl.ds(j, 1)], (8, 128)) for j in (1, 2)]
        return jnp.concatenate([k[0], jnp.where(sub >= 2, k[1], k[0])], axis=0)

    def side(p, width):
        return 0 if p < width else 1 if p < width + 16 else 2

    def first_middle(p, m, acc):
        value, centre = y_stage(TA, p, 20, 24, m, S[p, pl.ds(12, 24)], R, 12)
        U1[p, pl.ds(8, 24)] = value
        return total_of(acc, own_terms(value, centre, [None] * 3)) if 4 <= p < 20 else acc

    acc = (zero, zero, zero)
    m = middle1(1)
    for p in range(6, 18):
        acc = first_middle(p, m, acc)

    halo = [p for p in range(28) if not HR <= p < HR + 16]
    outer = [p for p in range(24) if not 6 <= p < 18]
    receive((0,), (0,))
    for p in halo:
        z_stage(R, 8, MZ, SZ, 16, p, 32)
    for p in outer:
        x_stage(MZ, SZ, TA, p, 16, 32)
    receive((2, 1), (0,))
    m = [middle1(dx) for dx in range(3)]
    for p in outer:
        acc = first_middle(p, m[side(p, 4)], acc)
    for p in range(24):
        z_stage(U1, 8, MZ2, SZ2, 16, p, 24)
    for p in range(20):
        x_stage(MZ2, SZ2, TB, p, 16, 24)
    m = [middle2(dx) for dx in range(3)]
    acc2 = (zero, zero, zero)
    for p in range(20):
        value, centre = y_stage(TB, p, 18, 16, m[side(p, 2)], S[p + 2, pl.ds(14, 16)], U1, 10)
        U2[p, pl.ds(8, 16)] = value
        if 2 <= p < 18:
            acc2 = total_of(acc2, own_terms(value, centre, [None] * 2))
    for p in range(20):
        z_stage(U2, 8, MZ3, SZ3, 16, p, 16)
    for p in range(16):
        x_stage(MZ3, SZ3, TC, p, 16, 16)

    receive((0,), (1,))
    for p in range(HR, HR + 16):
        z_stage(R, 0, MZ, SZ, 8, p, 8)
        z_stage(R, 40, MZ, SZ, 48, p, 8)
    for p in range(6, 18):
        x_stage(MZ, SZ, TA, p, 8, 8)
        x_stage(MZ, SZ, TA, p, 48, 8)
    receive((0,), (2,))
    for p in halo:
        z_stage(R, 0, MZ, SZ, 8, p, 8)
        z_stage(R, 40, MZ, SZ, 48, p, 8)
    for p in outer:
        x_stage(MZ, SZ, TA, p, 8, 8)
        x_stage(MZ, SZ, TA, p, 48, 8)
    receive((2, 1), (1, 2))
    masks = [mask_from(dx, -4) for dx in range(3)]
    for p in range(24):
        m = masks[side(p, 4)]
        for row, first, keep in ((0, 4, sub >= 4), (32, 36, sub < 4)):
            value, centre = y_stage(TA, p, row + 12, 8, m[row:row + 8], S[p, pl.ds(first, 8)], R, first)
            U1[p, pl.ds(row, 8)] = value
            if 4 <= p < 20:
                acc = total_of(acc, own_terms(value, centre, [keep]))
    mu1, mu2, sum1 = acc

    for p in range(24):
        z_stage(U1, 0, MZ2, SZ2, 8, p, 8)
        z_stage(U1, 32, MZ2, SZ2, 40, p, 8)
    for p in range(20):
        x_stage(MZ2, SZ2, TB, p, 8, 8)
        x_stage(MZ2, SZ2, TB, p, 40, 8)
    masks = [mask_from(dx, -2) for dx in range(3)]
    for p in range(20):
        m = masks[side(p, 2)]
        for row, rows, keep in ((0, 8, [sub >= 2]), (24, 16, [None, sub < 2])):
            value, centre = y_stage(TB, p, row + 10, rows, m[row:row + rows],
                                    S[p + 2, pl.ds(row + 6, rows)], U1, row + 2)
            U2[p, pl.ds(row, rows)] = value
            if 2 <= p < 18:
                acc2 = total_of(acc2, own_terms(value, centre, keep))
    mu3, mu4, sum2 = acc2

    for p in range(20):
        z_stage(U2, 0, MZ3, SZ3, 8, p, 8)
        z_stage(U2, 24, MZ3, SZ3, 32, p, 16)
    for p in range(16):
        x_stage(MZ3, SZ3, TC, p, 8, 8)
        x_stage(MZ3, SZ3, TC, p, 32, 16)
    sub16 = lax.broadcasted_iota(jnp.int32, (16, 128), 0)
    lane16 = lax.broadcasted_iota(jnp.int32, (16, 128), 1)
    lane1 = lax.broadcasted_iota(jnp.int32, (1, 128), 1)
    rows = jnp.zeros((16, 128), jnp.float32)
    for k, acc in ((0, mu0), (1, mu1), (2, mu2), (3, mu3), (4, mu4), (6, sum0), (7, sum1), (8, sum2)):
        rows = jnp.where(sub16 == k, jnp.sum(acc, axis=0, keepdims=True), rows)
    total = jnp.sum(rows, axis=1, keepdims=True)
    spread = jnp.where(lane16 == sub16, total, 0.0)
    values = jnp.sum(spread, axis=0, keepdims=True)
    coarse = jnp.zeros((1, 128), jnp.float32)
    for k in range(6):
        coarse = jnp.where(lane1 == k, 1.5 * 2.0 ** (26 + k), coarse)
    mu5 = zero
    for p in range(16):
        value, centre = y_stage(TC, p, 10, 32, own, S[p + 4, pl.ds(8, 32)], U2, 2)
        w = value * centre
        mu5 = mu5 + ((w[0:8] + w[8:16]) + (w[16:24] + w[24:32]))

    last = jnp.sum(jnp.sum(mu5, axis=0, keepdims=True), axis=1, keepdims=True)
    values = jnp.where(lane1 == 5, last, values)
    rounded = (values + coarse) - coarse
    high = jnp.where(lane1 < 6, rounded, values)
    rest = jnp.where(lane1 < 6, values - rounded, 0.0)
    row = high + pltpu.roll(rest, 64, 1)
    row = jnp.where(lane1 == 9, count.astype(jnp.float32), row)

    pending = []
    mine = gy * 2 + core
    ar1[mine] = row
    for j in (10, 6, 9, 7, 11, 5, 8, 2, 14, 13, 3, 1, 15, 12, 4, 0):
        for c in (1 - core, core):
            if j == 0 and c is core:
                continue
            pltpu.make_async_remote_copy(
                ar1.at[mine], ar1.at[mine], asem.at[0], arsem.at[0],
                device_id=(2 * z + c, lax.rem(gy + j, NGY)), device_id_type=MESH).start()
    wait = pltpu.make_async_remote_copy(
        ar1.at[pl.ds(0, 31)], ar1.at[pl.ds(0, 31)], asem.at[0], arsem.at[0],
        device_id=(2 * z + 1 - core, gy), device_id_type=MESH)
    for i, ok in enumerate(has):
        @pl.when(ok)
        def _():
            for c in pieces(i, (0, 1, 2)):
                c.wait_send()
    wait.wait_recv()
    pending.append(wait)

    ar2[z] = tree([ar1[j] for j in range(32)])
    pl.semaphore_wait(token, 2)
    for off in (8, 7, -7, 6, -6, 5, -5, 4, -4, 3, -3, 2, -2, 1, -1):
        pltpu.make_async_remote_copy(
            ar2.at[z], ar2.at[z], asem.at[1], arsem.at[1],
            device_id=(at_z(off), gy), device_id_type=MESH).start()
    pending.pop().wait_send()
    wait = pltpu.make_async_remote_copy(
        ar2.at[pl.ds(0, 15)], ar2.at[pl.ds(0, 15)], asem.at[1], arsem.at[1],
        device_id=(at_z(1), gy), device_id_type=MESH)
    wait.wait_recv()
    pending.append(wait)
    row = tree([ar2[j] for j in range(16)])

    goal = jnp.where(sub16 < 10, sub16, sub16 + 54)
    picked = jnp.sum(jnp.where(lane16 == goal, row, 0.0), axis=1, keepdims=True)
    value = [jnp.broadcast_to(picked[k:k + 1], (8, 128)) for k in range(16)]
    mu = [two_sum(value[k], value[10 + k]) for k in range(6)]
    c0, c1, c2 = cg_weights(mu)
    iso = (c0 * value[6] + c1 * value[7] + c2 * value[8]) / (value[9] * float(BLK ** 3))

    def tile5(v):
        return jnp.concatenate([v] * 5, axis=0)

    iso_out[...] = iso
    c0, c1, c2 = tile5(c0), tile5(c1), tile5(c2)

    def solve(p, carry):
        x_out[p] = c0 * R[HR + p, pl.ds(8, 40)] + c1 * U1[4 + p, pl.ds(4, 40)] + c2 * U2[2 + p, pl.ds(2, 40)]
        return carry

    lax.fori_loop(0, 17, solve, 0, unroll=True)

    for c in pending:
        c.wait_send()


def crossing_kernel(x_ref, iso_ref, vis, ind_out, cross_out, G, W, BR, vis_s, sem):
    load = pltpu.make_async_copy(vis.at[0], vis_s, sem.at[0])
    load.start()
    store = pltpu.make_async_copy(x_ref.at[pl.ds(0, 16), pl.ds(0, 32)], ind_out, sem.at[1])
    store.start()
    lane = lax.broadcasted_iota(jnp.int32, (8, 128), 1)
    iso = jnp.concatenate([iso_ref[...]] * 5, axis=0)

    for p in range(17):
        G[p] = sigmoid4(x_ref[p] - iso)
    BR[pl.ds(16 * 96, 96)] = jnp.zeros((96, 128), jnp.float32)

    lane32 = lax.broadcasted_iota(jnp.int32, (32, 128), 1)
    edge = lane32 == 127
    empty = sigmoid4(0.0 - iso[0:32])
    group = lane // BLK
    odd = [(group // (1 << bit)) % 2 == 1 for bit in range(3)]
    stores = [store]
    for e in range(3):
        for p in range(16):
            g = G[p, pl.ds(0, 32)]
            if e == 0:
                other = G[p + 1, pl.ds(0, 32)]
            elif e == 1:
                other = G[p, pl.ds(1, 32)]
            else:
                other = jnp.where(edge, empty, pltpu.roll(g, 127, 1))
            h = crossing_weight(g, other)
            for w in range(2):
                W[e, pl.ds((p // 4) * 128 + w * 64 + p % 4 * 16, 16)] = h[16 * w:16 * w + 16]
        for first in range(0, 8, 4):
            parts = range(first, first + 4)
            vs = {}
            for part in parts:
                vs[part] = [W[e, pl.ds(part * 64 + (-j) % 8, 8, stride=8)] for j in range(8)]
            for part in parts:
                vs[part] = [v if j == 0 else pltpu.roll(v, 16 * ((-j) % 8), 1) for j, v in enumerate(vs[part])]
            for bit in range(3):
                for part in parts:
                    old = vs[part]
                    vs[part] = [jnp.where(odd[bit], old[(t - (1 << bit)) % 8], old[t]) for t in range(8)]
            for part in parts:
                vs[part] = [v if t == 0 else pltpu.roll(v, 128 - 16 * t, 1) for t, v in enumerate(vs[part])]
            for part in parts:
                w, ib = part % 2, part // 2
                for t in range(8):
                    BR[pl.ds((w * 8 + t) * 96 + e * 32 + ib * 8, 8)] = vs[part][t]
        if e == 0:
            load.wait()
            slots = []
            for q in range(VIS):
                n = vis_s[0, q]
                slots.append(jnp.where(n >= 0, n, 16) * 96)
        for q in range(VIS):
            start = pl.multiple_of(slots[q] + e * 32, 8)
            stores.append(pltpu.make_async_copy(
                BR.at[pl.ds(start, 32)], cross_out.at[pl.ds(q * 96 + e * 32, 32)], sem.at[2 + q * 3 + e]))
            stores[-1].start()
    for c in stores:
        c.wait()


def body(right_side, screening, active_blocks, visible_bricks):
    f32 = jnp.float32
    right_side, screening, active_blocks, visible_bricks = (
        pltpu.with_memory_space_constraint(v, pltpu.HBM)
        for v in (right_side, screening, active_blocks, visible_bricks))
    hbm = pl.BlockSpec(memory_space=pltpu.HBM)
    vmem = pl.BlockSpec(memory_space=pltpu.VMEM)
    x, iso = pl.pallas_call(
        solve_kernel,
        out_shape=(jax.ShapeDtypeStruct((17, 40, 128), f32), jax.ShapeDtypeStruct((8, 128), f32)),
        in_specs=[hbm] * 3,
        out_specs=(vmem, vmem),
        scratch_shapes=[
            pltpu.VMEM((28, 48, 128), f32),
            pltpu.VMEM((24, 48, 128), f32),
            pltpu.VMEM((3, 4, 128), f32),
            pltpu.VMEM((24, 48, 128), f32),
            pltpu.VMEM((20, 48, 128), f32),
            pltpu.VMEM((28, 64, 128), f32),
            pltpu.VMEM((28, 64, 128), f32),
            pltpu.VMEM((24, 56, 128), f32),
            pltpu.VMEM((24, 56, 128), f32),
            pltpu.VMEM((20, 56, 128), f32),
            pltpu.VMEM((20, 56, 128), f32),
            pltpu.VMEM((3, 24, 64, 128), f32),
            pltpu.VMEM((3, 20, 56, 128), f32),
            pltpu.VMEM((3, 16, 56, 128), f32),
            pltpu.SMEM((1, ACT), jnp.int32),
            pltpu.VMEM((32, 1, 128), f32),
            pltpu.VMEM((16, 1, 128), f32),
            pltpu.SemaphoreType.DMA((3,)),
            pltpu.SemaphoreType.DMA((8, 3)),
            pltpu.SemaphoreType.DMA((8, 3)),
            pltpu.SemaphoreType.DMA((2,)),
            pltpu.SemaphoreType.DMA((2,)),
            pltpu.SemaphoreType.REGULAR,
        ],
        compiler_params=pltpu.CompilerParams(
            collective_id=0, has_side_effects=True, vmem_limit_bytes=32 << 20),
    )(right_side, screening, active_blocks)
    indicator, crossing = pl.pallas_call(
        crossing_kernel,
        out_shape=(jax.ShapeDtypeStruct((16, 32, 128), f32), jax.ShapeDtypeStruct((VIS * 96, 128), f32)),
        in_specs=[vmem, vmem, hbm],
        out_specs=(hbm, hbm),
        scratch_shapes=[
            pltpu.VMEM((17, 40, 128), f32),
            pltpu.VMEM((3, 512, 128), f32),
            pltpu.VMEM((17 * 96, 128), f32),
            pltpu.SMEM((1, VIS), jnp.int32),
            pltpu.SemaphoreType.DMA((2 + 3 * VIS,)),
        ],
        compiler_params=pltpu.CompilerParams(vmem_limit_bytes=24 << 20),
    )(x, iso, visible_bricks)
    return indicator, crossing.reshape(VIS, 1, 3, BLK ** 3)


def solution(mesh):
    spec = P("gx", "gy", None)
    return jax.shard_map(
        body,
        mesh=mesh,
        in_specs=(spec, spec, spec, spec),
        out_specs=(spec, P("gx", "gy", None, None)),
        check_vma=False,
    )
```

```python
import jax
import jax.numpy as jnp
from jax import lax
from jax.experimental import pallas as pl
from jax.experimental.pallas import tpu as pltpu
from jax.sharding import PartitionSpec as P

MESH = pl.DeviceIdType.MESH
BLK = 16
ACT = 12
VIS = 8
NGX = 32
NGY = 16
NZ = 16
SIGMA = 2.5
HR = 6
HS = 4
SCALE = 1.0 / 86400.0
NEIGHBOURS = [(1, 1), (1, -1), (-1, 1), (-1, -1), (0, 1), (0, -1), (1, 0), (-1, 0)]


def two_sum(a, b):
    s = a + b
    t = s - a
    return s, (a - (s - t)) + (b - t)


def quick_two_sum(a, b):
    s = a + b
    return s, b - (s - a)


def split(a):
    c = 4097.0 * a
    hi = c - (c - a)
    return hi, a - hi


def two_prod(a, b):
    p = a * b
    ah, al = split(a)
    bh, bl = split(b)
    return p, ((ah * bh - p) + ah * bl + al * bh) + al * bl


def dd_add(x, y):
    s, e = two_sum(x[0], y[0])
    return quick_two_sum(s, e + (x[1] + y[1]))


def dd_neg(x):
    return -x[0], -x[1]


def dd_sub(x, y):
    return dd_add(x, dd_neg(y))


def dd_mul(x, y):
    p, e = two_prod(x[0], y[0])
    return quick_two_sum(p, e + (x[0] * y[1] + x[1] * y[0]))


def dd_div(x, y):
    q = x[0] / y[0]
    r = dd_sub(x, dd_mul(y, (q, jnp.zeros_like(q))))
    return quick_two_sum(q, r[0] / y[0])


def cg_weights(mu):
    one = (jnp.ones_like(mu[0][0]), jnp.zeros_like(mu[0][0]))
    inv = dd_div(one, mu[0])
    row = [dd_mul(m, inv) for m in mu[1:]]
    a = row[0]
    level = [dd_sub(row[k + 1], dd_mul(a, row[k])) for k in range(4)]
    first = [(jnp.zeros_like(a[0]), jnp.zeros_like(a[0]))] + level
    central = []
    for _ in range(4):
        first = [dd_sub(first[k + 1], dd_mul(a, first[k])) for k in range(len(first) - 1)]
        central.append(first[0])
    m2, m3, m4, m5 = central
    tiny = 1e-30
    m2s = (jnp.maximum(m2[0], tiny), jnp.where(m2[0] > tiny, m2[1], 0.0))
    b1 = dd_div(m3, m2s)
    m22 = dd_mul(m2, m2)
    h2 = dd_sub(dd_sub(m4, dd_mul(b1, m3)), m22)
    h2s = jnp.maximum(h2[0], tiny)
    inner = dd_sub(dd_mul(b1, m3), dd_add(m4, m4))
    inner = dd_add(inner, dd_add(m22, m22))
    top = dd_add(m5, dd_mul(b1, inner))
    m23 = dd_mul(m2, m3)
    top = dd_sub(top, dd_add(m23, m23))
    d0 = a[0] + SIGMA
    d1 = jnp.clip(d0 + b1[0], 0.25, 9.0)
    d2 = jnp.clip(d0 + top[0] / h2s, 0.25, 9.0)
    beta1 = jnp.maximum(m2[0], 0.0)
    beta2 = jnp.clip(h2[0] / m2s[0], 0.0, 25.0)
    bb1 = d1 - d0
    minor = d1 * d2 - beta2
    y2 = 1.0 / (d0 * minor - beta1 * d2)
    y1 = -d2 * y2
    y0 = minor * y2
    c2 = y2
    c1 = y1 - y2 * (2.0 * a[0] + bb1)
    c0 = y0 - a[0] * y1 + y2 * (a[0] * a[0] + a[0] * bb1 - m2[0])
    return c0, c1, c2


def tree(parts):
    while len(parts) > 1:
        parts = [a + b for a, b in zip(parts[::2], parts[1::2])]
    return parts[0]


def sigmoid4(v):
    return 1.0 / (1.0 + jnp.exp(-4.0 * v))


def crossing_weight(lower, upper):
    return lower * (1.0 - upper) + (1.0 - lower) * upper


def solve_kernel(rhs, scr, act, x_out, iso_out,
           R, S, M, U1, U2, MZ, SZ, MZ2, SZ2, MZ3, SZ3, TA, TB, TC, act_s, ar1, ar2,
                 lsem, ssem, rsem, asem, arsem, token):
    gx = lax.axis_index("gx")
    gy = lax.axis_index("gy")
    z = gx // 2
    core = lax.rem(gx, 2)

    def at_z(off):
        return lax.rem(z + off + NZ, NZ) * 2 + core

    loads = [
        pltpu.make_async_copy(act.at[0], act_s, lsem.at[0]),
        pltpu.make_async_copy(rhs, R.at[pl.ds(HR, 16), pl.ds(8, 32)], lsem.at[1]),
        pltpu.make_async_copy(scr, S.at[pl.ds(HS, 16), pl.ds(8, 32)], lsem.at[2]),
    ]
    for c in loads:
        c.start()

    bar = pltpu.get_barrier_semaphore()

    def tell(x, y):
        pl.semaphore_signal(bar, inc=1, device_id=(x, y), device_id_type=MESH)

    other_chip = lax.rem(gx + 2 * core - 1 + NGX, NGX)
    for dy in (1, -1):
        tell(other_chip, lax.rem(gy + dy + NGY, NGY))
    tell(other_chip, gy)
    for j in (1, 15, 10, 6, 9, 7, 11, 5, 8, 2, 14, 13, 3, 12, 4):
        for c in (1 - core, core):
            tell(2 * z + c, lax.rem(gy + j, NGY))
    tell(2 * z + 1 - core, gy)
    for off in (4, -4, 3, -3, 2, -2, 1, -1):
        tell(at_z(off), gy)
    has = []
    for dx, dy in NEIGHBOURS:
        ok = None
        for cond in ([gx < NGX - 1] if dx == 1 else []) + ([gx > 0] if dx == -1 else []) + (
            [gy < NGY - 1] if dy == 1 else []) + ([gy > 0] if dy == -1 else []):
            ok = cond if ok is None else jnp.logical_and(ok, cond)
        has.append(ok)
    @pl.when(gx == 0)
    def _():
        R[pl.ds(0, HR)] = jnp.zeros((HR, 48, 128), jnp.float32)
        S[pl.ds(0, HS)] = jnp.zeros((HS, 48, 128), jnp.float32)
        M[0] = jnp.zeros((4, 128), jnp.float32)

    @pl.when(gx == NGX - 1)
    def _():
        R[pl.ds(HR + 16, HR)] = jnp.zeros((HR, 48, 128), jnp.float32)
        S[pl.ds(HS + 16, HS)] = jnp.zeros((HS, 48, 128), jnp.float32)
        M[2] = jnp.zeros((4, 128), jnp.float32)

    def clear_rows(row, kind):
        R[:, pl.ds(row, 8)] = jnp.zeros((28, 8, 128), jnp.float32)
        S[:, pl.ds(row, 8)] = jnp.zeros((24, 8, 128), jnp.float32)
        M[:, pl.ds(kind, 1)] = jnp.zeros((3, 1, 128), jnp.float32)

    @pl.when(gy == 0)
    def _():
        clear_rows(0, 0)

    @pl.when(gy == NGY - 1)
    def _():
        clear_rows(40, 3)

    lane = lax.broadcasted_iota(jnp.int32, (8, 128), 1)
    loads[0].wait()
    entries = [act_s[0, q] for q in range(ACT)]
    count = jnp.int32(0)
    for e in entries:
        count = count + jnp.where(e >= 0, 1, 0)
    for w in range(2):
        number = lane // BLK + 8 * w
        own = jnp.zeros((8, 128), jnp.float32)
        for e in entries:
            own = jnp.where(number == e, 1.0, own)
        M[1, pl.ds(1 + w, 1)] = own[0:1]
    loads[1].wait()
    loads[2].wait()

    def mask_rows(dx, kinds):
        tiles = [jnp.broadcast_to(M[dx, pl.ds(k, 1)], (8, 128)) for k in range(4)]
        return jnp.concatenate([tiles[k] for k in kinds], axis=0)

    own = mask_rows(1, (1, 1, 2, 2))

    def prepare(p, carry):
        R[HR + p, pl.ds(8, 32)] = R[HR + p, pl.ds(8, 32)] * own
        S[HS + p, pl.ds(8, 32)] = S[HS + p, pl.ds(8, 32)] - SIGMA
        return carry

    lax.fori_loop(0, 16, prepare, 0, unroll=4)

    pl.semaphore_wait(bar, 42)
    for off in (4, -4):
        pl.semaphore_signal(token, inc=1, device_id=(at_z(off), gy), device_id_type=MESH)

    def pieces(i, which):
        dx, dy = NEIGHBOURS[i]
        out = []
        for n in which:
            if n == 2:
                first, size = {0: (1, 2), 1: (2, 1), -1: (1, 1)}[dy]
                src = M.at[1, pl.ds(first, size)]
                dst = M.at[1 - dx, pl.ds({0: 1, 1: 0, -1: 3}[dy], size)]
            else:
                ref, h = ((R, HR), (S, HS))[n]
                planes = {0: (h, h, 16), 1: (16, 0, h), -1: (h, h + 16, h)}[dx]
                rows = {0: (8, 8, 32), 1: (40 - h, 8 - h, h), -1: (8, 40, h)}[dy]
                src = ref.at[pl.ds(planes[0], planes[2]), pl.ds(rows[0], rows[2])]
                dst = ref.at[pl.ds(planes[1], planes[2]), pl.ds(rows[1], rows[2])]
            out.append(pltpu.make_async_remote_copy(
                src, dst, ssem.at[i, n], rsem.at[i, n],
                device_id=(gx + dx, gy + dy), device_id_type=MESH))
        return out

    opposite = [NEIGHBOURS.index((-dx, -dy)) for dx, dy in NEIGHBOURS]

    def receive(which, kinds=(0, 1, 2)):
        for i in range(8):
            dx, dy = NEIGHBOURS[i]
            if (2 if dx and dy else 0 if dx else 1) not in kinds:
                continue

            @pl.when(has[opposite[i]])
            def _():
                for c in pieces(i, which):
                    c.wait_recv()

    for which in ((0,), (2, 1)):
        for i, ok in enumerate(has):
            @pl.when(ok)
            def _():
                for c in pieces(i, which):
                    c.start()

    zero = jnp.zeros((8, 128), jnp.float32)
    sub = lax.broadcasted_iota(jnp.int32, (8, 128), 0)

    lanes = lax.broadcasted_iota(jnp.int32, (48, 128), 1)

    def z_stage(src, row, mz, sz, out_row, p, rows):
        v = src[p, pl.ds(row, rows)]
        at = lanes[0:rows]
        p1 = jnp.where(at < 1, 0.0, pltpu.roll(v, 1, 1)) + jnp.where(at > 126, 0.0, pltpu.roll(v, 127, 1))
        p2 = jnp.where(at < 2, 0.0, pltpu.roll(v, 2, 1)) + jnp.where(at > 125, 0.0, pltpu.roll(v, 126, 1))
        mz[p, pl.ds(out_row, rows)] = 66.0 * v + 26.0 * p1 + p2
        sz[p, pl.ds(out_row, rows)] = 6.0 * v - 2.0 * p1 - p2

    def x_stage(mz, sz, to, p, row, rows):
        def at(ref, off):
            return ref[p + off, pl.ds(row, rows)]

        s1 = at(sz, 1) + at(sz, 3)
        s2 = at(sz, 0) + at(sz, 4)
        m1 = at(mz, 1) + at(mz, 3)
        m2 = at(mz, 0) + at(mz, 4)
        m0 = at(mz, 2)
        one = (66.0 * at(sz, 2) + 26.0 * s1 + s2) + (6.0 * m0 - 2.0 * m1 - m2)
        two = 66.0 * m0 + 26.0 * m1 + m2
        to[0, p, pl.ds(row, rows)] = (66.0 * SCALE) * one + (6.0 * SCALE) * two
        to[1, p, pl.ds(row, rows)] = (26.0 * SCALE) * one - (2.0 * SCALE) * two
        to[2, p, pl.ds(row, rows)] = SCALE * (one - two)

    def y_stage(to, p, row, rows, m, scr_rows, src, src_row):
        def at(k, off):
            return to[k, p, pl.ds(row + off, rows)]

        k = at(0, 0) + ((at(1, -1) + at(1, 1)) + (at(2, -2) + at(2, 2)))
        centre = src[p + 2, pl.ds(src_row, rows)]
        return m * (k + scr_rows * centre), centre

    def total_of(acc, terms):
        return tuple(x + y for x, y in zip(acc, terms))

    def own_terms(value, centre, keep):
        terms = []
        for prod in (value * centre, value * value, value):
            t = [prod[8 * k:8 * k + 8] for k in range(len(keep))]
            t = [x if c is None else jnp.where(c, x, 0.0) for x, c in zip(t, keep)]
            while len(t) > 1:
                t = [x + y for x, y in zip(t[::2], t[1::2])] + t[len(t) - len(t) % 2:]
            terms.append(t[0])
        return terms

    def mask_from(dx, base):
        k = [jnp.broadcast_to(M[dx, pl.ds(j, 1)], (8, 128)) for j in range(4)]
        cut = sub >= -base
        return jnp.concatenate([jnp.where(cut, k[1], k[0]), k[1], jnp.where(cut, k[2], k[1]), k[2],
                                jnp.where(cut, k[3], k[2])], axis=0)

    mu0, sum0 = zero, zero
    for p in range(HR, HR + 16):
        z_stage(R, 8, MZ, SZ, 16, p, 32)
        v = R[p, pl.ds(8, 32)]
        w = v * v
        mu0 = mu0 + ((w[0:8] + w[8:16]) + (w[16:24] + w[24:32]))
        sum0 = sum0 + ((v[0:8] + v[8:16]) + (v[16:24] + v[24:32]))
    for p in range(6, 18):
        x_stage(MZ, SZ, TA, p, 16, 32)
    def middle1(dx):
        k = [jnp.broadcast_to(M[dx, pl.ds(j, 1)], (8, 128)) for j in (1, 2)]
        return jnp.concatenate([k[0], jnp.where(sub >= 4, k[1], k[0]), k[1]], axis=0)

    def middle2(dx):
        k = [jnp.broadcast_to(M[dx, pl.ds(j, 1)], (8, 128)) for j in (1, 2)]
        return jnp.concatenate([k[0], jnp.where(sub >= 2, k[1], k[0])], axis=0)

    def side(p, width):
        return 0 if p < width else 1 if p < width + 16 else 2

    def first_middle(p, m, acc):
        value, centre = y_stage(TA, p, 20, 24, m, S[p, pl.ds(12, 24)], R, 12)
        U1[p, pl.ds(8, 24)] = value
        return total_of(acc, own_terms(value, centre, [None] * 3)) if 4 <= p < 20 else acc

    acc = (zero, zero, zero)
    m = middle1(1)
    for p in range(6, 18):
        acc = first_middle(p, m, acc)

    halo = [p for p in range(28) if not HR <= p < HR + 16]
    outer = [p for p in range(24) if not 6 <= p < 18]
    receive((0,), (0,))
    for p in halo:
        z_stage(R, 8, MZ, SZ, 16, p, 32)
    for p in outer:
        x_stage(MZ, SZ, TA, p, 16, 32)
    receive((2, 1), (0,))
    m = [middle1(dx) for dx in range(3)]
    for p in outer:
        acc = first_middle(p, m[side(p, 4)], acc)
    for p in range(24):
        z_stage(U1, 8, MZ2, SZ2, 16, p, 24)
    for p in range(20):
        x_stage(MZ2, SZ2, TB, p, 16, 24)
    m = [middle2(dx) for dx in range(3)]
    acc2 = (zero, zero, zero)
    for p in range(20):
        value, centre = y_stage(TB, p, 18, 16, m[side(p, 2)], S[p + 2, pl.ds(14, 16)], U1, 10)
        U2[p, pl.ds(8, 16)] = value
        if 2 <= p < 18:
            acc2 = total_of(acc2, own_terms(value, centre, [None] * 2))
    for p in range(20):
        z_stage(U2, 8, MZ3, SZ3, 16, p, 16)
    for p in range(16):
        x_stage(MZ3, SZ3, TC, p, 16, 16)

    receive((0,), (1,))
    for p in range(HR, HR + 16):
        z_stage(R, 0, MZ, SZ, 8, p, 8)
        z_stage(R, 40, MZ, SZ, 48, p, 8)
    for p in range(6, 18):
        x_stage(MZ, SZ, TA, p, 8, 8)
        x_stage(MZ, SZ, TA, p, 48, 8)
    receive((0,), (2,))
    for p in halo:
        z_stage(R, 0, MZ, SZ, 8, p, 8)
        z_stage(R, 40, MZ, SZ, 48, p, 8)
    for p in outer:
        x_stage(MZ, SZ, TA, p, 8, 8)
        x_stage(MZ, SZ, TA, p, 48, 8)
    receive((2, 1), (1, 2))
    masks = [mask_from(dx, -4) for dx in range(3)]
    for p in range(24):
        m = masks[side(p, 4)]
        for row, first, keep in ((0, 4, sub >= 4), (32, 36, sub < 4)):
            value, centre = y_stage(TA, p, row + 12, 8, m[row:row + 8], S[p, pl.ds(first, 8)], R, first)
            U1[p, pl.ds(row, 8)] = value
            if 4 <= p < 20:
                acc = total_of(acc, own_terms(value, centre, [keep]))
    mu1, mu2, sum1 = acc

    for p in range(24):
        z_stage(U1, 0, MZ2, SZ2, 8, p, 8)
        z_stage(U1, 32, MZ2, SZ2, 40, p, 8)
    for p in range(20):
        x_stage(MZ2, SZ2, TB, p, 8, 8)
        x_stage(MZ2, SZ2, TB, p, 40, 8)
    masks = [mask_from(dx, -2) for dx in range(3)]
    for p in range(20):
        m = masks[side(p, 2)]
        for row, rows, keep in ((0, 8, [sub >= 2]), (24, 16, [None, sub < 2])):
            value, centre = y_stage(TB, p, row + 10, rows, m[row:row + rows],
                                    S[p + 2, pl.ds(row + 6, rows)], U1, row + 2)
            U2[p, pl.ds(row, rows)] = value
            if 2 <= p < 18:
                acc2 = total_of(acc2, own_terms(value, centre, keep))
    mu3, mu4, sum2 = acc2

    for p in range(20):
        z_stage(U2, 0, MZ3, SZ3, 8, p, 8)
        z_stage(U2, 24, MZ3, SZ3, 32, p, 16)
    for p in range(16):
        x_stage(MZ3, SZ3, TC, p, 8, 8)
        x_stage(MZ3, SZ3, TC, p, 32, 16)
    sub16 = lax.broadcasted_iota(jnp.int32, (16, 128), 0)
    lane16 = lax.broadcasted_iota(jnp.int32, (16, 128), 1)
    lane1 = lax.broadcasted_iota(jnp.int32, (1, 128), 1)
    rows = jnp.zeros((16, 128), jnp.float32)
    for k, acc in ((0, mu0), (1, mu1), (2, mu2), (3, mu3), (4, mu4), (6, sum0), (7, sum1), (8, sum2)):
        rows = jnp.where(sub16 == k, jnp.sum(acc, axis=0, keepdims=True), rows)
    total = jnp.sum(rows, axis=1, keepdims=True)
    spread = jnp.where(lane16 == sub16, total, 0.0)
    values = jnp.sum(spread, axis=0, keepdims=True)
    coarse = jnp.zeros((1, 128), jnp.float32)
    for k in range(6):
        coarse = jnp.where(lane1 == k, 1.5 * 2.0 ** (26 + k), coarse)
    mu5 = zero
    for p in range(16):
        value, centre = y_stage(TC, p, 10, 32, own, S[p + 4, pl.ds(8, 32)], U2, 2)
        w = value * centre
        mu5 = mu5 + ((w[0:8] + w[8:16]) + (w[16:24] + w[24:32]))

    last = jnp.sum(jnp.sum(mu5, axis=0, keepdims=True), axis=1, keepdims=True)
    values = jnp.where(lane1 == 5, last, values)
    rounded = (values + coarse) - coarse
    high = jnp.where(lane1 < 6, rounded, values)
    rest = jnp.where(lane1 < 6, values - rounded, 0.0)
    row = high + pltpu.roll(rest, 64, 1)
    row = jnp.where(lane1 == 9, count.astype(jnp.float32), row)

    pending = []
    mine = gy * 2 + core
    ar1[mine] = row
    for j in (10, 6, 9, 7, 11, 5, 8, 2, 14, 13, 3, 1, 15, 12, 4, 0):
        for c in (1 - core, core):
            if j == 0 and c is core:
                continue
            pltpu.make_async_remote_copy(
                ar1.at[mine], ar1.at[mine], asem.at[0], arsem.at[0],
                device_id=(2 * z + c, lax.rem(gy + j, NGY)), device_id_type=MESH).start()
    wait = pltpu.make_async_remote_copy(
        ar1.at[pl.ds(0, 31)], ar1.at[pl.ds(0, 31)], asem.at[0], arsem.at[0],
        device_id=(2 * z + 1 - core, gy), device_id_type=MESH)
    for i, ok in enumerate(has):
        @pl.when(ok)
        def _():
            for c in pieces(i, (0, 1, 2)):
                c.wait_send()
    wait.wait_recv()
    pending.append(wait)

    ar2[z] = tree([ar1[j] for j in range(32)])
    pl.semaphore_wait(token, 2)
    for off in (8, 7, -7, 6, -6, 5, -5, 4, -4, 3, -3, 2, -2, 1, -1):
        pltpu.make_async_remote_copy(
            ar2.at[z], ar2.at[z], asem.at[1], arsem.at[1],
            device_id=(at_z(off), gy), device_id_type=MESH).start()
    pending.pop().wait_send()
    wait = pltpu.make_async_remote_copy(
        ar2.at[pl.ds(0, 15)], ar2.at[pl.ds(0, 15)], asem.at[1], arsem.at[1],
        device_id=(at_z(1), gy), device_id_type=MESH)
    wait.wait_recv()
    pending.append(wait)
    row = tree([ar2[j] for j in range(16)])

    goal = jnp.where(sub16 < 10, sub16, sub16 + 54)
    picked = jnp.sum(jnp.where(lane16 == goal, row, 0.0), axis=1, keepdims=True)
    value = [jnp.broadcast_to(picked[k:k + 1], (8, 128)) for k in range(16)]
    mu = [two_sum(value[k], value[10 + k]) for k in range(6)]
    c0, c1, c2 = cg_weights(mu)
    iso = (c0 * value[6] + c1 * value[7] + c2 * value[8]) / (value[9] * float(BLK ** 3))

    def tile5(v):
        return jnp.concatenate([v] * 5, axis=0)

    iso_out[...] = iso
    c0, c1, c2 = tile5(c0), tile5(c1), tile5(c2)

    def solve(p, carry):
        x_out[p] = c0 * R[HR + p, pl.ds(8, 40)] + c1 * U1[4 + p, pl.ds(4, 40)] + c2 * U2[2 + p, pl.ds(2, 40)]
        return carry

    lax.fori_loop(0, 17, solve, 0, unroll=True)

    for c in pending:
        c.wait_send()


def crossing_kernel(x_ref, iso_ref, vis, ind_out, cross_out, G, W, BR, vis_s, sem):
    load = pltpu.make_async_copy(vis.at[0], vis_s, sem.at[0])
    load.start()
    store = pltpu.make_async_copy(x_ref.at[pl.ds(0, 16), pl.ds(0, 32)], ind_out, sem.at[1])
    store.start()
    lane = lax.broadcasted_iota(jnp.int32, (8, 128), 1)
    iso = jnp.concatenate([iso_ref[...]] * 5, axis=0)

    for p in range(17):
        G[p] = sigmoid4(x_ref[p] - iso)
    BR[pl.ds(16 * 96, 96)] = jnp.zeros((96, 128), jnp.float32)

    lane32 = lax.broadcasted_iota(jnp.int32, (32, 128), 1)
    edge = lane32 == 127
    empty = sigmoid4(0.0 - iso[0:32])
    group = lane // BLK
    odd = [(group // (1 << bit)) % 2 == 1 for bit in range(3)]
    stores = [store]
    for e in range(3):
        for p in range(16):
            g = G[p, pl.ds(0, 32)]
            if e == 0:
                other = G[p + 1, pl.ds(0, 32)]
            elif e == 1:
                other = G[p, pl.ds(1, 32)]
            else:
                other = jnp.where(edge, empty, pltpu.roll(g, 127, 1))
            h = crossing_weight(g, other)
            for w in range(2):
                W[e, pl.ds((p // 4) * 128 + w * 64 + p % 4 * 16, 16)] = h[16 * w:16 * w + 16]
        for first in range(0, 8, 4):
            parts = range(first, first + 4)
            vs = {}
            for part in parts:
                vs[part] = [W[e, pl.ds(part * 64 + (-j) % 8, 8, stride=8)] for j in range(8)]
            for part in parts:
                vs[part] = [v if j == 0 else pltpu.roll(v, 16 * ((-j) % 8), 1) for j, v in enumerate(vs[part])]
            for bit in range(3):
                for part in parts:
                    old = vs[part]
                    vs[part] = [jnp.where(odd[bit], old[(t - (1 << bit)) % 8], old[t]) for t in range(8)]
            for part in parts:
                vs[part] = [v if t == 0 else pltpu.roll(v, 128 - 16 * t, 1) for t, v in enumerate(vs[part])]
            for part in parts:
                w, ib = part % 2, part // 2
                for t in range(8):
                    BR[pl.ds((w * 8 + t) * 96 + e * 32 + ib * 8, 8)] = vs[part][t]
        if e == 0:
            load.wait()
            slots = []
            for q in range(VIS):
                n = vis_s[0, q]
                slots.append(jnp.where(n >= 0, n, 16) * 96)
        for q in range(VIS):
            start = pl.multiple_of(slots[q] + e * 32, 8)
            stores.append(pltpu.make_async_copy(
                BR.at[pl.ds(start, 32)], cross_out.at[pl.ds(q * 96 + e * 32, 32)], sem.at[2 + q * 3 + e]))
            stores[-1].start()
    for c in stores:
        c.wait()


def body(right_side, screening, active_blocks, visible_bricks):
    f32 = jnp.float32
    right_side, screening, active_blocks, visible_bricks = (
        pltpu.with_memory_space_constraint(v, pltpu.HBM)
        for v in (right_side, screening, active_blocks, visible_bricks))
    hbm = pl.BlockSpec(memory_space=pltpu.HBM)
    vmem = pl.BlockSpec(memory_space=pltpu.VMEM)
    x, iso = pl.pallas_call(
        solve_kernel,
        out_shape=(jax.ShapeDtypeStruct((17, 40, 128), f32), jax.ShapeDtypeStruct((8, 128), f32)),
        in_specs=[hbm] * 3,
        out_specs=(vmem, vmem),
        scratch_shapes=[
            pltpu.VMEM((28, 48, 128), f32),
            pltpu.VMEM((24, 48, 128), f32),
            pltpu.VMEM((3, 4, 128), f32),
            pltpu.VMEM((24, 48, 128), f32),
            pltpu.VMEM((20, 48, 128), f32),
            pltpu.VMEM((28, 64, 128), f32),
            pltpu.VMEM((28, 64, 128), f32),
            pltpu.VMEM((24, 56, 128), f32),
            pltpu.VMEM((24, 56, 128), f32),
            pltpu.VMEM((20, 56, 128), f32),
            pltpu.VMEM((20, 56, 128), f32),
            pltpu.VMEM((3, 24, 64, 128), f32),
            pltpu.VMEM((3, 20, 56, 128), f32),
            pltpu.VMEM((3, 16, 56, 128), f32),
            pltpu.SMEM((1, ACT), jnp.int32),
            pltpu.VMEM((32, 1, 128), f32),
            pltpu.VMEM((16, 1, 128), f32),
            pltpu.SemaphoreType.DMA((3,)),
            pltpu.SemaphoreType.DMA((8, 3)),
            pltpu.SemaphoreType.DMA((8, 3)),
            pltpu.SemaphoreType.DMA((2,)),
            pltpu.SemaphoreType.DMA((2,)),
            pltpu.SemaphoreType.REGULAR,
        ],
        compiler_params=pltpu.CompilerParams(
            collective_id=0, has_side_effects=True, vmem_limit_bytes=32 << 20),
    )(right_side, screening, active_blocks)
    indicator, crossing = pl.pallas_call(
        crossing_kernel,
        out_shape=(jax.ShapeDtypeStruct((16, 32, 128), f32), jax.ShapeDtypeStruct((VIS * 96, 128), f32)),
        in_specs=[vmem, vmem, hbm],
        out_specs=(hbm, hbm),
        scratch_shapes=[
            pltpu.VMEM((17, 40, 128), f32),
            pltpu.VMEM((3, 512, 128), f32),
            pltpu.VMEM((17 * 96, 128), f32),
            pltpu.SMEM((1, VIS), jnp.int32),
            pltpu.SemaphoreType.DMA((2 + 3 * VIS,)),
        ],
        compiler_params=pltpu.CompilerParams(vmem_limit_bytes=24 << 20),
    )(x, iso, visible_bricks)
    return indicator, crossing.reshape(VIS, 1, 3, BLK ** 3)


def solution(mesh):
    spec = P("gx", "gy", None)
    return jax.shard_map(
        body,
        mesh=mesh,
        in_specs=(spec, spec, spec, spec),
        out_specs=(spec, P("gx", "gy", None, None)),
        check_vma=False,
    )
```

```python
import jax
import jax.numpy as jnp
from jax import lax
from jax.experimental import pallas as pl
from jax.experimental.pallas import tpu as pltpu
from jax.sharding import PartitionSpec as P

MESH = pl.DeviceIdType.MESH
BLK = 16
ACT = 12
VIS = 8
NGX = 32
NGY = 16
NZ = 16
SIGMA = 2.5
HR = 6
HS = 4
SCALE = 1.0 / 86400.0
NEIGHBOURS = [(1, 1), (1, -1), (-1, 1), (-1, -1), (0, 1), (0, -1), (1, 0), (-1, 0)]


def two_sum(a, b):
    s = a + b
    t = s - a
    return s, (a - (s - t)) + (b - t)


def quick_two_sum(a, b):
    s = a + b
    return s, b - (s - a)


def split(a):
    c = 4097.0 * a
    hi = c - (c - a)
    return hi, a - hi


def two_prod(a, b):
    p = a * b
    ah, al = split(a)
    bh, bl = split(b)
    return p, ((ah * bh - p) + ah * bl + al * bh) + al * bl


def dd_add(x, y):
    s, e = two_sum(x[0], y[0])
    return quick_two_sum(s, e + (x[1] + y[1]))


def dd_neg(x):
    return -x[0], -x[1]


def dd_sub(x, y):
    return dd_add(x, dd_neg(y))


def dd_mul(x, y):
    p, e = two_prod(x[0], y[0])
    return quick_two_sum(p, e + (x[0] * y[1] + x[1] * y[0]))


def dd_div(x, y):
    q = x[0] / y[0]
    r = dd_sub(x, dd_mul(y, (q, jnp.zeros_like(q))))
    return quick_two_sum(q, r[0] / y[0])


def cg_weights(mu):
    one = (jnp.ones_like(mu[0][0]), jnp.zeros_like(mu[0][0]))
    inv = dd_div(one, mu[0])
    row = [dd_mul(m, inv) for m in mu[1:]]
    a = row[0]
    level = [dd_sub(row[k + 1], dd_mul(a, row[k])) for k in range(4)]
    first = [(jnp.zeros_like(a[0]), jnp.zeros_like(a[0]))] + level
    central = []
    for _ in range(4):
        first = [dd_sub(first[k + 1], dd_mul(a, first[k])) for k in range(len(first) - 1)]
        central.append(first[0])
    m2, m3, m4, m5 = central
    tiny = 1e-30
    m2s = (jnp.maximum(m2[0], tiny), jnp.where(m2[0] > tiny, m2[1], 0.0))
    b1 = dd_div(m3, m2s)
    m22 = dd_mul(m2, m2)
    h2 = dd_sub(dd_sub(m4, dd_mul(b1, m3)), m22)
    h2s = jnp.maximum(h2[0], tiny)
    inner = dd_sub(dd_mul(b1, m3), dd_add(m4, m4))
    inner = dd_add(inner, dd_add(m22, m22))
    top = dd_add(m5, dd_mul(b1, inner))
    m23 = dd_mul(m2, m3)
    top = dd_sub(top, dd_add(m23, m23))
    d0 = a[0] + SIGMA
    d1 = jnp.clip(d0 + b1[0], 0.25, 9.0)
    d2 = jnp.clip(d0 + top[0] / h2s, 0.25, 9.0)
    beta1 = jnp.maximum(m2[0], 0.0)
    beta2 = jnp.clip(h2[0] / m2s[0], 0.0, 25.0)
    bb1 = d1 - d0
    minor = d1 * d2 - beta2
    y2 = 1.0 / (d0 * minor - beta1 * d2)
    y1 = -d2 * y2
    y0 = minor * y2
    c2 = y2
    c1 = y1 - y2 * (2.0 * a[0] + bb1)
    c0 = y0 - a[0] * y1 + y2 * (a[0] * a[0] + a[0] * bb1 - m2[0])
    return c0, c1, c2


def tree(parts):
    while len(parts) > 1:
        parts = [a + b for a, b in zip(parts[::2], parts[1::2])]
    return parts[0]


def sigmoid4(v):
    return 1.0 / (1.0 + jnp.exp(-4.0 * v))


def crossing_weight(lower, upper):
    return lower * (1.0 - upper) + (1.0 - lower) * upper


def solve_kernel(rhs, scr, act, x_out, iso_out,
           R, S, M, U1, U2, MZ, SZ, MZ2, SZ2, MZ3, SZ3, TA, TB, TC, act_s, ar1, ar2,
                 lsem, ssem, rsem, asem, arsem, token):
    gx = lax.axis_index("gx")
    gy = lax.axis_index("gy")
    z = gx // 2
    core = lax.rem(gx, 2)

    def at_z(off):
        return lax.rem(z + off + NZ, NZ) * 2 + core

    loads = [
        pltpu.make_async_copy(act.at[0], act_s, lsem.at[0]),
        pltpu.make_async_copy(rhs, R.at[pl.ds(HR, 16), pl.ds(8, 32)], lsem.at[1]),
        pltpu.make_async_copy(scr, S.at[pl.ds(HS, 16), pl.ds(8, 32)], lsem.at[2]),
    ]
    for c in loads:
        c.start()

    bar = pltpu.get_barrier_semaphore()

    def tell(x, y):
        pl.semaphore_signal(bar, inc=1, device_id=(x, y), device_id_type=MESH)

    other_chip = lax.rem(gx + 2 * core - 1 + NGX, NGX)
    for dy in (1, -1):
        tell(other_chip, lax.rem(gy + dy + NGY, NGY))
    tell(other_chip, gy)
    for j in (1, 15, 10, 6, 9, 7, 11, 5, 8, 2, 14, 13, 3, 12, 4):
        for c in (1 - core, core):
            tell(2 * z + c, lax.rem(gy + j, NGY))
    tell(2 * z + 1 - core, gy)
    for off in (4, -4, 3, -3, 2, -2, 1, -1):
        tell(at_z(off), gy)
    has = []
    for dx, dy in NEIGHBOURS:
        ok = None
        for cond in ([gx < NGX - 1] if dx == 1 else []) + ([gx > 0] if dx == -1 else []) + (
            [gy < NGY - 1] if dy == 1 else []) + ([gy > 0] if dy == -1 else []):
            ok = cond if ok is None else jnp.logical_and(ok, cond)
        has.append(ok)
    @pl.when(gx == 0)
    def _():
        R[pl.ds(0, HR)] = jnp.zeros((HR, 48, 128), jnp.float32)
        S[pl.ds(0, HS)] = jnp.zeros((HS, 48, 128), jnp.float32)
        M[0] = jnp.zeros((4, 128), jnp.float32)

    @pl.when(gx == NGX - 1)
    def _():
        R[pl.ds(HR + 16, HR)] = jnp.zeros((HR, 48, 128), jnp.float32)
        S[pl.ds(HS + 16, HS)] = jnp.zeros((HS, 48, 128), jnp.float32)
        M[2] = jnp.zeros((4, 128), jnp.float32)

    def clear_rows(row, kind):
        R[:, pl.ds(row, 8)] = jnp.zeros((28, 8, 128), jnp.float32)
        S[:, pl.ds(row, 8)] = jnp.zeros((24, 8, 128), jnp.float32)
        M[:, pl.ds(kind, 1)] = jnp.zeros((3, 1, 128), jnp.float32)

    @pl.when(gy == 0)
    def _():
        clear_rows(0, 0)

    @pl.when(gy == NGY - 1)
    def _():
        clear_rows(40, 3)

    lane = lax.broadcasted_iota(jnp.int32, (8, 128), 1)
    loads[0].wait()
    entries = [act_s[0, q] for q in range(ACT)]
    count = jnp.int32(0)
    for e in entries:
        count = count + jnp.where(e >= 0, 1, 0)
    for w in range(2):
        number = lane // BLK + 8 * w
        own = jnp.zeros((8, 128), jnp.float32)
        for e in entries:
            own = jnp.where(number == e, 1.0, own)
        M[1, pl.ds(1 + w, 1)] = own[0:1]
    loads[1].wait()
    loads[2].wait()

    def mask_rows(dx, kinds):
        tiles = [jnp.broadcast_to(M[dx, pl.ds(k, 1)], (8, 128)) for k in range(4)]
        return jnp.concatenate([tiles[k] for k in kinds], axis=0)

    own = mask_rows(1, (1, 1, 2, 2))

    def prepare(p, carry):
        R[HR + p, pl.ds(8, 32)] = R[HR + p, pl.ds(8, 32)] * own
        S[HS + p, pl.ds(8, 32)] = S[HS + p, pl.ds(8, 32)] - SIGMA
        return carry

    lax.fori_loop(0, 16, prepare, 0, unroll=4)

    pl.semaphore_wait(bar, 42)
    for off in (4, -4):
        pl.semaphore_signal(token, inc=1, device_id=(at_z(off), gy), device_id_type=MESH)

    def pieces(i, which):
        dx, dy = NEIGHBOURS[i]
        out = []
        for n in which:
            if n == 2:
                first, size = {0: (1, 2), 1: (2, 1), -1: (1, 1)}[dy]
                src = M.at[1, pl.ds(first, size)]
                dst = M.at[1 - dx, pl.ds({0: 1, 1: 0, -1: 3}[dy], size)]
            else:
                ref, h = ((R, HR), (S, HS))[n]
                planes = {0: (h, h, 16), 1: (16, 0, h), -1: (h, h + 16, h)}[dx]
                rows = {0: (8, 8, 32), 1: (40 - h, 8 - h, h), -1: (8, 40, h)}[dy]
                src = ref.at[pl.ds(planes[0], planes[2]), pl.ds(rows[0], rows[2])]
                dst = ref.at[pl.ds(planes[1], planes[2]), pl.ds(rows[1], rows[2])]
            out.append(pltpu.make_async_remote_copy(
                src, dst, ssem.at[i, n], rsem.at[i, n],
                device_id=(gx + dx, gy + dy), device_id_type=MESH))
        return out

    opposite = [NEIGHBOURS.index((-dx, -dy)) for dx, dy in NEIGHBOURS]

    def receive(which, kinds=(0, 1, 2)):
        for i in range(8):
            dx, dy = NEIGHBOURS[i]
            if (2 if dx and dy else 0 if dx else 1) not in kinds:
                continue

            @pl.when(has[opposite[i]])
            def _():
                for c in pieces(i, which):
                    c.wait_recv()

    for which, order in (((0,), (6, 7, 0, 1, 2, 3, 4, 5)), ((2, 1), range(8))):
        for i in order:
            @pl.when(has[i])
            def _():
                for c in pieces(i, which):
                    c.start()

    zero = jnp.zeros((8, 128), jnp.float32)
    sub = lax.broadcasted_iota(jnp.int32, (8, 128), 0)

    lanes = lax.broadcasted_iota(jnp.int32, (48, 128), 1)

    def z_stage(src, row, mz, sz, out_row, p, rows):
        v = src[p, pl.ds(row, rows)]
        at = lanes[0:rows]
        p1 = jnp.where(at < 1, 0.0, pltpu.roll(v, 1, 1)) + jnp.where(at > 126, 0.0, pltpu.roll(v, 127, 1))
        p2 = jnp.where(at < 2, 0.0, pltpu.roll(v, 2, 1)) + jnp.where(at > 125, 0.0, pltpu.roll(v, 126, 1))
        mz[p, pl.ds(out_row, rows)] = 66.0 * v + 26.0 * p1 + p2
        sz[p, pl.ds(out_row, rows)] = 6.0 * v - 2.0 * p1 - p2

    def x_stage(mz, sz, to, p, row, rows):
        def at(ref, off):
            return ref[p + off, pl.ds(row, rows)]

        s1 = at(sz, 1) + at(sz, 3)
        s2 = at(sz, 0) + at(sz, 4)
        m1 = at(mz, 1) + at(mz, 3)
        m2 = at(mz, 0) + at(mz, 4)
        m0 = at(mz, 2)
        one = (66.0 * at(sz, 2) + 26.0 * s1 + s2) + (6.0 * m0 - 2.0 * m1 - m2)
        two = 66.0 * m0 + 26.0 * m1 + m2
        to[0, p, pl.ds(row, rows)] = (66.0 * SCALE) * one + (6.0 * SCALE) * two
        to[1, p, pl.ds(row, rows)] = (26.0 * SCALE) * one - (2.0 * SCALE) * two
        to[2, p, pl.ds(row, rows)] = SCALE * (one - two)

    def y_stage(to, p, row, rows, m, scr_rows, src, src_row):
        def at(k, off):
            return to[k, p, pl.ds(row + off, rows)]

        k = at(0, 0) + ((at(1, -1) + at(1, 1)) + (at(2, -2) + at(2, 2)))
        centre = src[p + 2, pl.ds(src_row, rows)]
        return m * (k + scr_rows * centre), centre

    def total_of(acc, terms):
        return tuple(x + y for x, y in zip(acc, terms))

    def own_terms(value, centre, keep):
        terms = []
        for prod in (value * centre, value * value, value):
            t = [prod[8 * k:8 * k + 8] for k in range(len(keep))]
            t = [x if c is None else jnp.where(c, x, 0.0) for x, c in zip(t, keep)]
            while len(t) > 1:
                t = [x + y for x, y in zip(t[::2], t[1::2])] + t[len(t) - len(t) % 2:]
            terms.append(t[0])
        return terms

    def mask_from(dx, base):
        k = [jnp.broadcast_to(M[dx, pl.ds(j, 1)], (8, 128)) for j in range(4)]
        cut = sub >= -base
        return jnp.concatenate([jnp.where(cut, k[1], k[0]), k[1], jnp.where(cut, k[2], k[1]), k[2],
                                jnp.where(cut, k[3], k[2])], axis=0)

    mu0, sum0 = zero, zero
    for p in range(HR, HR + 16):
        z_stage(R, 8, MZ, SZ, 16, p, 32)
        v = R[p, pl.ds(8, 32)]
        w = v * v
        mu0 = mu0 + ((w[0:8] + w[8:16]) + (w[16:24] + w[24:32]))
        sum0 = sum0 + ((v[0:8] + v[8:16]) + (v[16:24] + v[24:32]))
    for p in range(6, 18):
        x_stage(MZ, SZ, TA, p, 16, 32)
    def middle1(dx):
        k = [jnp.broadcast_to(M[dx, pl.ds(j, 1)], (8, 128)) for j in (1, 2)]
        return jnp.concatenate([k[0], jnp.where(sub >= 4, k[1], k[0]), k[1]], axis=0)

    def middle2(dx):
        k = [jnp.broadcast_to(M[dx, pl.ds(j, 1)], (8, 128)) for j in (1, 2)]
        return jnp.concatenate([k[0], jnp.where(sub >= 2, k[1], k[0])], axis=0)

    def side(p, width):
        return 0 if p < width else 1 if p < width + 16 else 2

    def first_middle(p, m, acc):
        value, centre = y_stage(TA, p, 20, 24, m, S[p, pl.ds(12, 24)], R, 12)
        U1[p, pl.ds(8, 24)] = value
        return total_of(acc, own_terms(value, centre, [None] * 3)) if 4 <= p < 20 else acc

    acc = (zero, zero, zero)
    m = middle1(1)
    for p in range(6, 18):
        acc = first_middle(p, m, acc)

    halo = [p for p in range(28) if not HR <= p < HR + 16]
    outer = [p for p in range(24) if not 6 <= p < 18]
    receive((0,), (0,))
    for p in halo:
        z_stage(R, 8, MZ, SZ, 16, p, 32)
    for p in outer:
        x_stage(MZ, SZ, TA, p, 16, 32)
    receive((2, 1), (0,))
    m = [middle1(dx) for dx in range(3)]
    for p in outer:
        acc = first_middle(p, m[side(p, 4)], acc)
    for p in range(24):
        z_stage(U1, 8, MZ2, SZ2, 16, p, 24)
    for p in range(20):
        x_stage(MZ2, SZ2, TB, p, 16, 24)
    m = [middle2(dx) for dx in range(3)]
    acc2 = (zero, zero, zero)
    for p in range(20):
        value, centre = y_stage(TB, p, 18, 16, m[side(p, 2)], S[p + 2, pl.ds(14, 16)], U1, 10)
        U2[p, pl.ds(8, 16)] = value
        if 2 <= p < 18:
            acc2 = total_of(acc2, own_terms(value, centre, [None] * 2))
    for p in range(20):
        z_stage(U2, 8, MZ3, SZ3, 16, p, 16)
    for p in range(16):
        x_stage(MZ3, SZ3, TC, p, 16, 16)

    receive((0,), (1,))
    for p in range(HR, HR + 16):
        z_stage(R, 0, MZ, SZ, 8, p, 8)
        z_stage(R, 40, MZ, SZ, 48, p, 8)
    for p in range(6, 18):
        x_stage(MZ, SZ, TA, p, 8, 8)
        x_stage(MZ, SZ, TA, p, 48, 8)
    receive((0,), (2,))
    for p in halo:
        z_stage(R, 0, MZ, SZ, 8, p, 8)
        z_stage(R, 40, MZ, SZ, 48, p, 8)
    for p in outer:
        x_stage(MZ, SZ, TA, p, 8, 8)
        x_stage(MZ, SZ, TA, p, 48, 8)
    receive((2, 1), (1, 2))
    masks = [mask_from(dx, -4) for dx in range(3)]
    for p in range(24):
        m = masks[side(p, 4)]
        for row, first, keep in ((0, 4, sub >= 4), (32, 36, sub < 4)):
            value, centre = y_stage(TA, p, row + 12, 8, m[row:row + 8], S[p, pl.ds(first, 8)], R, first)
            U1[p, pl.ds(row, 8)] = value
            if 4 <= p < 20:
                acc = total_of(acc, own_terms(value, centre, [keep]))
    mu1, mu2, sum1 = acc

    for p in range(24):
        z_stage(U1, 0, MZ2, SZ2, 8, p, 8)
        z_stage(U1, 32, MZ2, SZ2, 40, p, 8)
    for p in range(20):
        x_stage(MZ2, SZ2, TB, p, 8, 8)
        x_stage(MZ2, SZ2, TB, p, 40, 8)
    masks = [mask_from(dx, -2) for dx in range(3)]
    for p in range(20):
        m = masks[side(p, 2)]
        for row, rows, keep in ((0, 8, [sub >= 2]), (24, 16, [None, sub < 2])):
            value, centre = y_stage(TB, p, row + 10, rows, m[row:row + rows],
                                    S[p + 2, pl.ds(row + 6, rows)], U1, row + 2)
            U2[p, pl.ds(row, rows)] = value
            if 2 <= p < 18:
                acc2 = total_of(acc2, own_terms(value, centre, keep))
    mu3, mu4, sum2 = acc2

    for p in range(20):
        z_stage(U2, 0, MZ3, SZ3, 8, p, 8)
        z_stage(U2, 24, MZ3, SZ3, 32, p, 16)
    for p in range(16):
        x_stage(MZ3, SZ3, TC, p, 8, 8)
        x_stage(MZ3, SZ3, TC, p, 32, 16)
    sub16 = lax.broadcasted_iota(jnp.int32, (16, 128), 0)
    lane16 = lax.broadcasted_iota(jnp.int32, (16, 128), 1)
    lane1 = lax.broadcasted_iota(jnp.int32, (1, 128), 1)
    rows = jnp.zeros((16, 128), jnp.float32)
    for k, acc in ((0, mu0), (1, mu1), (2, mu2), (3, mu3), (4, mu4), (6, sum0), (7, sum1), (8, sum2)):
        rows = jnp.where(sub16 == k, jnp.sum(acc, axis=0, keepdims=True), rows)
    total = jnp.sum(rows, axis=1, keepdims=True)
    spread = jnp.where(lane16 == sub16, total, 0.0)
    values = jnp.sum(spread, axis=0, keepdims=True)
    coarse = jnp.zeros((1, 128), jnp.float32)
    for k in range(6):
        coarse = jnp.where(lane1 == k, 1.5 * 2.0 ** (26 + k), coarse)
    mu5 = zero
    for p in range(16):
        value, centre = y_stage(TC, p, 10, 32, own, S[p + 4, pl.ds(8, 32)], U2, 2)
        w = value * centre
        mu5 = mu5 + ((w[0:8] + w[8:16]) + (w[16:24] + w[24:32]))

    last = jnp.sum(jnp.sum(mu5, axis=0, keepdims=True), axis=1, keepdims=True)
    values = jnp.where(lane1 == 5, last, values)
    rounded = (values + coarse) - coarse
    high = jnp.where(lane1 < 6, rounded, values)
    rest = jnp.where(lane1 < 6, values - rounded, 0.0)
    row = high + pltpu.roll(rest, 64, 1)
    row = jnp.where(lane1 == 9, count.astype(jnp.float32), row)

    pending = []
    mine = gy * 2 + core
    ar1[mine] = row
    for j in (10, 6, 9, 7, 11, 5, 8, 2, 14, 13, 3, 1, 15, 12, 4, 0):
        for c in (1 - core, core):
            if j == 0 and c is core:
                continue
            pltpu.make_async_remote_copy(
                ar1.at[mine], ar1.at[mine], asem.at[0], arsem.at[0],
                device_id=(2 * z + c, lax.rem(gy + j, NGY)), device_id_type=MESH).start()
    wait = pltpu.make_async_remote_copy(
        ar1.at[pl.ds(0, 31)], ar1.at[pl.ds(0, 31)], asem.at[0], arsem.at[0],
        device_id=(2 * z + 1 - core, gy), device_id_type=MESH)
    for i, ok in enumerate(has):
        @pl.when(ok)
        def _():
            for c in pieces(i, (0, 1, 2)):
                c.wait_send()
    wait.wait_recv()
    pending.append(wait)

    ar2[z] = tree([ar1[j] for j in range(32)])
    pl.semaphore_wait(token, 2)
    for off in (8, 7, -7, 6, -6, 5, -5, 4, -4, 3, -3, 2, -2, 1, -1):
        pltpu.make_async_remote_copy(
            ar2.at[z], ar2.at[z], asem.at[1], arsem.at[1],
            device_id=(at_z(off), gy), device_id_type=MESH).start()
    pending.pop().wait_send()
    wait = pltpu.make_async_remote_copy(
        ar2.at[pl.ds(0, 15)], ar2.at[pl.ds(0, 15)], asem.at[1], arsem.at[1],
        device_id=(at_z(1), gy), device_id_type=MESH)
    wait.wait_recv()
    pending.append(wait)
    row = tree([ar2[j] for j in range(16)])

    goal = jnp.where(sub16 < 10, sub16, sub16 + 54)
    picked = jnp.sum(jnp.where(lane16 == goal, row, 0.0), axis=1, keepdims=True)
    value = [jnp.broadcast_to(picked[k:k + 1], (8, 128)) for k in range(16)]
    mu = [two_sum(value[k], value[10 + k]) for k in range(6)]
    c0, c1, c2 = cg_weights(mu)
    iso = (c0 * value[6] + c1 * value[7] + c2 * value[8]) / (value[9] * float(BLK ** 3))

    def tile5(v):
        return jnp.concatenate([v] * 5, axis=0)

    iso_out[...] = iso
    c0, c1, c2 = tile5(c0), tile5(c1), tile5(c2)

    def solve(p, carry):
        x_out[p] = c0 * R[HR + p, pl.ds(8, 40)] + c1 * U1[4 + p, pl.ds(4, 40)] + c2 * U2[2 + p, pl.ds(2, 40)]
        return carry

    lax.fori_loop(0, 17, solve, 0, unroll=True)

    for c in pending:
        c.wait_send()


def crossing_kernel(x_ref, iso_ref, vis, ind_out, cross_out, G, W, BR, vis_s, sem):
    load = pltpu.make_async_copy(vis.at[0], vis_s, sem.at[0])
    load.start()
    store = pltpu.make_async_copy(x_ref.at[pl.ds(0, 16), pl.ds(0, 32)], ind_out, sem.at[1])
    store.start()
    lane = lax.broadcasted_iota(jnp.int32, (8, 128), 1)
    iso = jnp.concatenate([iso_ref[...]] * 5, axis=0)

    for p in range(17):
        G[p] = sigmoid4(x_ref[p] - iso)
    BR[pl.ds(16 * 96, 96)] = jnp.zeros((96, 128), jnp.float32)

    lane32 = lax.broadcasted_iota(jnp.int32, (32, 128), 1)
    edge = lane32 == 127
    empty = sigmoid4(0.0 - iso[0:32])
    group = lane // BLK
    odd = [(group // (1 << bit)) % 2 == 1 for bit in range(3)]
    stores = [store]
    for e in range(3):
        for p in range(16):
            g = G[p, pl.ds(0, 32)]
            if e == 0:
                other = G[p + 1, pl.ds(0, 32)]
            elif e == 1:
                other = G[p, pl.ds(1, 32)]
            else:
                other = jnp.where(edge, empty, pltpu.roll(g, 127, 1))
            h = crossing_weight(g, other)
            for w in range(2):
                W[e, pl.ds((p // 4) * 128 + w * 64 + p % 4 * 16, 16)] = h[16 * w:16 * w + 16]
        for first in range(0, 8, 4):
            parts = range(first, first + 4)
            vs = {}
            for part in parts:
                vs[part] = [W[e, pl.ds(part * 64 + (-j) % 8, 8, stride=8)] for j in range(8)]
            for part in parts:
                vs[part] = [v if j == 0 else pltpu.roll(v, 16 * ((-j) % 8), 1) for j, v in enumerate(vs[part])]
            for bit in range(3):
                for part in parts:
                    old = vs[part]
                    vs[part] = [jnp.where(odd[bit], old[(t - (1 << bit)) % 8], old[t]) for t in range(8)]
            for part in parts:
                vs[part] = [v if t == 0 else pltpu.roll(v, 128 - 16 * t, 1) for t, v in enumerate(vs[part])]
            for part in parts:
                w, ib = part % 2, part // 2
                for t in range(8):
                    BR[pl.ds((w * 8 + t) * 96 + e * 32 + ib * 8, 8)] = vs[part][t]
        if e == 0:
            load.wait()
            slots = []
            for q in range(VIS):
                n = vis_s[0, q]
                slots.append(jnp.where(n >= 0, n, 16) * 96)
        for q in range(VIS):
            start = pl.multiple_of(slots[q] + e * 32, 8)
            stores.append(pltpu.make_async_copy(
                BR.at[pl.ds(start, 32)], cross_out.at[pl.ds(q * 96 + e * 32, 32)], sem.at[2 + q * 3 + e]))
            stores[-1].start()
    for c in stores:
        c.wait()


def body(right_side, screening, active_blocks, visible_bricks):
    f32 = jnp.float32
    right_side, screening, active_blocks, visible_bricks = (
        pltpu.with_memory_space_constraint(v, pltpu.HBM)
        for v in (right_side, screening, active_blocks, visible_bricks))
    hbm = pl.BlockSpec(memory_space=pltpu.HBM)
    vmem = pl.BlockSpec(memory_space=pltpu.VMEM)
    x, iso = pl.pallas_call(
        solve_kernel,
        out_shape=(jax.ShapeDtypeStruct((17, 40, 128), f32), jax.ShapeDtypeStruct((8, 128), f32)),
        in_specs=[hbm] * 3,
        out_specs=(vmem, vmem),
        scratch_shapes=[
            pltpu.VMEM((28, 48, 128), f32),
            pltpu.VMEM((24, 48, 128), f32),
            pltpu.VMEM((3, 4, 128), f32),
            pltpu.VMEM((24, 48, 128), f32),
            pltpu.VMEM((20, 48, 128), f32),
            pltpu.VMEM((28, 64, 128), f32),
            pltpu.VMEM((28, 64, 128), f32),
            pltpu.VMEM((24, 56, 128), f32),
            pltpu.VMEM((24, 56, 128), f32),
            pltpu.VMEM((20, 56, 128), f32),
            pltpu.VMEM((20, 56, 128), f32),
            pltpu.VMEM((3, 24, 64, 128), f32),
            pltpu.VMEM((3, 20, 56, 128), f32),
            pltpu.VMEM((3, 16, 56, 128), f32),
            pltpu.SMEM((1, ACT), jnp.int32),
            pltpu.VMEM((32, 1, 128), f32),
            pltpu.VMEM((16, 1, 128), f32),
            pltpu.SemaphoreType.DMA((3,)),
            pltpu.SemaphoreType.DMA((8, 3)),
            pltpu.SemaphoreType.DMA((8, 3)),
            pltpu.SemaphoreType.DMA((2,)),
            pltpu.SemaphoreType.DMA((2,)),
            pltpu.SemaphoreType.REGULAR,
        ],
        compiler_params=pltpu.CompilerParams(
            collective_id=0, has_side_effects=True, vmem_limit_bytes=32 << 20),
    )(right_side, screening, active_blocks)
    indicator, crossing = pl.pallas_call(
        crossing_kernel,
        out_shape=(jax.ShapeDtypeStruct((16, 32, 128), f32), jax.ShapeDtypeStruct((VIS * 96, 128), f32)),
        in_specs=[vmem, vmem, hbm],
        out_specs=(hbm, hbm),
        scratch_shapes=[
            pltpu.VMEM((17, 40, 128), f32),
            pltpu.VMEM((3, 512, 128), f32),
            pltpu.VMEM((17 * 96, 128), f32),
            pltpu.SMEM((1, VIS), jnp.int32),
            pltpu.SemaphoreType.DMA((2 + 3 * VIS,)),
        ],
        compiler_params=pltpu.CompilerParams(vmem_limit_bytes=24 << 20),
    )(x, iso, visible_bricks)
    return indicator, crossing.reshape(VIS, 1, 3, BLK ** 3)


def solution(mesh):
    spec = P("gx", "gy", None)
    return jax.shard_map(
        body,
        mesh=mesh,
        in_specs=(spec, spec, spec, spec),
        out_specs=(spec, P("gx", "gy", None, None)),
        check_vma=False,
    )
```
